128 devices in a mesh: fsdp: 32 (over y, x_hi, z), red: 4 (over x_lo, core).
Axes of the slice: x: 4 (x_hi: 2, x_lo: 2; x = x_hi * 2 + x_lo), y: 4, z: 4, core: 2. Of those that a mesh axis runs over, the one named last changes fastest.
Arguments:
- layer_input: bfloat16 [2, 8192, 16384], P(None, 'fsdp', 'red'), may hold values from -6 to 6
- kv_cotangent: bfloat16 [2, 8192, 1024], P(None, 'fsdp'), may hold values from -16 to 16
- failed_member: int32 [32], P('fsdp'), may hold values from 0 to 4
- master: float32 [2, 1024, 16384], P(None, 'fsdp', 'red'), may hold values from -0.046875 to 0.046875
- first_moment: float32 [2, 1024, 16384], P(None, 'fsdp', 'red'), may hold values from -4 to 4
- second_moment: float32 [2, 1024, 16384], P(None, 'fsdp', 'red'), may hold values from 0.05 to 2
- loss_scale: float32 [32, 4], P('fsdp', 'red'), may hold values from 2 to 8
- spare_master: float32 [2, 1024, 16384], P(None, 'fsdp', 'red'), may hold values from -0.046875 to 0.046875
- spare_first: float32 [2, 1024, 16384], P(None, 'fsdp', 'red'), may hold values from -4 to 4
- spare_second: float32 [2, 1024, 16384], P(None, 'fsdp', 'red'), may hold values from 0.05 to 2
- spare_scale: float32 [32, 4], P('fsdp', 'red'), may hold values from 2 to 8
Outputs:
- kv_out: bfloat16 [2, 8192, 1024], P(None, 'fsdp', 'red')
- input_grad: bfloat16 [2, 8192, 16384], P(None, 'fsdp', 'red')
- new_master: float32 [2, 1024, 16384], P(None, 'fsdp', 'red')
- new_first: float32 [2, 1024, 16384], P(None, 'fsdp', 'red')
- new_second: float32 [2, 1024, 16384], P(None, 'fsdp', 'red')
The draws below stay inside these ranges and needn't reach their ends.
Inputs may be any that keep to these rules, and one draw needn't show every extreme that they name: failed_member[f] is the member of redundancy group f (index along red) whose state was lost; the value 4 means that group lost nothing.
All inputs are finite; a program needn't handle non-finite values.
Results may differ from the reference program's by a relative error of at most 0.017.
Values may be sent and summed in bfloat16 or wider, within the bound.
A program may use at most 128 MiB of HBM per device.

```python
import math
import jax
import jax.numpy as jnp
from jax import lax

D = 16384
LAYERS = 2
TOK_DEV = 256
C = 1024
TOKENS = 8192
N_FSDP = 32
N_RED = 4


def draw_kv_cotangent(key, part):
    position = jnp.arange(C).astype(jnp.float32) / (C - 1)
    low_scale = 0.5
    high_scale = 2.5
    values = jnp.clip(jax.random.normal(key, (LAYERS, TOKENS, C), jnp.float32), -6.0, 6.0)
    column_scale = jnp.exp(jnp.log(low_scale) + (jnp.log(high_scale) - jnp.log(low_scale)) * position)
    return (values * column_scale[None, None, :]).astype(jnp.bfloat16)


def place_ends(drawn, own_key, smallest, largest):
    longest = drawn.shape.index(max(drawn.shape))
    spots = []
    for shift in (0, 1):
        where = [jax.random.randint(jax.random.fold_in(own_key, axis), (), 0, length) for axis, length in enumerate(drawn.shape)]
        where[longest] = (where[longest] + shift) % drawn.shape[longest]
        spots.append(tuple(where))
    return drawn.at[spots[0]].set(smallest).at[spots[1]].set(largest)


def block_scale(key, extent, pieces, low, high):
    def one(axis_at, shards_of):
        heights = jax.random.uniform(jax.random.fold_in(jax.random.fold_in(key, 6), axis_at), (shards_of,), jnp.float32, low / len(pieces), high / len(pieces))
        return jnp.repeat(jnp.exp(heights), extent[axis_at] // shards_of).reshape((-1,) + (1,) * (len(extent) - axis_at - 1))

    level = one(*pieces[0])
    for cut in pieces[1:]:
        level = level * one(*cut)
    return level


def noise(rng, extent, deviation, limit, split=(), kind=jnp.bfloat16):
    entries = deviation * jax.random.normal(rng, extent, jnp.float32)
    if split:
        entries = entries * block_scale(rng, extent, split, -0.22, 0.18)
    return jnp.clip(entries, -limit, limit).astype(kind)


def setup_inputs(seed: int = 0) -> dict:
    keys = jax.random.split(jax.random.key(seed), 12)
    layer_input = noise(keys[0], (LAYERS, TOKENS, D), 1.0, 6.0, ((1, 32), (2, 4)))
    kv_cotangent = draw_kv_cotangent(jax.random.fold_in(keys[11], 71), 0)
    failed_member = place_ends(jax.random.randint(keys[2], (N_FSDP,), 0, N_RED + 1), jax.random.fold_in(keys[2], 1), 0, N_RED).astype(jnp.int32)
    master = noise(keys[3], (LAYERS, C, D), D ** -0.5, 0.046875, ((1, 32), (2, 4)), jnp.float32)
    first_moment = noise(keys[4], (LAYERS, C, D), 0.5, 4.0, ((1, 32), (2, 4)), jnp.float32)
    second_moment = jnp.clip(jnp.exp(math.log(2.0) - 3.6888794 * jax.random.uniform(keys[5], (LAYERS, C, D), jnp.float32) ** block_scale(keys[5], (LAYERS, C, D), ((1, 32), (2, 4)), -0.2, 0.2)), 0.05, 2.0)
    loss_scale = jnp.clip(jnp.exp(math.log(8.0) - 1.3862944 * jax.random.uniform(keys[6], (N_FSDP, N_RED), jnp.float32) ** block_scale(keys[6], (N_FSDP, N_RED), ((0, 32), (1, 4)), -0.2, 0.2)), 2.0, 8.0)
    spare_master = noise(keys[7], (LAYERS, C, D), D ** -0.5, 0.046875, ((1, 32), (2, 4)), jnp.float32)
    spare_first = noise(keys[8], (LAYERS, C, D), 0.5, 4.0, ((1, 32), (2, 4)), jnp.float32)
    spare_second = jnp.clip(jnp.exp(math.log(2.0) - 3.6888794 * jax.random.uniform(keys[9], (LAYERS, C, D), jnp.float32) ** block_scale(keys[9], (LAYERS, C, D), ((1, 32), (2, 4)), -0.2, 0.2)), 0.05, 2.0)
    spare_scale = jnp.clip(jnp.exp(math.log(8.0) - 1.3862944 * jax.random.uniform(keys[10], (N_FSDP, N_RED), jnp.float32) ** block_scale(keys[10], (N_FSDP, N_RED), ((0, 32), (1, 4)), -0.2, 0.2)), 2.0, 8.0)
    return dict(layer_input=layer_input, kv_cotangent=kv_cotangent, failed_member=failed_member, master=master, first_moment=first_moment, second_moment=second_moment, loss_scale=loss_scale, spare_master=spare_master, spare_first=spare_first, spare_second=spare_second, spare_scale=spare_scale)


BETA_FIRST = 0.9
BETA_SECOND = 0.95
LEARN_RATE = 0.01
DECAY_RATE = 0.1
ADAM_EPS = 1e-08
MEAN_EPS = 1e-06

def reference(layer_input, kv_cotangent, failed_member, master, first_moment, second_moment, loss_scale, spare_master, spare_first, spare_second, spare_scale):
    block_rows = C // N_FSDP
    block_cols = D // N_RED
    owner = (jnp.arange(C) // block_rows).astype(jnp.int32)
    member = (jnp.arange(D) // block_cols).astype(jnp.int32)
    replaced = (failed_member[owner][:, None] == member[None, :])[None]
    master_now = jnp.where(replaced, jnp.roll(spare_master, block_cols, axis=2), master)
    first_now = jnp.where(replaced, jnp.roll(spare_first, block_cols, axis=2), first_moment)
    second_now = jnp.where(replaced, jnp.roll(spare_second, block_cols, axis=2), second_moment)
    scale_lost = failed_member[:, None] == jnp.arange(N_RED).astype(jnp.int32)[None, :]
    scale_now = jnp.where(scale_lost, jnp.roll(spare_scale, 1, axis=1), loss_scale)
    scale_full = jnp.repeat(jnp.repeat(scale_now, block_rows, axis=0), block_cols, axis=1)
    weights = master_now.astype(jnp.bfloat16)
    kv_list = []
    input_list = []
    weight_list = []
    for layer_index in range(LAYERS):
        full_weight = weights[layer_index]
        inputs = layer_input[layer_index]
        upstream = kv_cotangent[layer_index]
        kv_list.append(lax.dot_general(inputs, full_weight, (((1,), (1,)), ((), ())), preferred_element_type=jnp.float32).astype(jnp.bfloat16))
        input_list.append(jnp.dot(upstream, full_weight, preferred_element_type=jnp.float32).astype(jnp.bfloat16))

        def add_group(carry, group, inputs=inputs, upstream=upstream):
            offset = (group * TOK_DEV).astype(jnp.int32)
            rows_in = lax.dynamic_slice_in_dim(inputs, offset, TOK_DEV, 0)
            rows_up = lax.dynamic_slice_in_dim(upstream, offset, TOK_DEV, 0)
            partial_sum = lax.dot_general(rows_up, rows_in, (((0,), (0,)), ((), ())), preferred_element_type=jnp.float32)
            rounded = lax.optimization_barrier(partial_sum.astype(jnp.bfloat16))
            return (carry + rounded.astype(jnp.float32), None)
        summed, _ = lax.scan(add_group, jnp.zeros((C, D), jnp.float32), jnp.arange(N_FSDP).astype(jnp.int32))
        weight_list.append(summed)
    gradient = jnp.stack(weight_list) / scale_full[None]
    mean_square = jnp.sum(gradient * gradient) / (LAYERS * C * D)
    factor = jnp.minimum(1.0, lax.rsqrt(mean_square + MEAN_EPS))
    clipped = gradient * factor
    new_first = BETA_FIRST * first_now + (1.0 - BETA_FIRST) * clipped
    new_second = BETA_SECOND * second_now + (1.0 - BETA_SECOND) * clipped * clipped
    new_master = master_now - LEARN_RATE * (new_first / (jnp.sqrt(new_second) + ADAM_EPS) + DECAY_RATE * master_now)
    return (jnp.stack(kv_list), jnp.stack(input_list), new_master, new_first, new_second)
```

```python
import functools

import jax
import jax.numpy as jnp
from jax import lax
from jax.experimental import pallas as pl
from jax.experimental.pallas import tpu as pltpu
from jax.sharding import Mesh
from jax.sharding import PartitionSpec as P

Y, XH, Z, XL, CO = "fsdp_0", "fsdp_1", "fsdp_2", "red_0", "red_1"
RED = (XL, CO)
FSDP = (Y, XH, Z)
MESH_ID = pl.DeviceIdType.MESH

BETA_FIRST = 0.9
BETA_SECOND = 0.95
LEARN_RATE = 0.01
DECAY_RATE = 0.1
ADAM_EPS = 1e-08
MEAN_EPS = 1e-06

NK = 4
BF = jnp.bfloat16
F32 = jnp.float32


def kernel(
    entries,
    x_in,
    u_in,
    failed,
    scale_own,
    scale_spare,
    master,
    first,
    second,
    sp_master,
    sp_first,
    sp_second,
    kv_out,
    ig_out,
    nm_out,
    nf_out,
    ns_out,
    xbuf,
    ubuf,
    ut,
    wsb,
    wbuf,
    dwbuf,
    r1a,
    r1b,
    r1c,
    s1,
    r2a,
    r2b,
    r2c,
    s2,
    gbuf,
    igb,
    kvp,
    kvs,
    kvr,
    ka,
    kb,
    kc,
    kvo,
    st,
    spf,
    spb,
    spr,
    scs,
    scr,
    nacc,
    nsend,
    npl,
    nsend2,
    nxc,
    loc,
    sp_s,
    sp_r,
    u_s,
    u_r,
    x_s,
    x_r,
    w_s,
    w_r,
    ag_s,
    ag_r,
    rs_s,
    rs_r,
    g_s,
    g_r,
    ig_s,
    ig_r,
    kv_s,
    kv_r,
    np_s,
    np_r,
    nx_s,
    nx_r,
):
    layers, tok, cols = x_in.shape
    half = cols // 2
    ck = half // NK
    rows = master.shape[1]
    feats = u_in.shape[2]
    y, xh, z, xl, c = (lax.axis_index(a) for a in (Y, XH, Z, XL, CO))
    x = 2 * xh + xl
    me_r = 2 * xl + c

    def ring(v, d):
        return lax.rem(v + (d + 4), 4)

    def to_x(v, core=None):
        dev = {XH: v // 2, XL: lax.rem(v, 2)}
        if core is not None:
            dev[CO] = core
        return dev

    xn = {d: ring(x, d) for d in (1, -1)}
    xn_h = {d: xn[d] // 2 for d in (1, -1)}
    plane_axis = {0: (Y, Z), 1: (Z, Y)}
    plane_pos = {Y: y, Z: z}
    DIRS = ((0, 1), (1, -1))

    def remote(src, dst, ss, rs, dev):
        return pltpu.make_async_remote_copy(
            src_ref=src, dst_ref=dst, send_sem=ss, recv_sem=rs, device_id=dev, device_id_type=MESH_ID
        )

    sends = []

    states = (master, first, second)
    spares = (sp_master, sp_first, sp_second)
    loads_sp = [pltpu.make_async_copy(spares[i], spf.at[i], loc.at[i]) for i in range(3)]
    loads_st = [pltpu.make_async_copy(states[i], st.at[i], loc.at[3 + i]) for i in range(3)]
    load_u = pltpu.make_async_copy(u_in, ubuf.at[:, xh], loc.at[6])
    loads_sp[0].start()
    loads_st[0].start()
    load_u.start()
    loads_sp[1].start()
    loads_sp[2].start()
    loads_st[1].start()
    loads_st[2].start()

    nxt_r = lax.rem(me_r + 1, 4)
    prv_r = lax.rem(me_r + 3, 4)
    plane_peers = [(dy, dz) for dy in range(4) for dz in range(4) if (dy, dz) != (0, 0)]
    xc_peers = [(dx, dc) for dx in range(4) for dc in range(2) if (dx, dc) != (0, 0)]

    def plane_dev(dy, dz):
        return {Y: lax.rem(y + dy, 4), Z: lax.rem(z + dz, 4)}

    def xc_dev(dx, dc):
        v = lax.rem(x + dx, 4)
        return {XH: v // 2, XL: lax.rem(v, 2), CO: lax.rem(c + dc, 2)}

    barrier = pltpu.get_barrier_semaphore()
    for p in plane_peers:
        pl.semaphore_signal(barrier, inc=1, device_id=plane_dev(*p), device_id_type=MESH_ID)
    for p in xc_peers:
        pl.semaphore_signal(barrier, inc=1, device_id=xc_dev(*p), device_id_type=MESH_ID)

    loads_sp[0].wait()
    for l in range(layers):
        spb[0, l] = spf[0, l].astype(BF)
    scs[...] = jnp.broadcast_to(scale_spare[...], scs.shape)
    pl.semaphore_wait(barrier, len(plane_peers) + len(xc_peers))

    nxt_dev = {XL: nxt_r // 2, CO: lax.rem(nxt_r, 2)}

    def spare_copy(i, l):
        if i == 0:
            return remote(spb.at[0, l], spr.at[0, l], sp_s.at[l], sp_r.at[l], nxt_dev)
        return remote(spb.at[i], spr.at[i], sp_s.at[1 + i], sp_r.at[1 + i], nxt_dev)

    for l in range(layers):
        spare_copy(0, l).start()
    scale_copy = remote(scs, scr, sp_s.at[4], sp_r.at[4], nxt_dev)
    scale_copy.start()

    def x_copy(k, l, di, d):
        src = x_in.at[l, :, pl.ds(pl.multiple_of(xn_h[d] * half + k * ck, ck), ck)]
        return remote(src, xbuf.at[k, l, xh], x_s.at[k, l, di], x_r.at[k, l, di], to_x(xn[d]))

    for di, d in DIRS:
        x_copy(0, 0, di, d).start()

    def w_copy(l, di, d):
        return remote(
            wsb.at[xn_h[d], :, l], wbuf.at[:, l, y, xh, z], w_s.at[l, di], w_r.at[l, di], to_x(xn[d])
        )

    lost = jnp.broadcast_to(failed[...], (rows, ck)) == me_r
    loads_st[0].wait()
    for l in range(layers):
        spare_copy(0, l).wait_recv()
        for j in range(2 * NK):
            span = slice(j * ck, (j + 1) * ck)
            now = jnp.where(lost, spr[0, l, :, span].astype(F32), st[0, l, :, span])
            st[0, l, :, span] = now
            wsb[j // NK, j % NK, l] = now.astype(BF)
        for di, d in DIRS:
            w_copy(l, di, d).start()

    load_u.wait()
    u_far = lax.rem(x + 1 + 2 * (1 - lax.rem(x, 2)), 4)
    u_copy = remote(u_in.at[c], ubuf.at[c, xh], u_s.at[0], u_r.at[0], to_x(u_far))
    u_copy.start()
    u_fwd = remote(ubuf.at[c, 1 - xh], ubuf.at[c, 1 - xh], u_s.at[1], u_r.at[1], {CO: 1 - c})

    for di, d in DIRS:
        x_copy(0, 1, di, d).start()
    for l in range(layers):
        for di, d in DIRS:
            x_copy(1, l, di, d).start()
    for i in (1, 2):
        loads_sp[i].wait()
        for l in range(layers):
            spb[i, l] = spf[i, l].astype(BF)
        spare_copy(i, 0).start()
    for k in range(2, NK):
        for l in range(layers):
            for di, d in DIRS:
                x_copy(k, l, di, d).start()

    def region(k, l, stage, p, h):
        hs = slice(None) if h is None else h
        if l == 0:
            return wbuf.at[k, 0, p, hs, z] if stage == 0 else wbuf.at[k, 0, :, hs, p]
        return wbuf.at[k, 1, y, hs, p] if stage == 0 else wbuf.at[k, 1, p, hs, :]

    def ag_copy(k, l, stage, step, di, d):
        axis = plane_axis[l][stage]
        pos = plane_pos[axis]
        ref = region(k, l, stage, pos, None) if step == 0 else region(k, l, stage, ring(pos, -d), di)
        n = stage * 2 + step
        return remote(ref, ref, ag_s.at[k, l, n, di], ag_r.at[k, l, n, di], {axis: ring(pos, d)})

    def ag_start(k, stage):
        for l in range(layers):
            for di, d in DIRS:
                ag_copy(k, l, stage, 0, di, d).start()

    def ag_forward(k, stage):
        for l in range(layers):
            for di, d in DIRS:
                ag_copy(k, l, stage, 0, di, d).wait_recv()
                ag_copy(k, l, stage, 1, di, d).start()

    def ag_finish(k, stage):
        for l in range(layers):
            for di, d in DIRS:
                ag_copy(k, l, stage, 1, di, d).wait_recv()

    def dw_piece(k, l, p, h):
        return dwbuf.at[k, 0, :, h, p] if l == 0 else dwbuf.at[k, 1, p, h, :]

    def rs_parts(k, l, stage):
        axis = plane_axis[l][1 - stage]
        if stage == 0:
            return axis, (lambda p, h: dw_piece(k, l, p, h)), r1a, r1b, r1c
        return axis, (lambda p, h: s1.at[k, l, h, p]), r2a, r2b, r2c

    def rs_copy(k, l, stage, what, di, d):
        axis, piece, ra, rb, rc = rs_parts(k, l, stage)
        pos = plane_pos[axis]
        if what == 0:
            src, dst = piece(ring(pos, 2), di), ra.at[k, l, di]
        elif what == 1:
            src, dst = piece(ring(pos, d), 1 - di), rb.at[k, l, di]
        else:
            src, dst = ra.at[k, l, di], rc.at[k, l, di]
        n = stage * 3 + what
        return remote(src, dst, rs_s.at[k, l, n, di], rs_r.at[k, l, n, di], {axis: ring(pos, d)})

    def rs_start(k, l, stage):
        for what in (0, 1):
            for di, d in DIRS:
                rs_copy(k, l, stage, what, di, d).start()

    def each(stage, fn):
        if stage == 0:

            @pl.loop(0, 4)
            def _(j):
                fn(j)
        else:
            fn(None)

    def at(ref, j):
        return ref[j] if j is not None else ref[...]

    def rs_forward(k, stage):
        for l in range(layers):
            axis, piece, ra, rb, rc = rs_parts(k, l, stage)
            pos = plane_pos[axis]
            for di, d in DIRS:
                rs_copy(k, l, stage, 0, di, d).wait_recv()
                own = piece(ring(pos, d), di)
                acc = ra.at[k, l, di]

                def add(j, own=own, acc=acc):
                    total = (at(acc, j).astype(F32) + at(own, j).astype(F32)).astype(BF)
                    if j is None:
                        acc[...] = total
                    else:
                        acc[j] = total

                each(stage, add)
                rs_copy(k, l, stage, 2, di, d).start()

    def rs_finish(k, stage):
        for l in range(layers):
            axis, piece, ra, rb, rc = rs_parts(k, l, stage)
            pos = plane_pos[axis]
            for what in (1, 2):
                for di, d in DIRS:
                    rs_copy(k, l, stage, what, di, d).wait_recv()
            for h in range(2):
                own = piece(pos, h)
                through = rc.at[k, l, h]
                direct = rb.at[k, l, 1 - h]
                out = s1.at[k, l, h] if stage == 0 else s2.at[k, l, h]

                def add(j, own=own, through=through, direct=direct, out=out):
                    total = at(own, j).astype(F32) + at(through, j).astype(F32) + at(direct, j).astype(F32)
                    if j is None:
                        out[...] = total.astype(BF)
                    else:
                        out[j] = total.astype(BF)

                each(stage, add)
            if stage == 0:
                rs_start(k, l, 1)
            else:
                for di, d in DIRS:
                    g_copy(k, l, di, d).start()

    def g_copy(k, l, di, d):
        return remote(
            s2.at[k, l, xn_h[d]], gbuf.at[k, l, xh], g_s.at[k, l, di], g_r.at[k, l, di], to_x(xn[d])
        )

    def transpose_u():
        for l in range(layers):

            @pl.loop(0, 4)
            def _(j):
                span = pl.ds(pl.multiple_of(j * (feats // 4), feats // 4), feats // 4)
                for t in range(2):
                    ut[l, j, :, t * tok : (t + 1) * tok] = ubuf[l, t, :, span].T

    def grad_product(k):
        for l in range(layers):
            for di, d in DIRS:
                x_copy(k, l, di, d).wait_recv()

            @pl.loop(0, 4)
            def _(j):
                inputs = xbuf[k, l].reshape(2 * tok, ck)
                part = jnp.dot(ut[l, j], inputs, preferred_element_type=F32)
                dwbuf[k, l, j] = part.astype(BF).reshape(2, 4, rows, ck)

            rs_start(k, l, 0)

    def weight_products(k, begin):
        for l in range(layers):

            @pl.loop(0, 4)
            def _(j):
                inputs = xbuf[k, l].reshape(2 * tok, ck)
                weight = wbuf[k, l, j].reshape(8 * rows, ck)
                part = lax.dot_general(
                    inputs, weight, (((1,), (1,)), ((), ())), preferred_element_type=F32
                ).reshape(2, tok, 8 * rows)
                if begin is True:
                    kvp[j, l] = part
                else:
                    kvp[j, l] += part

            @pl.loop(0, 2)
            def _(t):
                weight = wbuf[k, l].reshape(feats, ck)
                igb[k, l, t] = jnp.dot(ubuf[l, t], weight, preferred_element_type=F32).astype(BF)

            for di, d in DIRS:
                ig_copy(k, l, di, d).start()

    def ig_copy(k, l, di, d):
        dst = ig_out.at[l, :, pl.ds(pl.multiple_of(xh * half + k * ck, ck), ck)]
        return remote(igb.at[k, l, xn_h[d]], dst, ig_s.at[k, l, di], ig_r.at[k, l, di], to_x(xn[d]))

    for l in range(layers):
        for di, d in DIRS:
            w_copy(l, di, d).wait_recv()
    for k in range(NK):
        ag_start(k, 0)

    @pl.loop(0, 4)
    def _(j):
        kvp[j] = jnp.zeros(kvp.shape[1:], F32)

    u_copy.wait_recv()
    u_fwd.start()
    ag_forward(0, 0)
    u_fwd.wait_recv()
    transpose_u()

    @pl.loop(0, NK)
    def _(i):
        @pl.when(i > 0)
        def _():
            ag_forward(i, 0)
            rs_forward(i - 1, 0)

        ag_finish(i, 0)
        ag_start(i, 1)
        grad_product(i)

        @pl.when(i > 0)
        def _():
            rs_finish(i - 1, 0)

        ag_forward(i, 1)

        @pl.when(i > 0)
        def _():
            weight_products(i - 1, False)
            rs_forward(i - 1, 1)

        ag_finish(i, 1)

        @pl.when(i > 0)
        def _():
            rs_finish(i - 1, 1)

    last = NK - 1
    rs_forward(last, 0)
    weight_products(last, False)

    for v in range(2):
        kvs[v] = kvp[2 * v + (1 - c)].astype(BF)
    kv_core = remote(kvs, kvr, kv_s.at[0], kv_r.at[0], {CO: 1 - c})
    kv_core.start()
    rs_finish(last, 0)
    kv_core.wait_recv()
    for v in range(2):
        for l in range(layers):
            kvr[v, l] = (kvr[v, l].astype(F32) + kvp[2 * v + c, l]).astype(BF)

    def kv_piece(v, l):
        return kvr.at[lax.rem(v, 2), l, v // 2]

    def kv_copy(what, di, d):
        if what == 0:
            src, dst = kv_piece(ring(x, 2), di), ka.at[di]
        elif what == 1:
            src, dst = kv_piece(ring(x, d), 1 - di), kb.at[di]
        else:
            src, dst = ka.at[di], kc.at[di]
        n = 1 + what * 2 + di
        return remote(src, dst, kv_s.at[n], kv_r.at[n], to_x(xn[d]))

    for what in (0, 1):
        for di, d in DIRS:
            kv_copy(what, di, d).start()
    rs_forward(last, 1)
    for di, d in DIRS:
        kv_copy(0, di, d).wait_recv()
        ka[di] = (ka[di].astype(F32) + kv_piece(ring(x, d), di)[...].astype(F32)).astype(BF)
        kv_copy(2, di, d).start()
    rs_finish(last, 1)

    scale_copy.wait_recv()
    lost_tile = jnp.broadcast_to(failed[...], scr.shape) == me_r
    scr[...] = jnp.where(lost_tile, scr[...], jnp.broadcast_to(scale_own[...], scr.shape))
    scale = jnp.broadcast_to(scr[0:1, 0:1], (rows, ck))
    nacc[...] = jnp.zeros(nacc.shape, F32)
    for k in range(NK):
        for l in range(layers):
            for di, d in DIRS:
                g_copy(k, l, di, d).wait_recv()

    @pl.loop(0, NK)
    def _(k):
        for l in range(layers):
            for h in range(2):
                grad = gbuf[k, l, h].astype(F32) / scale
                nacc[...] += grad * grad

    tile = jnp.zeros((8, 128), F32)
    for i in range(rows // 8):
        for j in range(ck // 128):
            tile = tile + nacc[8 * i : 8 * i + 8, 128 * j : 128 * j + 128]
    nsend[...] = tile
    np_copies = [
        remote(nsend, npl.at[i], np_s.at[i], np_r.at[i], plane_dev(*p)) for i, p in enumerate(plane_peers)
    ]
    for cp in np_copies:
        cp.start()
    for what in (1, 2):
        for di, d in DIRS:
            kv_copy(what, di, d).wait_recv()
    for h in range(2):
        own = kv_piece(x, h)[...].astype(F32)
        kvo[h] = (own + kc[h].astype(F32) + kb[1 - h].astype(F32)).astype(BF)
    kv_store = pltpu.make_async_copy(kvo, kv_out, loc.at[7])
    kv_store.start()
    total = nsend[...]
    for i, cp in enumerate(np_copies):
        cp.wait_recv()
        total = total + npl[i]
    nsend2[...] = total
    nx_copies = [
        remote(nsend2, nxc.at[i], nx_s.at[i], nx_r.at[i], xc_dev(*p)) for i, p in enumerate(xc_peers)
    ]
    for cp in nx_copies:
        cp.start()
    for i in (1, 2):
        loads_st[i].wait()
        spare_copy(i, 0).wait_recv()
    total = nsend2[...]
    for i, cp in enumerate(nx_copies):
        cp.wait_recv()
        total = total + nxc[i]
    squares = jnp.sum(jnp.sum(total, axis=1, keepdims=True), axis=0, keepdims=True)
    factor = jnp.minimum(1.0, lax.rsqrt(squares / entries + MEAN_EPS))
    factor = jnp.broadcast_to(factor, (rows, ck))

    @pl.loop(0, 2 * NK)
    def _(j):
        span = pl.ds(pl.multiple_of(j * ck, ck), ck)
        h = j // NK
        k = lax.rem(j, NK)
        for l in range(layers):
            clipped = gbuf[k, l, h].astype(F32) / scale * factor
            first_now = jnp.where(lost, spr[1, l, :, span].astype(F32), st[1, l, :, span])
            second_now = jnp.where(lost, spr[2, l, :, span].astype(F32), st[2, l, :, span])
            master_now = st[0, l, :, span]
            new_first = BETA_FIRST * first_now + (1.0 - BETA_FIRST) * clipped
            new_second = BETA_SECOND * second_now + (1.0 - BETA_SECOND) * clipped * clipped
            st[0, l, :, span] = master_now - LEARN_RATE * (
                new_first / (jnp.sqrt(new_second) + ADAM_EPS) + DECAY_RATE * master_now
            )
            st[1, l, :, span] = new_first
            st[2, l, :, span] = new_second

    stores = [
        pltpu.make_async_copy(st.at[i], out, loc.at[8 + i]) for i, out in enumerate((nm_out, nf_out, ns_out))
    ]
    for cp in stores:
        cp.start()

    for l in range(layers):
        spare_copy(0, l).wait_send()
    for i in (1, 2):
        spare_copy(i, 0).wait_send()
    scale_copy.wait_send()
    u_copy.wait_send()
    u_fwd.wait_send()
    kv_core.wait_send()
    for l in range(layers):
        for di, d in DIRS:
            w_copy(l, di, d).wait_send()
    for what in range(3):
        for di, d in DIRS:
            kv_copy(what, di, d).wait_send()
    for cp in np_copies + nx_copies:
        cp.wait_send()

    @pl.loop(0, NK)
    def _(k):
        for l in range(layers):
            for di, d in DIRS:
                x_copy(k, l, di, d).wait_send()
                ig_copy(k, l, di, d).wait_send()
                g_copy(k, l, di, d).wait_send()
                for stage in range(2):
                    for step in range(2):
                        ag_copy(k, l, stage, step, di, d).wait_send()
                    for what in range(3):
                        rs_copy(k, l, stage, what, di, d).wait_send()
                ig_copy(k, l, di, d).wait_recv()

    kv_store.wait()
    for cp in stores:
        cp.wait()


def local(
    layer_input,
    kv_cotangent,
    failed_member,
    master,
    first_moment,
    second_moment,
    loss_scale,
    spare_master,
    spare_first,
    spare_second,
    spare_scale,
):
    layers, tok, cols = layer_input.shape
    rows = master.shape[1]
    feats = kv_cotangent.shape[2]
    half = cols // 2
    ck = half // NK
    entries = float(layers * rows * lax.axis_size(FSDP) * cols * lax.axis_size(RED))
    any_ = pl.BlockSpec(memory_space=pl.ANY)
    vmem = pl.BlockSpec(memory_space=pltpu.VMEM)
    sem = pltpu.SemaphoreType.DMA
    scratch = [
        pltpu.VMEM((NK, layers, 2, tok, ck), BF),
        pltpu.VMEM((layers, 2, tok, feats), BF),
        pltpu.VMEM((layers, 4, feats // 4, 2 * tok), BF),
        pltpu.VMEM((2, NK, layers, rows, ck), BF),
        pltpu.VMEM((NK, layers, 4, 2, 4, rows, ck), BF),
        pltpu.VMEM((NK, layers, 4, 2, 4, rows, ck), BF),
        pltpu.VMEM((NK, layers, 2, 4, rows, ck), BF),
        pltpu.VMEM((NK, layers, 2, 4, rows, ck), BF),
        pltpu.VMEM((NK, layers, 2, 4, rows, ck), BF),
        pltpu.VMEM((NK, layers, 2, 4, rows, ck), BF),
        pltpu.VMEM((NK, layers, 2, rows, ck), BF),
        pltpu.VMEM((NK, layers, 2, rows, ck), BF),
        pltpu.VMEM((NK, layers, 2, rows, ck), BF),
        pltpu.VMEM((NK, layers, 2, rows, ck), BF),
        pltpu.VMEM((NK, layers, 2, rows, ck), BF),
        pltpu.VMEM((NK, layers, 2, tok, ck), BF),
        pltpu.VMEM((4, layers, 2, tok, feats // 4), F32),
        pltpu.VMEM((2, layers, 2, tok, feats // 4), BF),
        pltpu.VMEM((2, layers, 2, tok, feats // 4), BF),
        pltpu.VMEM((2, tok, feats // 4), BF),
        pltpu.VMEM((2, tok, feats // 4), BF),
        pltpu.VMEM((2, tok, feats // 4), BF),
        pltpu.VMEM((2, tok, feats // 4), BF),
        pltpu.VMEM((3, layers, rows, cols), F32),
        pltpu.VMEM((3, layers, rows, cols), F32),
        pltpu.VMEM((3, layers, rows, cols), BF),
        pltpu.VMEM((3, layers, rows, cols), BF),
        pltpu.VMEM((8, 128), F32),
        pltpu.VMEM((8, 128), F32),
        pltpu.VMEM((rows, ck), F32),
        pltpu.VMEM((8, 128), F32),
        pltpu.VMEM((15, 8, 128), F32),
        pltpu.VMEM((8, 128), F32),
        pltpu.VMEM((7, 8, 128), F32),
        sem((11,)),
        sem((5,)),
        sem((5,)),
        sem((2,)),
        sem((2,)),
        sem((NK, layers, 2)),
        sem((NK, layers, 2)),
        sem((layers, 2)),
        sem((layers, 2)),
        sem((NK, layers, 4, 2)),
        sem((NK, layers, 4, 2)),
        sem((NK, layers, 6, 2)),
        sem((NK, layers, 6, 2)),
        sem((NK, layers, 2)),
        sem((NK, layers, 2)),
        sem((NK, layers, 2)),
        sem((NK, layers, 2)),
        sem((7,)),
        sem((7,)),
        sem((15,)),
        sem((15,)),
        sem((7,)),
        sem((7,)),
    ]
    return pl.pallas_call(
        functools.partial(kernel, entries),
        out_shape=(
            jax.ShapeDtypeStruct((layers, tok, feats // 4), BF),
            jax.ShapeDtypeStruct((layers, tok, cols), BF),
            jax.ShapeDtypeStruct(master.shape, F32),
            jax.ShapeDtypeStruct(master.shape, F32),
            jax.ShapeDtypeStruct(master.shape, F32),
        ),
        in_specs=[any_, any_, vmem, vmem, vmem] + [any_] * 6,
        out_specs=(any_,) * 5,
        scratch_shapes=scratch,
        compiler_params=pltpu.CompilerParams(
            collective_id=0, has_side_effects=True, vmem_limit_bytes=67043328
        ),
        name="restore_step",
    )(
        layer_input,
        kv_cotangent,
        failed_member.reshape(1, 1),
        loss_scale,
        spare_scale,
        master,
        first_moment,
        second_moment,
        spare_master,
        spare_first,
        spare_second,
    )


def solution(mesh):
    split = Mesh(mesh.devices.reshape(4, 2, 4, 2, 2), (Y, XH, Z, XL, CO))
    placed = (
        P(None, FSDP, RED),
        P(None, FSDP, None),
        P(FSDP),
        P(None, FSDP, RED),
        P(None, FSDP, RED),
        P(None, FSDP, RED),
        P(FSDP, RED),
        P(None, FSDP, RED),
        P(None, FSDP, RED),
        P(None, FSDP, RED),
        P(FSDP, RED),
    )
    return jax.shard_map(
        local,
        mesh=split,
        in_specs=placed,
        out_specs=(P(None, FSDP, RED),) * 5,
        check_vma=False,
    )
```

```python
import functools

import jax
import jax.numpy as jnp
from jax import lax
from jax.experimental import pallas as pl
from jax.experimental.pallas import tpu as pltpu
from jax.sharding import Mesh
from jax.sharding import PartitionSpec as P

Y, XH, Z, XL, CO = "fsdp_0", "fsdp_1", "fsdp_2", "red_0", "red_1"
RED = (XL, CO)
FSDP = (Y, XH, Z)
MESH_ID = pl.DeviceIdType.MESH

BETA_FIRST = 0.9
BETA_SECOND = 0.95
LEARN_RATE = 0.01
DECAY_RATE = 0.1
ADAM_EPS = 1e-08
MEAN_EPS = 1e-06

NK = 4
SPARES_AT = 4
ORDER = (
    ("INI",),
    ("WSEL", 0),
    ("WSEL", 1),
    ("XREST",),
    ("A1", 0, 0),
    ("A1", 1, 0),
    ("A1", 2, 0),
    ("A1", 3, 0),
    ("A1", 0, 1),
    ("A1", 1, 1),
    ("A1", 2, 1),
    ("A1", 3, 1),
    ("F0", 0, 0),
    ("F0", 1, 0),
    ("F0", 2, 0),
    ("F0", 0, 1),
    ("F0", 3, 0),
    ("F0", 1, 1),
    ("S1", 0, 0),
    ("UF",),
    ("S1", 1, 0),
    ("F0", 2, 1),
    ("S1", 2, 0),
    ("S1", 3, 0),
    ("F0", 3, 1),
    ("TR",),
    ("S1", 0, 1),
    ("S1", 1, 1),
    ("DW", 0, 0),
    ("F1", 0, 0),
    ("DW", 0, 1),
    ("F1", 0, 1),
    ("F1", 1, 0),
    ("S1", 2, 1),
    ("DW", 1, 0),
    ("F1", 1, 1),
    ("RF0", 0, 1),
    ("F1", 2, 0),
    ("DW", 1, 1),
    ("WD", 0, 1),
    ("KV", 0, 1),
    ("IG", 0, 1),
    ("S1", 3, 1),
    ("F1", 3, 0),
    ("DW", 2, 0),
    ("RF0", 0, 0),
    ("F1", 2, 1),
    ("WD", 1, 1),
    ("KV", 1, 1),
    ("IG", 1, 1),
    ("WD", 0, 0),
    ("KV", 0, 0),
    ("RE0", 0, 1),
    ("WD", 1, 0),
    ("KV", 1, 0),
    ("RF0", 1, 1),
    ("IG", 0, 0),
    ("RF0", 1, 0),
    ("IG", 1, 0),
    ("DW", 2, 1),
    ("DW", 3, 0),
    ("WD", 2, 0),
    ("KV", 2, 0),
    ("IG", 2, 0),
    ("F1", 3, 1),
    ("WD", 3, 0),
    ("KV", 3, 0),
    ("IG", 3, 0),
    ("WD", 2, 1),
    ("KV", 2, 1),
    ("RF0", 2, 0),
    ("RE0", 1, 1),
    ("IG", 2, 1),
    ("DW", 3, 1),
    ("RF0", 2, 1),
    ("RE0", 0, 0),
    ("RF1", 0, 1),
    ("WD", 3, 1),
    ("KV", 3, 1),
    ("KVC",),
    ("RE0", 1, 0),
    ("RF0", 3, 1),
    ("RF0", 3, 0),
    ("KVA",),
    ("RE0", 2, 1),
    ("RE0", 2, 0),
    ("RF1", 0, 0),
    ("RF1", 1, 1),
    ("RF1", 1, 0),
    ("RE1", 0, 1),
    ("RE0", 3, 0),
    ("RE0", 3, 1),
    ("RF1", 2, 1),
    ("RF1", 2, 0),
    ("RE1", 1, 1),
    ("RE1", 0, 0),
    ("RE1", 1, 0),
    ("RF1", 3, 1),
    ("RF1", 3, 0),
    ("RE1", 2, 1),
    ("RE1", 2, 0),
    ("RE1", 3, 1),
    ("RE1", 3, 0),
    ("SQ",),
    ("NX",),
    ("IG", 3, 1),
    ("KVF",),
    ("AD",),
    ("END",),
    ("KVE",),
)
BF = jnp.bfloat16
F32 = jnp.float32


def kernel(
    entries,
    x_in,
    u_in,
    failed,
    scale_own,
    scale_spare,
    master,
    first,
    second,
    sp_master,
    sp_first,
    sp_second,
    kv_out,
    ig_out,
    nm_out,
    nf_out,
    ns_out,
    xbuf,
    ubuf,
    ut,
    wsb,
    wbuf,
    dwbuf,
    r1a,
    r1b,
    r1c,
    s1,
    r2a,
    r2b,
    r2c,
    s2,
    gbuf,
    igb,
    kvp,
    kvs,
    kvr,
    ka,
    kb,
    kc,
    kvo,
    st,
    spf,
    spb,
    spr,
    scs,
    scr,
    scn,
    nacc,
    nsend,
    npl,
    nsend2,
    nxc,
    loc,
    sp_s,
    sp_r,
    u_s,
    u_r,
    x_s,
    x_r,
    w_s,
    w_r,
    ag_s,
    ag_r,
    rs_s,
    rs_r,
    g_s,
    g_r,
    ig_s,
    ig_r,
    kv_s,
    kv_r,
    np_s,
    np_r,
    nx_s,
    nx_r,
    sc_s,
    sc_r,
):
    layers, tok, cols = x_in.shape
    half = cols // 2
    ck = half // NK
    rows = master.shape[1]
    feats = u_in.shape[2]
    y, xh, z, xl, c = (lax.axis_index(a) for a in (Y, XH, Z, XL, CO))
    x = 2 * xh + xl
    me_r = 2 * xl + c

    def ring(v, d):
        return lax.rem(v + (d + 4), 4)

    def to_x(v, core=None):
        dev = {XH: v // 2, XL: lax.rem(v, 2)}
        if core is not None:
            dev[CO] = core
        return dev

    xn = {d: ring(x, d) for d in (1, -1)}
    xn_h = {d: xn[d] // 2 for d in (1, -1)}
    plane_axis = {0: (Y, Z), 1: (Z, Y)}
    plane_pos = {Y: y, Z: z}
    DIRS = ((0, 1), (1, -1))

    def remote(src, dst, ss, rs, dev):
        return pltpu.make_async_remote_copy(
            src_ref=src, dst_ref=dst, send_sem=ss, recv_sem=rs, device_id=dev, device_id_type=MESH_ID
        )

    states = (master, first, second)
    spares = (sp_master, sp_first, sp_second)
    loads_sp = [pltpu.make_async_copy(spares[i], spf.at[i], loc.at[i]) for i in range(3)]
    loads_st = [pltpu.make_async_copy(states[i], st.at[i], loc.at[3 + i]) for i in range(3)]
    load_u = pltpu.make_async_copy(u_in, ubuf.at[:, xh], loc.at[6])
    loads_sp[0].start()
    loads_st[0].start()
    load_u.start()
    loads_sp[1].start()
    loads_sp[2].start()
    loads_st[1].start()
    loads_st[2].start()

    nxt_r = lax.rem(me_r + 1, 4)
    prv_r = lax.rem(me_r + 3, 4)
    plane_peers = [(dy, dz) for dy in range(4) for dz in range(4) if (dy, dz) != (0, 0)]
    xc_peers = [(dx, dc) for dx in range(4) for dc in range(2) if (dx, dc) != (0, 0)]

    def plane_dev(dy, dz):
        return {Y: lax.rem(y + dy, 4), Z: lax.rem(z + dz, 4)}

    def xc_dev(dx, dc):
        v = lax.rem(x + dx, 4)
        return {XH: v // 2, XL: lax.rem(v, 2), CO: lax.rem(c + dc, 2)}

    barrier = pltpu.get_barrier_semaphore()
    for p in plane_peers:
        pl.semaphore_signal(barrier, inc=1, device_id=plane_dev(*p), device_id_type=MESH_ID)
    for p in xc_peers:
        pl.semaphore_signal(barrier, inc=1, device_id=xc_dev(*p), device_id_type=MESH_ID)

    nxt_dev = {XL: nxt_r // 2, CO: lax.rem(nxt_r, 2)}

    def spare_copy(i, l):
        if i == 0:
            return remote(spb.at[0, l], spr.at[0, l], sp_s.at[l], sp_r.at[l], nxt_dev)
        return remote(spb.at[i], spr.at[i], sp_s.at[1 + i], sp_r.at[1 + i], nxt_dev)

    scale_copy = remote(scs, scr, sp_s.at[4], sp_r.at[4], nxt_dev)

    def sc_copy(di, d):
        return remote(scr, scn.at[xh], sc_s.at[di], sc_r.at[di], to_x(xn[d]))

    def x_copy(k, l, di, d):
        src = x_in.at[l, :, pl.ds(pl.multiple_of(xn_h[d] * half + k * ck, ck), ck)]
        return remote(src, xbuf.at[k, l, xh], x_s.at[k, l, di], x_r.at[k, l, di], to_x(xn[d]))

    def w_copy(l, di, d):
        return remote(
            wsb.at[xn_h[d], :, l], wbuf.at[:, l, y, xh, z], w_s.at[l, di], w_r.at[l, di], to_x(xn[d])
        )

    u_far = lax.rem(x + 1 + 2 * (1 - lax.rem(x, 2)), 4)

    def u_copy(part):
        span = slice(part * (tok // 2), (part + 1) * (tok // 2))
        return remote(u_in.at[c, span], ubuf.at[c, xh, span], u_s.at[part], u_r.at[part], to_x(u_far))

    u_fwd = remote(ubuf.at[c, 1 - xh], ubuf.at[c, 1 - xh], u_s.at[2], u_r.at[2], {CO: 1 - c})

    def region(k, l, stage, p, h):
        hs = slice(None) if h is None else h
        if l == 0:
            return wbuf.at[k, 0, p, hs, z] if stage == 0 else wbuf.at[k, 0, :, hs, p]
        return wbuf.at[k, 1, y, hs, p] if stage == 0 else wbuf.at[k, 1, p, hs, :]

    def ag_copy(k, l, stage, step, di, d):
        axis = plane_axis[l][stage]
        pos = plane_pos[axis]
        ref = region(k, l, stage, pos, None) if step == 0 else region(k, l, stage, ring(pos, -d), di)
        n = stage * 2 + step
        return remote(ref, ref, ag_s.at[k, l, n, di], ag_r.at[k, l, n, di], {axis: ring(pos, d)})

    def dw_piece(k, l, p, h):
        return dwbuf.at[k, 0, :, h, p] if l == 0 else dwbuf.at[k, 1, p, h, :]

    def rs_parts(k, l, stage):
        axis = plane_axis[l][1 - stage]
        if stage == 0:
            return axis, (lambda p, h: dw_piece(k, l, p, h)), r1a, r1b, r1c
        return axis, (lambda p, h: s1.at[k, l, h, p]), r2a, r2b, r2c

    def rs_copy(k, l, stage, what, di, d):
        axis, piece, ra, rb, rc = rs_parts(k, l, stage)
        pos = plane_pos[axis]
        if what == 0:
            src, dst = piece(ring(pos, 2), di), ra.at[k, l, di]
        elif what == 1:
            src, dst = piece(ring(pos, d), 1 - di), rb.at[k, l, di]
        else:
            src, dst = ra.at[k, l, di], rc.at[k, l, di]
        n = stage * 3 + what
        return remote(src, dst, rs_s.at[k, l, n, di], rs_r.at[k, l, n, di], {axis: ring(pos, d)})

    def rs_start(k, l, stage):
        for what in (0, 1):
            for di, d in DIRS:
                rs_copy(k, l, stage, what, di, d).start()

    def each(stage, fn):
        if stage == 0:

            @pl.loop(0, 4)
            def _(j):
                fn(j)
        else:
            fn(None)

    def at(ref, j):
        return ref[j] if j is not None else ref[...]

    def rs_forward(k, l, stage):
        axis, piece, ra, rb, rc = rs_parts(k, l, stage)
        pos = plane_pos[axis]
        for di, d in DIRS:
            rs_copy(k, l, stage, 0, di, d).wait_recv()
            own = piece(ring(pos, d), di)
            acc = ra.at[k, l, di]

            def add(j, own=own, acc=acc):
                total = (at(acc, j).astype(F32) + at(own, j).astype(F32)).astype(BF)
                if j is None:
                    acc[...] = total
                else:
                    acc[j] = total

            each(stage, add)
            rs_copy(k, l, stage, 2, di, d).start()

    def rs_finish(k, l, stage):
        axis, piece, ra, rb, rc = rs_parts(k, l, stage)
        pos = plane_pos[axis]
        for what in (1, 2):
            for di, d in DIRS:
                rs_copy(k, l, stage, what, di, d).wait_recv()
        for h in range(2):
            own = piece(pos, h)
            through = rc.at[k, l, h]
            direct = rb.at[k, l, 1 - h]
            out = s1.at[k, l, h] if stage == 0 else s2.at[k, l, h]

            def add(j, own=own, through=through, direct=direct, out=out):
                total = at(own, j).astype(F32) + at(through, j).astype(F32) + at(direct, j).astype(F32)
                if j is None:
                    out[...] = total.astype(BF)
                else:
                    out[j] = total.astype(BF)

            each(stage, add)

    def g_copy(k, l, di, d):
        return remote(
            s2.at[k, l, xn_h[d]], gbuf.at[k, l, xh], g_s.at[k, l, di], g_r.at[k, l, di], to_x(xn[d])
        )

    def ig_copy(k, l, di, d):
        dst = ig_out.at[l, :, pl.ds(pl.multiple_of(xh * half + k * ck, ck), ck)]
        return remote(igb.at[k, l, xn_h[d]], dst, ig_s.at[k, l, di], ig_r.at[k, l, di], to_x(xn[d]))

    kv_core = remote(kvs, kvr, kv_s.at[0], kv_r.at[0], {CO: 1 - c})

    def kv_piece(v, l):
        return kvr.at[lax.rem(v, 2), l, v // 2]

    def kv_copy(what, di, d):
        if what == 0:
            src, dst = kv_piece(ring(x, 2), di), ka.at[di]
        elif what == 1:
            src, dst = kv_piece(ring(x, d), 1 - di), kb.at[di]
        else:
            src, dst = ka.at[di], kc.at[di]
        n = 1 + what * 2 + di
        return remote(src, dst, kv_s.at[n], kv_r.at[n], to_x(xn[d]))

    kv_store = pltpu.make_async_copy(kvo, kv_out, loc.at[7])
    np_copies = [
        remote(nsend, npl.at[i], np_s.at[i], np_r.at[i], plane_dev(*p)) for i, p in enumerate(plane_peers)
    ]
    nx_copies = [
        remote(nsend2, nxc.at[i], nx_s.at[i], nx_r.at[i], xc_dev(*p)) for i, p in enumerate(xc_peers)
    ]
    stores = [
        pltpu.make_async_copy(st.at[i], out, loc.at[8 + i]) for i, out in enumerate((nm_out, nf_out, ns_out))
    ]

    lost = jnp.broadcast_to(failed[...], (rows, ck)) == me_r

    def begin():
        loads_sp[0].wait()
        for l in range(layers):
            spb[0, l] = spf[0, l].astype(BF)
        scs[...] = jnp.broadcast_to(scale_spare[...], scs.shape)
        pl.semaphore_wait(barrier, len(plane_peers) + len(xc_peers))
        u_copy(0).start()
        for l in range(layers):
            spare_copy(0, l).start()
        scale_copy.start()
        loads_st[0].wait()

    def recover(l):
        spare_copy(0, l).wait_recv()
        for j in range(2 * NK):
            span = slice(j * ck, (j + 1) * ck)
            now = jnp.where(lost, spr[0, l, :, span].astype(F32), st[0, l, :, span])
            st[0, l, :, span] = now
            wsb[j // NK, j % NK, l] = now.astype(BF)
        for di, d in DIRS:
            w_copy(l, di, d).start()

    def exchange():
        u_copy(1).start()
        n = 0
        for k in range(NK):
            for l in range(layers):
                for di, d in DIRS:
                    x_copy(k, l, di, d).start()
                if n == SPARES_AT:
                    for i in (1, 2):
                        loads_sp[i].wait()
                        for ll in range(layers):
                            spb[i, ll] = spf[i, ll].astype(BF)
                        spare_copy(i, 0).start()
                n += 1
        scale_copy.wait_recv()
        lost_tile = jnp.broadcast_to(failed[...], scr.shape) == me_r
        scr[...] = jnp.where(lost_tile, scr[...], jnp.broadcast_to(scale_own[...], scr.shape))
        nacc[...] = jnp.zeros(nacc.shape, F32)
        load_u.wait()
        for di, d in DIRS:
            sc_copy(di, d).start()

    def forward_u():
        for part in range(2):
            u_copy(part).wait_recv()
        u_fwd.start()

    def transpose_u():
        u_fwd.wait_recv()
        for l in range(layers):

            @pl.loop(0, 4)
            def _(j):
                span = pl.ds(pl.multiple_of(j * (feats // 4), feats // 4), feats // 4)
                for t in range(2):
                    ut[l, j, :, t * tok : (t + 1) * tok] = ubuf[l, t, :, span].T

    got_w = set()

    def gather_0(k, l):
        if l not in got_w:
            got_w.add(l)
            for di, d in DIRS:
                w_copy(l, di, d).wait_recv()
        for di, d in DIRS:
            ag_copy(k, l, 0, 0, di, d).start()

    def gather_forward(stage, k, l):
        for di, d in DIRS:
            ag_copy(k, l, stage, 0, di, d).wait_recv()
            ag_copy(k, l, stage, 1, di, d).start()

    def gather_1(k, l):
        for di, d in DIRS:
            ag_copy(k, l, 0, 1, di, d).wait_recv()
        for di, d in DIRS:
            ag_copy(k, l, 1, 0, di, d).start()

    def gathered(k, l):
        for di, d in DIRS:
            ag_copy(k, l, 1, 1, di, d).wait_recv()

    got_x = set()

    def need_x(k, l):
        if (k, l) not in got_x:
            got_x.add((k, l))
            for di, d in DIRS:
                x_copy(k, l, di, d).wait_recv()

    def grad_product(k, l):
        need_x(k, l)

        @pl.loop(0, 4)
        def _(j):
            inputs = xbuf[k, l].reshape(2 * tok, ck)
            part = jnp.dot(ut[l, j], inputs, preferred_element_type=F32)
            dwbuf[k, l, j] = part.astype(BF).reshape(2, 4, rows, ck)

        rs_start(k, l, 0)

    def finish_0(k, l):
        rs_finish(k, l, 0)
        rs_start(k, l, 1)

    got_scale = set()

    def finish_1(k, l):
        rs_finish(k, l, 1)
        for di, d in DIRS:
            g_copy(k, l, di, d).start()
        if not got_scale:
            got_scale.add(1)
            for di, d in DIRS:
                sc_copy(di, d).wait_recv()
        total = jnp.zeros((rows, ck), F32)
        for h in range(2):
            grad = s2[k, l, h].astype(F32) / jnp.broadcast_to(scn[h, 0:1, 0:1], (rows, ck))
            total = total + grad * grad
        nacc[...] += total

    kv_begun = set()

    def kv_product(k, l):
        need_x(k, l)
        fresh = l not in kv_begun
        kv_begun.add(l)

        @pl.loop(0, 4)
        def _(j):
            inputs = xbuf[k, l].reshape(2 * tok, ck)
            weight = wbuf[k, l, j].reshape(8 * rows, ck)
            part = lax.dot_general(
                inputs, weight, (((1,), (1,)), ((), ())), preferred_element_type=F32
            ).reshape(2, tok, 8 * rows)
            if fresh:
                kvp[j, l] = part
            else:
                kvp[j, l] += part

    def ig_product(k, l):
        @pl.loop(0, 2)
        def _(t):
            weight = wbuf[k, l].reshape(feats, ck)
            igb[k, l, t] = jnp.dot(ubuf[l, t], weight, preferred_element_type=F32).astype(BF)

        for di, d in DIRS:
            ig_copy(k, l, di, d).start()

    def kv_cores():
        for v in range(2):
            kvs[v] = kvp[2 * v + (1 - c)].astype(BF)
        kv_core.start()

    def kv_ring():
        kv_core.wait_recv()
        for v in range(2):
            for l in range(layers):
                kvr[v, l] = (kvr[v, l].astype(F32) + kvp[2 * v + c, l]).astype(BF)
        for what in (0, 1):
            for di, d in DIRS:
                kv_copy(what, di, d).start()

    def kv_forward():
        for di, d in DIRS:
            kv_copy(0, di, d).wait_recv()
            ka[di] = (ka[di].astype(F32) + kv_piece(ring(x, d), di)[...].astype(F32)).astype(BF)
            kv_copy(2, di, d).start()

    def kv_finish():
        for what in (1, 2):
            for di, d in DIRS:
                kv_copy(what, di, d).wait_recv()
        for h in range(2):
            own = kv_piece(x, h)[...].astype(F32)
            kvo[h] = (own + kc[h].astype(F32) + kb[1 - h].astype(F32)).astype(BF)
        kv_store.start()

    def squares_plane():
        tile = jnp.zeros((8, 128), F32)
        for i in range(rows // 8):
            for j in range(ck // 128):
                tile = tile + nacc[8 * i : 8 * i + 8, 128 * j : 128 * j + 128]
        nsend[...] = tile
        for cp in np_copies:
            cp.start()

    def squares_rest():
        total = nsend[...]
        for i, cp in enumerate(np_copies):
            cp.wait_recv()
            total = total + npl[i]
        nsend2[...] = total
        for cp in nx_copies:
            cp.start()

    def adam():
        for i in (1, 2):
            loads_st[i].wait()
            spare_copy(i, 0).wait_recv()
        for k in range(NK):
            for l in range(layers):
                for di, d in DIRS:
                    g_copy(k, l, di, d).wait_recv()
        total = nsend2[...]
        for i, cp in enumerate(nx_copies):
            cp.wait_recv()
            total = total + nxc[i]
        squares = jnp.sum(jnp.sum(total, axis=1, keepdims=True), axis=0, keepdims=True)
        factor = jnp.minimum(1.0, lax.rsqrt(squares / entries + MEAN_EPS))
        factor = jnp.broadcast_to(factor, (rows, ck))
        scale = jnp.broadcast_to(scr[0:1, 0:1], (rows, ck))

        @pl.loop(0, 2 * NK)
        def _(j):
            span = pl.ds(pl.multiple_of(j * ck, ck), ck)
            h = j // NK
            k = lax.rem(j, NK)
            for l in range(layers):
                clipped = gbuf[k, l, h].astype(F32) / scale * factor
                first_now = jnp.where(lost, spr[1, l, :, span].astype(F32), st[1, l, :, span])
                second_now = jnp.where(lost, spr[2, l, :, span].astype(F32), st[2, l, :, span])
                master_now = st[0, l, :, span]
                new_first = BETA_FIRST * first_now + (1.0 - BETA_FIRST) * clipped
                new_second = BETA_SECOND * second_now + (1.0 - BETA_SECOND) * clipped * clipped
                st[0, l, :, span] = master_now - LEARN_RATE * (
                    new_first / (jnp.sqrt(new_second) + ADAM_EPS) + DECAY_RATE * master_now
                )
                st[1, l, :, span] = new_first
                st[2, l, :, span] = new_second

        for cp in stores:
            cp.start()

    steps = {
        "INI": begin,
        "WSEL": recover,
        "XREST": exchange,
        "UF": forward_u,
        "TR": transpose_u,
        "A1": gather_0,
        "F0": functools.partial(gather_forward, 0),
        "S1": gather_1,
        "F1": functools.partial(gather_forward, 1),
        "WD": gathered,
        "DW": grad_product,
        "RF0": lambda k, l: rs_forward(k, l, 0),
        "RE0": finish_0,
        "RF1": lambda k, l: rs_forward(k, l, 1),
        "RE1": finish_1,
        "KV": kv_product,
        "IG": ig_product,
        "KVC": kv_cores,
        "KVA": kv_ring,
        "KVF": kv_forward,
        "KVE": kv_finish,
        "SQ": squares_plane,
        "NX": squares_rest,
        "AD": adam,
        "END": lambda: None,
    }
    for name, *where in ORDER:
        steps[name](*where)

    for l in range(layers):
        spare_copy(0, l).wait_send()
    for i in (1, 2):
        spare_copy(i, 0).wait_send()
    scale_copy.wait_send()
    for part in range(2):
        u_copy(part).wait_send()
    for di, d in DIRS:
        sc_copy(di, d).wait_send()
    u_fwd.wait_send()
    kv_core.wait_send()
    for l in range(layers):
        for di, d in DIRS:
            w_copy(l, di, d).wait_send()
    for what in range(3):
        for di, d in DIRS:
            kv_copy(what, di, d).wait_send()
    for cp in np_copies + nx_copies:
        cp.wait_send()

    @pl.loop(0, NK)
    def _(k):
        for l in range(layers):
            for di, d in DIRS:
                x_copy(k, l, di, d).wait_send()
                ig_copy(k, l, di, d).wait_send()
                g_copy(k, l, di, d).wait_send()
                for stage in range(2):
                    for step in range(2):
                        ag_copy(k, l, stage, step, di, d).wait_send()
                    for what in range(3):
                        rs_copy(k, l, stage, what, di, d).wait_send()
                ig_copy(k, l, di, d).wait_recv()

    kv_store.wait()
    for cp in stores:
        cp.wait()


def local(
    layer_input,
    kv_cotangent,
    failed_member,
    master,
    first_moment,
    second_moment,
    loss_scale,
    spare_master,
    spare_first,
    spare_second,
    spare_scale,
):
    layers, tok, cols = layer_input.shape
    rows = master.shape[1]
    feats = kv_cotangent.shape[2]
    half = cols // 2
    ck = half // NK
    entries = float(layers * rows * lax.axis_size(FSDP) * cols * lax.axis_size(RED))
    any_ = pl.BlockSpec(memory_space=pl.ANY)
    vmem = pl.BlockSpec(memory_space=pltpu.VMEM)
    sem = pltpu.SemaphoreType.DMA
    scratch = [
        pltpu.VMEM((NK, layers, 2, tok, ck), BF),
        pltpu.VMEM((layers, 2, tok, feats), BF),
        pltpu.VMEM((layers, 4, feats // 4, 2 * tok), BF),
        pltpu.VMEM((2, NK, layers, rows, ck), BF),
        pltpu.VMEM((NK, layers, 4, 2, 4, rows, ck), BF),
        pltpu.VMEM((NK, layers, 4, 2, 4, rows, ck), BF),
        pltpu.VMEM((NK, layers, 2, 4, rows, ck), BF),
        pltpu.VMEM((NK, layers, 2, 4, rows, ck), BF),
        pltpu.VMEM((NK, layers, 2, 4, rows, ck), BF),
        pltpu.VMEM((NK, layers, 2, 4, rows, ck), BF),
        pltpu.VMEM((NK, layers, 2, rows, ck), BF),
        pltpu.VMEM((NK, layers, 2, rows, ck), BF),
        pltpu.VMEM((NK, layers, 2, rows, ck), BF),
        pltpu.VMEM((NK, layers, 2, rows, ck), BF),
        pltpu.VMEM((NK, layers, 2, rows, ck), BF),
        pltpu.VMEM((NK, layers, 2, tok, ck), BF),
        pltpu.VMEM((4, layers, 2, tok, feats // 4), F32),
        pltpu.VMEM((2, layers, 2, tok, feats // 4), BF),
        pltpu.VMEM((2, layers, 2, tok, feats // 4), BF),
        pltpu.VMEM((2, tok, feats // 4), BF),
        pltpu.VMEM((2, tok, feats // 4), BF),
        pltpu.VMEM((2, tok, feats // 4), BF),
        pltpu.VMEM((2, tok, feats // 4), BF),
        pltpu.VMEM((3, layers, rows, cols), F32),
        pltpu.VMEM((3, layers, rows, cols), F32),
        pltpu.VMEM((3, layers, rows, cols), BF),
        pltpu.VMEM((3, layers, rows, cols), BF),
        pltpu.VMEM((8, 128), F32),
        pltpu.VMEM((8, 128), F32),
        pltpu.VMEM((2, 8, 128), F32),
        pltpu.VMEM((rows, ck), F32),
        pltpu.VMEM((8, 128), F32),
        pltpu.VMEM((15, 8, 128), F32),
        pltpu.VMEM((8, 128), F32),
        pltpu.VMEM((7, 8, 128), F32),
        sem((11,)),
        sem((5,)),
        sem((5,)),
        sem((3,)),
        sem((3,)),
        sem((NK, layers, 2)),
        sem((NK, layers, 2)),
        sem((layers, 2)),
        sem((layers, 2)),
        sem((NK, layers, 4, 2)),
        sem((NK, layers, 4, 2)),
        sem((NK, layers, 6, 2)),
        sem((NK, layers, 6, 2)),
        sem((NK, layers, 2)),
        sem((NK, layers, 2)),
        sem((NK, layers, 2)),
        sem((NK, layers, 2)),
        sem((7,)),
        sem((7,)),
        sem((15,)),
        sem((15,)),
        sem((7,)),
        sem((7,)),
        sem((2,)),
        sem((2,)),
    ]
    return pl.pallas_call(
        functools.partial(kernel, entries),
        out_shape=(
            jax.ShapeDtypeStruct((layers, tok, feats // 4), BF),
            jax.ShapeDtypeStruct((layers, tok, cols), BF),
            jax.ShapeDtypeStruct(master.shape, F32),
            jax.ShapeDtypeStruct(master.shape, F32),
            jax.ShapeDtypeStruct(master.shape, F32),
        ),
        in_specs=[any_, any_, vmem, vmem, vmem] + [any_] * 6,
        out_specs=(any_,) * 5,
        scratch_shapes=scratch,
        compiler_params=pltpu.CompilerParams(
            collective_id=0, has_side_effects=True, vmem_limit_bytes=67043328
        ),
        name="restore_step",
    )(
        layer_input,
        kv_cotangent,
        failed_member.reshape(1, 1),
        loss_scale,
        spare_scale,
        master,
        first_moment,
        second_moment,
        spare_master,
        spare_first,
        spare_second,
    )


def solution(mesh):
    split = Mesh(mesh.devices.reshape(4, 2, 4, 2, 2), (Y, XH, Z, XL, CO))
    placed = (
        P(None, FSDP, RED),
        P(None, FSDP, None),
        P(FSDP),
        P(None, FSDP, RED),
        P(None, FSDP, RED),
        P(None, FSDP, RED),
        P(FSDP, RED),
        P(None, FSDP, RED),
        P(None, FSDP, RED),
        P(None, FSDP, RED),
        P(FSDP, RED),
    )
    return jax.shard_map(
        local,
        mesh=split,
        in_specs=placed,
        out_specs=(P(None, FSDP, RED),) * 5,
        check_vma=False,
    )
```

```python
import functools

import jax
import jax.numpy as jnp
from jax import lax
from jax.experimental import pallas as pl
from jax.experimental.pallas import tpu as pltpu
from jax.sharding import Mesh
from jax.sharding import PartitionSpec as P

Y, XH, Z, XL, CO = "fsdp_0", "fsdp_1", "fsdp_2", "red_0", "red_1"
RED = (XL, CO)
FSDP = (Y, XH, Z)
MESH_ID = pl.DeviceIdType.MESH

BETA_FIRST = 0.9
BETA_SECOND = 0.95
LEARN_RATE = 0.01
DECAY_RATE = 0.1
ADAM_EPS = 1e-08
MEAN_EPS = 1e-06

NK = 4
SPARES_AT = 4
ORDER = (
    ("INI",),
    ("WSEL", 0),
    ("WSEL", 1),
    ("XREST",),
    ("A1", 0, 0),
    ("A1", 1, 0),
    ("A1", 2, 0),
    ("A1", 3, 0),
    ("A1", 0, 1),
    ("A1", 1, 1),
    ("A1", 2, 1),
    ("A1", 3, 1),
    ("F0", 0, 0),
    ("F0", 1, 0),
    ("F0", 2, 0),
    ("F0", 0, 1),
    ("F0", 3, 0),
    ("F0", 1, 1),
    ("S1", 0, 0),
    ("UF",),
    ("S1", 1, 0),
    ("F0", 2, 1),
    ("S1", 2, 0),
    ("S1", 3, 0),
    ("F0", 3, 1),
    ("TR",),
    ("S1", 0, 1),
    ("S1", 1, 1),
    ("DW", 0, 0),
    ("F1", 0, 0),
    ("DW", 0, 1),
    ("F1", 0, 1),
    ("F1", 1, 0),
    ("S1", 2, 1),
    ("DW", 1, 0),
    ("F1", 1, 1),
    ("RF0", 0, 1),
    ("F1", 2, 0),
    ("DW", 1, 1),
    ("WD", 0, 1),
    ("KV", 0, 1),
    ("IG", 0, 1),
    ("S1", 3, 1),
    ("F1", 3, 0),
    ("DW", 2, 0),
    ("RF0", 0, 0),
    ("F1", 2, 1),
    ("WD", 1, 1),
    ("KV", 1, 1),
    ("IG", 1, 1),
    ("WD", 0, 0),
    ("KV", 0, 0),
    ("RE0", 0, 1),
    ("WD", 1, 0),
    ("KV", 1, 0),
    ("RF0", 1, 1),
    ("IG", 0, 0),
    ("RF0", 1, 0),
    ("IG", 1, 0),
    ("DW", 2, 1),
    ("DW", 3, 0),
    ("WD", 2, 0),
    ("KV", 2, 0),
    ("IG", 2, 0),
    ("F1", 3, 1),
    ("WD", 3, 0),
    ("KV", 3, 0),
    ("IG", 3, 0),
    ("WD", 2, 1),
    ("KV", 2, 1),
    ("RF0", 2, 0),
    ("RE0", 1, 1),
    ("IG", 2, 1),
    ("DW", 3, 1),
    ("RF0", 2, 1),
    ("RE0", 0, 0),
    ("RF1", 0, 1),
    ("WD", 3, 1),
    ("KV", 3, 1),
    ("KVC",),
    ("RE0", 1, 0),
    ("RF0", 3, 1),
    ("RF0", 3, 0),
    ("KVA",),
    ("RE0", 2, 1),
    ("RE0", 2, 0),
    ("RF1", 0, 0),
    ("RF1", 1, 1),
    ("RF1", 1, 0),
    ("RE1", 0, 1),
    ("RE0", 3, 0),
    ("RE0", 3, 1),
    ("RF1", 2, 1),
    ("RF1", 2, 0),
    ("RE1", 1, 1),
    ("RE1", 0, 0),
    ("RE1", 1, 0),
    ("RF1", 3, 1),
    ("RF1", 3, 0),
    ("RE1", 2, 1),
    ("RE1", 2, 0),
    ("RE1", 3, 1),
    ("RE1", 3, 0),
    ("SQ",),
    ("NX",),
    ("IG", 3, 1),
    ("KVF",),
    ("AD",),
    ("END",),
    ("KVE",),
)
BF = jnp.bfloat16
F32 = jnp.float32


def kernel(
    entries,
    x_in,
    u_in,
    failed,
    scale_own,
    scale_spare,
    master,
    first,
    second,
    sp_master,
    sp_first,
    sp_second,
    kv_out,
    ig_out,
    nm_out,
    nf_out,
    ns_out,
    xbuf,
    ubuf,
    ut,
    wsb,
    wbuf,
    dwbuf,
    r1a,
    r1b,
    r1c,
    s1,
    r2a,
    r2b,
    r2c,
    s2,
    gbuf,
    igb,
    kvp,
    kvs,
    kvr,
    ka,
    kb,
    kc,
    spf,
    spb,
    spr,
    scs,
    scr,
    scn,
    nacc,
    nsend,
    npl,
    nsend2,
    nxc,
    loc,
    sp_s,
    sp_r,
    u_s,
    u_r,
    x_s,
    x_r,
    w_s,
    w_r,
    ag_s,
    ag_r,
    rs_s,
    rs_r,
    g_s,
    g_r,
    ig_s,
    ig_r,
    kv_s,
    kv_r,
    np_s,
    np_r,
    nx_s,
    nx_r,
    sc_s,
    sc_r,
):
    layers, tok, cols = x_in.shape
    half = cols // 2
    ck = half // NK
    rows = master.shape[1]
    feats = u_in.shape[2]
    y, xh, z, xl, c = (lax.axis_index(a) for a in (Y, XH, Z, XL, CO))
    x = 2 * xh + xl
    me_r = 2 * xl + c

    def ring(v, d):
        return lax.rem(v + (d + 4), 4)

    def to_x(v, core=None):
        dev = {XH: v // 2, XL: lax.rem(v, 2)}
        if core is not None:
            dev[CO] = core
        return dev

    xn = {d: ring(x, d) for d in (1, -1)}
    xn_h = {d: xn[d] // 2 for d in (1, -1)}
    plane_axis = {0: (Y, Z), 1: (Z, Y)}
    plane_pos = {Y: y, Z: z}
    DIRS = ((0, 1), (1, -1))

    def remote(src, dst, ss, rs, dev):
        return pltpu.make_async_remote_copy(
            src_ref=src, dst_ref=dst, send_sem=ss, recv_sem=rs, device_id=dev, device_id_type=MESH_ID
        )

    states = (master, first, second)
    st = (nm_out, nf_out, ns_out)
    spares = (sp_master, sp_first, sp_second)
    loads_sp = [pltpu.make_async_copy(spares[i], spf.at[i], loc.at[i]) for i in range(3)]
    loads_st = [pltpu.make_async_copy(states[i], st[i], loc.at[3 + i]) for i in range(3)]
    load_u = pltpu.make_async_copy(u_in, ubuf.at[:, xh], loc.at[6])
    loads_sp[0].start()
    loads_st[0].start()
    load_u.start()
    loads_sp[1].start()
    loads_sp[2].start()
    loads_st[1].start()
    loads_st[2].start()

    nxt_r = lax.rem(me_r + 1, 4)
    prv_r = lax.rem(me_r + 3, 4)
    plane_peers = [(dy, dz) for dy in range(4) for dz in range(4) if (dy, dz) != (0, 0)]
    xc_peers = [(dx, dc) for dx in range(4) for dc in range(2) if (dx, dc) != (0, 0)]

    def plane_dev(dy, dz):
        return {Y: lax.rem(y + dy, 4), Z: lax.rem(z + dz, 4)}

    def xc_dev(dx, dc):
        v = lax.rem(x + dx, 4)
        return {XH: v // 2, XL: lax.rem(v, 2), CO: lax.rem(c + dc, 2)}

    barrier = pltpu.get_barrier_semaphore()
    for p in plane_peers:
        pl.semaphore_signal(barrier, inc=1, device_id=plane_dev(*p), device_id_type=MESH_ID)
    for p in xc_peers:
        pl.semaphore_signal(barrier, inc=1, device_id=xc_dev(*p), device_id_type=MESH_ID)

    nxt_dev = {XL: nxt_r // 2, CO: lax.rem(nxt_r, 2)}

    def spare_copy(i, l):
        if i == 0:
            return remote(spb.at[0, l], spr.at[0, l], sp_s.at[l], sp_r.at[l], nxt_dev)
        return remote(spb.at[i], spr.at[i], sp_s.at[1 + i], sp_r.at[1 + i], nxt_dev)

    scale_copy = remote(scs, scr, sp_s.at[4], sp_r.at[4], nxt_dev)

    def sc_copy(di, d):
        return remote(scr, scn.at[xh], sc_s.at[di], sc_r.at[di], to_x(xn[d]))

    def x_copy(k, l, di, d):
        src = x_in.at[l, :, pl.ds(pl.multiple_of(xn_h[d] * half + k * ck, ck), ck)]
        return remote(src, xbuf.at[k, l, xh], x_s.at[k, l, di], x_r.at[k, l, di], to_x(xn[d]))

    def w_copy(l, di, d):
        return remote(
            wsb.at[xn_h[d], :, l], wbuf.at[:, l, y, xh, z], w_s.at[l, di], w_r.at[l, di], to_x(xn[d])
        )

    u_far = lax.rem(x + 1 + 2 * (1 - lax.rem(x, 2)), 4)

    def u_copy(part):
        span = slice(part * (tok // 2), (part + 1) * (tok // 2))
        return remote(u_in.at[c, span], ubuf.at[c, xh, span], u_s.at[part], u_r.at[part], to_x(u_far))

    u_fwd = remote(ubuf.at[c, 1 - xh], ubuf.at[c, 1 - xh], u_s.at[2], u_r.at[2], {CO: 1 - c})

    def region(k, l, stage, p, h):
        hs = slice(None) if h is None else h
        if l == 0:
            return wbuf.at[k, 0, p, hs, z] if stage == 0 else wbuf.at[k, 0, :, hs, p]
        return wbuf.at[k, 1, y, hs, p] if stage == 0 else wbuf.at[k, 1, p, hs, :]

    def ag_copy(k, l, stage, step, di, d):
        axis = plane_axis[l][stage]
        pos = plane_pos[axis]
        ref = region(k, l, stage, pos, None) if step == 0 else region(k, l, stage, ring(pos, -d), di)
        n = stage * 2 + step
        return remote(ref, ref, ag_s.at[k, l, n, di], ag_r.at[k, l, n, di], {axis: ring(pos, d)})

    def dw_piece(k, l, p, h):
        return dwbuf.at[k, 0, :, h, p] if l == 0 else dwbuf.at[k, 1, p, h, :]

    def rs_parts(k, l, stage):
        axis = plane_axis[l][1 - stage]
        if stage == 0:
            return axis, (lambda p, h: dw_piece(k, l, p, h)), r1a, r1b, r1c
        return axis, (lambda p, h: s1.at[k, l, h, p]), r2a, r2b, r2c

    def rs_copy(k, l, stage, what, di, d):
        axis, piece, ra, rb, rc = rs_parts(k, l, stage)
        pos = plane_pos[axis]
        if what == 0:
            src, dst = piece(ring(pos, 2), di), ra.at[k, l, di]
        elif what == 1:
            src, dst = piece(ring(pos, d), 1 - di), rb.at[k, l, di]
        else:
            src, dst = ra.at[k, l, di], rc.at[k, l, di]
        n = stage * 3 + what
        return remote(src, dst, rs_s.at[k, l, n, di], rs_r.at[k, l, n, di], {axis: ring(pos, d)})

    def rs_start(k, l, stage):
        for what in (0, 1):
            for di, d in DIRS:
                rs_copy(k, l, stage, what, di, d).start()

    def each(stage, fn):
        if stage == 0:

            @pl.loop(0, 4)
            def _(j):
                fn(j)
        else:
            fn(None)

    def at(ref, j):
        return ref[j] if j is not None else ref[...]

    def rs_forward(k, l, stage):
        axis, piece, ra, rb, rc = rs_parts(k, l, stage)
        pos = plane_pos[axis]
        for di, d in DIRS:
            rs_copy(k, l, stage, 0, di, d).wait_recv()
            own = piece(ring(pos, d), di)
            acc = ra.at[k, l, di]

            def add(j, own=own, acc=acc):
                total = (at(acc, j).astype(F32) + at(own, j).astype(F32)).astype(BF)
                if j is None:
                    acc[...] = total
                else:
                    acc[j] = total

            each(stage, add)
            rs_copy(k, l, stage, 2, di, d).start()

    def rs_finish(k, l, stage):
        axis, piece, ra, rb, rc = rs_parts(k, l, stage)
        pos = plane_pos[axis]
        for what in (1, 2):
            for di, d in DIRS:
                rs_copy(k, l, stage, what, di, d).wait_recv()
        for h in range(2):
            own = piece(pos, h)
            through = rc.at[k, l, h]
            direct = rb.at[k, l, 1 - h]
            out = s1.at[k, l, h] if stage == 0 else s2.at[k, l, h]

            def add(j, own=own, through=through, direct=direct, out=out):
                total = at(own, j).astype(F32) + at(through, j).astype(F32) + at(direct, j).astype(F32)
                if j is None:
                    out[...] = total.astype(BF)
                else:
                    out[j] = total.astype(BF)

            each(stage, add)

    def g_copy(k, l, di, d):
        return remote(
            s2.at[k, l, xn_h[d]], gbuf.at[k, l, xh], g_s.at[k, l, di], g_r.at[k, l, di], to_x(xn[d])
        )

    def ig_copy(k, l, di, d):
        dst = ig_out.at[l, :, pl.ds(pl.multiple_of(xh * half + k * ck, ck), ck)]
        return remote(igb.at[k, l, xn_h[d]], dst, ig_s.at[k, l, di], ig_r.at[k, l, di], to_x(xn[d]))

    kv_core = remote(kvs, kvr, kv_s.at[0], kv_r.at[0], {CO: 1 - c})

    def kv_piece(v, l):
        return kvr.at[lax.rem(v, 2), l, v // 2]

    def kv_copy(what, di, d):
        if what == 0:
            src, dst = kv_piece(ring(x, 2), di), ka.at[di]
        elif what == 1:
            src, dst = kv_piece(ring(x, d), 1 - di), kb.at[di]
        else:
            src, dst = ka.at[di], kc.at[di]
        n = 1 + what * 2 + di
        return remote(src, dst, kv_s.at[n], kv_r.at[n], to_x(xn[d]))

    np_copies = [
        remote(nsend, npl.at[i], np_s.at[i], np_r.at[i], plane_dev(*p)) for i, p in enumerate(plane_peers)
    ]
    nx_copies = [
        remote(nsend2, nxc.at[i], nx_s.at[i], nx_r.at[i], xc_dev(*p)) for i, p in enumerate(xc_peers)
    ]

    lost = jnp.broadcast_to(failed[...], (rows, ck)) == me_r

    def begin():
        loads_sp[0].wait()
        for l in range(layers):
            spb[0, l] = spf[0, l].astype(BF)
        scs[...] = jnp.broadcast_to(scale_spare[...], scs.shape)
        pl.semaphore_wait(barrier, len(plane_peers) + len(xc_peers))
        u_copy(0).start()
        for l in range(layers):
            spare_copy(0, l).start()
        scale_copy.start()
        loads_st[0].wait()

    def recover(l):
        spare_copy(0, l).wait_recv()
        for j in range(2 * NK):
            span = slice(j * ck, (j + 1) * ck)
            now = jnp.where(lost, spr[0, l, :, span].astype(F32), st[0][l, :, span])
            st[0][l, :, span] = now
            wsb[j // NK, j % NK, l] = now.astype(BF)
        for di, d in DIRS:
            w_copy(l, di, d).start()

    def exchange():
        u_copy(1).start()
        n = 0
        for k in range(NK):
            for l in range(layers):
                for di, d in DIRS:
                    x_copy(k, l, di, d).start()
                if n == SPARES_AT:
                    for i in (1, 2):
                        loads_sp[i].wait()
                        for ll in range(layers):
                            spb[i, ll] = spf[i, ll].astype(BF)
                        spare_copy(i, 0).start()
                n += 1
        scale_copy.wait_recv()
        lost_tile = jnp.broadcast_to(failed[...], scr.shape) == me_r
        scr[...] = jnp.where(lost_tile, scr[...], jnp.broadcast_to(scale_own[...], scr.shape))
        nacc[...] = jnp.zeros(nacc.shape, F32)
        load_u.wait()
        for di, d in DIRS:
            sc_copy(di, d).start()

    def forward_u():
        for part in range(2):
            u_copy(part).wait_recv()
        u_fwd.start()

    def transpose_u():
        u_fwd.wait_recv()
        for l in range(layers):

            @pl.loop(0, 4)
            def _(j):
                span = pl.ds(pl.multiple_of(j * (feats // 4), feats // 4), feats // 4)
                for t in range(2):
                    ut[l, j, :, t * tok : (t + 1) * tok] = ubuf[l, t, :, span].T

    got_w = set()

    def gather_0(k, l):
        if l not in got_w:
            got_w.add(l)
            for di, d in DIRS:
                w_copy(l, di, d).wait_recv()
        for di, d in DIRS:
            ag_copy(k, l, 0, 0, di, d).start()

    def gather_forward(stage, k, l):
        for di, d in DIRS:
            ag_copy(k, l, stage, 0, di, d).wait_recv()
            ag_copy(k, l, stage, 1, di, d).start()

    def gather_1(k, l):
        for di, d in DIRS:
            ag_copy(k, l, 0, 1, di, d).wait_recv()
        for di, d in DIRS:
            ag_copy(k, l, 1, 0, di, d).start()

    def gathered(k, l):
        for di, d in DIRS:
            ag_copy(k, l, 1, 1, di, d).wait_recv()

    got_x = set()

    def need_x(k, l):
        if (k, l) not in got_x:
            got_x.add((k, l))
            for di, d in DIRS:
                x_copy(k, l, di, d).wait_recv()

    def grad_product(k, l):
        need_x(k, l)

        @pl.loop(0, 4)
        def _(j):
            inputs = xbuf[k, l].reshape(2 * tok, ck)
            part = jnp.dot(ut[l, j], inputs, preferred_element_type=F32)
            dwbuf[k, l, j] = part.astype(BF).reshape(2, 4, rows, ck)

        rs_start(k, l, 0)

    def finish_0(k, l):
        rs_finish(k, l, 0)
        rs_start(k, l, 1)

    got_scale = set()

    def finish_1(k, l):
        rs_finish(k, l, 1)
        for di, d in DIRS:
            g_copy(k, l, di, d).start()
        if not got_scale:
            got_scale.add(1)
            for di, d in DIRS:
                sc_copy(di, d).wait_recv()
        total = jnp.zeros((rows, ck), F32)
        for h in range(2):
            grad = s2[k, l, h].astype(F32) / jnp.broadcast_to(scn[h, 0:1, 0:1], (rows, ck))
            total = total + grad * grad
        nacc[...] += total

    kv_begun = set()

    def kv_product(k, l):
        need_x(k, l)
        fresh = l not in kv_begun
        kv_begun.add(l)

        @pl.loop(0, 4)
        def _(j):
            inputs = xbuf[k, l].reshape(2 * tok, ck)
            weight = wbuf[k, l, j].reshape(8 * rows, ck)
            part = lax.dot_general(
                inputs, weight, (((1,), (1,)), ((), ())), preferred_element_type=F32
            ).reshape(2, tok, 8 * rows)
            if fresh:
                kvp[j, l] = part
            else:
                kvp[j, l] += part

    def ig_product(k, l):
        @pl.loop(0, 2)
        def _(t):
            weight = wbuf[k, l].reshape(feats, ck)
            igb[k, l, t] = jnp.dot(ubuf[l, t], weight, preferred_element_type=F32).astype(BF)

        for di, d in DIRS:
            ig_copy(k, l, di, d).start()

    def kv_cores():
        for v in range(2):
            kvs[v] = kvp[2 * v + (1 - c)].astype(BF)
        kv_core.start()

    def kv_ring():
        kv_core.wait_recv()
        for v in range(2):
            for l in range(layers):
                kvr[v, l] = (kvr[v, l].astype(F32) + kvp[2 * v + c, l]).astype(BF)
        for what in (0, 1):
            for di, d in DIRS:
                kv_copy(what, di, d).start()

    def kv_forward():
        for di, d in DIRS:
            kv_copy(0, di, d).wait_recv()
            ka[di] = (ka[di].astype(F32) + kv_piece(ring(x, d), di)[...].astype(F32)).astype(BF)
            kv_copy(2, di, d).start()

    def kv_finish():
        for what in (1, 2):
            for di, d in DIRS:
                kv_copy(what, di, d).wait_recv()
        for h in range(2):
            own = kv_piece(x, h)[...].astype(F32)
            kv_out[h] = (own + kc[h].astype(F32) + kb[1 - h].astype(F32)).astype(BF)

    def squares_plane():
        tile = jnp.zeros((8, 128), F32)
        for i in range(rows // 8):
            for j in range(ck // 128):
                tile = tile + nacc[8 * i : 8 * i + 8, 128 * j : 128 * j + 128]
        nsend[...] = tile
        for cp in np_copies:
            cp.start()

    def squares_rest():
        total = nsend[...]
        for i, cp in enumerate(np_copies):
            cp.wait_recv()
            total = total + npl[i]
        nsend2[...] = total
        for cp in nx_copies:
            cp.start()

    def adam():
        for i in (1, 2):
            loads_st[i].wait()
            spare_copy(i, 0).wait_recv()
        for k in range(NK):
            for l in range(layers):
                for di, d in DIRS:
                    g_copy(k, l, di, d).wait_recv()
        total = nsend2[...]
        for i, cp in enumerate(nx_copies):
            cp.wait_recv()
            total = total + nxc[i]
        squares = jnp.sum(jnp.sum(total, axis=1, keepdims=True), axis=0, keepdims=True)
        factor = jnp.minimum(1.0, lax.rsqrt(squares / entries + MEAN_EPS))
        factor = jnp.broadcast_to(factor, (rows, ck))
        scale = jnp.broadcast_to(scr[0:1, 0:1], (rows, ck))

        @pl.loop(0, 2 * NK)
        def _(j):
            span = pl.ds(pl.multiple_of(j * ck, ck), ck)
            h = j // NK
            k = lax.rem(j, NK)
            for l in range(layers):
                clipped = gbuf[k, l, h].astype(F32) / scale * factor
                first_now = jnp.where(lost, spr[1, l, :, span].astype(F32), st[1][l, :, span])
                second_now = jnp.where(lost, spr[2, l, :, span].astype(F32), st[2][l, :, span])
                master_now = st[0][l, :, span]
                new_first = BETA_FIRST * first_now + (1.0 - BETA_FIRST) * clipped
                new_second = BETA_SECOND * second_now + (1.0 - BETA_SECOND) * clipped * clipped
                st[0][l, :, span] = master_now - LEARN_RATE * (
                    new_first / (jnp.sqrt(new_second) + ADAM_EPS) + DECAY_RATE * master_now
                )
                st[1][l, :, span] = new_first
                st[2][l, :, span] = new_second

    steps = {
        "INI": begin,
        "WSEL": recover,
        "XREST": exchange,
        "UF": forward_u,
        "TR": transpose_u,
        "A1": gather_0,
        "F0": functools.partial(gather_forward, 0),
        "S1": gather_1,
        "F1": functools.partial(gather_forward, 1),
        "WD": gathered,
        "DW": grad_product,
        "RF0": lambda k, l: rs_forward(k, l, 0),
        "RE0": finish_0,
        "RF1": lambda k, l: rs_forward(k, l, 1),
        "RE1": finish_1,
        "KV": kv_product,
        "IG": ig_product,
        "KVC": kv_cores,
        "KVA": kv_ring,
        "KVF": kv_forward,
        "KVE": kv_finish,
        "SQ": squares_plane,
        "NX": squares_rest,
        "AD": adam,
        "END": lambda: None,
    }
    for name, *where in ORDER:
        steps[name](*where)

    for l in range(layers):
        spare_copy(0, l).wait_send()
    for i in (1, 2):
        spare_copy(i, 0).wait_send()
    scale_copy.wait_send()
    for part in range(2):
        u_copy(part).wait_send()
    for di, d in DIRS:
        sc_copy(di, d).wait_send()
    u_fwd.wait_send()
    kv_core.wait_send()
    for l in range(layers):
        for di, d in DIRS:
            w_copy(l, di, d).wait_send()
    for what in range(3):
        for di, d in DIRS:
            kv_copy(what, di, d).wait_send()
    for cp in np_copies + nx_copies:
        cp.wait_send()

    @pl.loop(0, NK)
    def _(k):
        for l in range(layers):
            for di, d in DIRS:
                x_copy(k, l, di, d).wait_send()
                ig_copy(k, l, di, d).wait_send()
                g_copy(k, l, di, d).wait_send()
                for stage in range(2):
                    for step in range(2):
                        ag_copy(k, l, stage, step, di, d).wait_send()
                    for what in range(3):
                        rs_copy(k, l, stage, what, di, d).wait_send()
                ig_copy(k, l, di, d).wait_recv()


def store(*refs):
    sems = refs[10]
    copies = [pltpu.make_async_copy(refs[i], refs[5 + i], sems.at[i]) for i in range(5)]
    for cp in copies:
        cp.start()
    for cp in copies:
        cp.wait()


def local(
    layer_input,
    kv_cotangent,
    failed_member,
    master,
    first_moment,
    second_moment,
    loss_scale,
    spare_master,
    spare_first,
    spare_second,
    spare_scale,
):
    layers, tok, cols = layer_input.shape
    rows = master.shape[1]
    feats = kv_cotangent.shape[2]
    half = cols // 2
    ck = half // NK
    entries = float(layers * rows * lax.axis_size(FSDP) * cols * lax.axis_size(RED))
    any_ = pl.BlockSpec(memory_space=pl.ANY)
    vmem = pl.BlockSpec(memory_space=pltpu.VMEM)
    sem = pltpu.SemaphoreType.DMA
    scratch = [
        pltpu.VMEM((NK, layers, 2, tok, ck), BF),
        pltpu.VMEM((layers, 2, tok, feats), BF),
        pltpu.VMEM((layers, 4, feats // 4, 2 * tok), BF),
        pltpu.VMEM((2, NK, layers, rows, ck), BF),
        pltpu.VMEM((NK, layers, 4, 2, 4, rows, ck), BF),
        pltpu.VMEM((NK, layers, 4, 2, 4, rows, ck), BF),
        pltpu.VMEM((NK, layers, 2, 4, rows, ck), BF),
        pltpu.VMEM((NK, layers, 2, 4, rows, ck), BF),
        pltpu.VMEM((NK, layers, 2, 4, rows, ck), BF),
        pltpu.VMEM((NK, layers, 2, 4, rows, ck), BF),
        pltpu.VMEM((NK, layers, 2, rows, ck), BF),
        pltpu.VMEM((NK, layers, 2, rows, ck), BF),
        pltpu.VMEM((NK, layers, 2, rows, ck), BF),
        pltpu.VMEM((NK, layers, 2, rows, ck), BF),
        pltpu.VMEM((NK, layers, 2, rows, ck), BF),
        pltpu.VMEM((NK, layers, 2, tok, ck), BF),
        pltpu.VMEM((4, layers, 2, tok, feats // 4), F32),
        pltpu.VMEM((2, layers, 2, tok, feats // 4), BF),
        pltpu.VMEM((2, layers, 2, tok, feats // 4), BF),
        pltpu.VMEM((2, tok, feats // 4), BF),
        pltpu.VMEM((2, tok, feats // 4), BF),
        pltpu.VMEM((2, tok, feats // 4), BF),
        pltpu.VMEM((3, layers, rows, cols), F32),
        pltpu.VMEM((3, layers, rows, cols), BF),
        pltpu.VMEM((3, layers, rows, cols), BF),
        pltpu.VMEM((8, 128), F32),
        pltpu.VMEM((8, 128), F32),
        pltpu.VMEM((2, 8, 128), F32),
        pltpu.VMEM((rows, ck), F32),
        pltpu.VMEM((8, 128), F32),
        pltpu.VMEM((15, 8, 128), F32),
        pltpu.VMEM((8, 128), F32),
        pltpu.VMEM((7, 8, 128), F32),
        sem((7,)),
        sem((5,)),
        sem((5,)),
        sem((3,)),
        sem((3,)),
        sem((NK, layers, 2)),
        sem((NK, layers, 2)),
        sem((layers, 2)),
        sem((layers, 2)),
        sem((NK, layers, 4, 2)),
        sem((NK, layers, 4, 2)),
        sem((NK, layers, 6, 2)),
        sem((NK, layers, 6, 2)),
        sem((NK, layers, 2)),
        sem((NK, layers, 2)),
        sem((NK, layers, 2)),
        sem((NK, layers, 2)),
        sem((7,)),
        sem((7,)),
        sem((15,)),
        sem((15,)),
        sem((7,)),
        sem((7,)),
        sem((2,)),
        sem((2,)),
    ]
    results = (
        jax.ShapeDtypeStruct((layers, tok, feats // 4), BF),
        jax.ShapeDtypeStruct((layers, tok, cols), BF),
    ) + (jax.ShapeDtypeStruct(master.shape, F32),) * 3
    held = pl.pallas_call(
        functools.partial(kernel, entries),
        out_shape=tuple(pltpu.VMEM(r.shape, r.dtype) for r in results),
        in_specs=[any_, any_, vmem, vmem, vmem] + [any_] * 6,
        out_specs=(vmem,) * 5,
        scratch_shapes=scratch,
        compiler_params=pltpu.CompilerParams(
            collective_id=0, has_side_effects=True, vmem_limit_bytes=55 << 20
        ),
        name="restore_step",
    )(
        layer_input,
        kv_cotangent,
        failed_member.reshape(1, 1),
        loss_scale,
        spare_scale,
        master,
        first_moment,
        second_moment,
        spare_master,
        spare_first,
        spare_second,
    )
    return pl.pallas_call(
        store,
        out_shape=results,
        in_specs=[vmem] * 5,
        out_specs=(any_,) * 5,
        scratch_shapes=[sem((5,))],
        compiler_params=pltpu.CompilerParams(vmem_limit_bytes=1 << 20),
        name="store_results",
    )(*[pltpu.with_memory_space_constraint(h, pltpu.VMEM) for h in held])


def solution(mesh):
    split = Mesh(mesh.devices.reshape(4, 2, 4, 2, 2), (Y, XH, Z, XL, CO))
    placed = (
        P(None, FSDP, RED),
        P(None, FSDP, None),
        P(FSDP),
        P(None, FSDP, RED),
        P(None, FSDP, RED),
        P(None, FSDP, RED),
        P(FSDP, RED),
        P(None, FSDP, RED),
        P(None, FSDP, RED),
        P(None, FSDP, RED),
        P(FSDP, RED),
    )
    return jax.shard_map(
        local,
        mesh=split,
        in_specs=placed,
        out_specs=(P(None, FSDP, RED),) * 5,
        check_vma=False,
    )
```

```python
import functools

import jax
import jax.numpy as jnp
from jax import lax
from jax.experimental import pallas as pl
from jax.experimental.pallas import tpu as pltpu
from jax.sharding import Mesh
from jax.sharding import PartitionSpec as P

Y, XH, Z, XL, CO = "fsdp_0", "fsdp_1", "fsdp_2", "red_0", "red_1"
RED = (XL, CO)
FSDP = (Y, XH, Z)
MESH_ID = pl.DeviceIdType.MESH

BETA_FIRST = 0.9
BETA_SECOND = 0.95
LEARN_RATE = 0.01
DECAY_RATE = 0.1
ADAM_EPS = 1e-08
MEAN_EPS = 1e-06

NK = 4
WID = (512, 512, 512, 256)
OFF = tuple(sum(WID[:k]) for k in range(NK))
EW = 512
SPARES_AT = 0
ORDER = (
    ("INI",),
    ("WSEL", 0),
    ("WSEL", 1),
    ("XREST",),
    ("A1", 0, 0),
    ("A1", 1, 0),
    ("A1", 2, 0),
    ("A1", 3, 0),
    ("A1", 4, 0),
    ("F0", 0, 0),
    ("A1", 0, 1),
    ("A1", 1, 1),
    ("A1", 2, 1),
    ("A1", 3, 1),
    ("F0", 1, 0),
    ("A1", 4, 1),
    ("F0", 2, 0),
    ("F0", 3, 0),
    ("F0", 0, 1),
    ("UF",),
    ("F0", 4, 0),
    ("F0", 1, 1),
    ("S1", 0, 0),
    ("S1", 1, 0),
    ("F0", 2, 1),
    ("S1", 2, 0),
    ("TR",),
    ("F0", 4, 1),
    ("S1", 4, 0),
    ("F0", 3, 1),
    ("S1", 0, 1),
    ("DW", 4, 1),
    ("S1", 1, 1),
    ("DW", 4, 0),
    ("S1", 3, 0),
    ("DW", 0, 0),
    ("F1", 0, 0),
    ("F1", 0, 1),
    ("RF0", 4, 1),
    ("F1", 1, 0),
    ("S1", 2, 1),
    ("DW", 0, 1),
    ("F1", 2, 0),
    ("F1", 1, 1),
    ("S1", 4, 1),
    ("DW", 1, 0),
    ("WD", 0, 1),
    ("IG", 0, 1),
    ("KV", 0, 1),
    ("F1", 4, 0),
    ("RE0", 4, 1),
    ("S1", 3, 1),
    ("DW", 1, 1),
    ("RF0", 4, 0),
    ("F1", 2, 1),
    ("DW", 2, 0),
    ("RF0", 0, 1),
    ("F1", 3, 0),
    ("RF0", 0, 0),
    ("DW", 2, 1),
    ("WD", 1, 1),
    ("IG", 1, 1),
    ("KV", 1, 1),
    ("DW", 3, 0),
    ("WD", 0, 0),
    ("IG", 0, 0),
    ("KV", 0, 0),
    ("F1", 4, 1),
    ("WD", 1, 0),
    ("IG", 1, 0),
    ("DW", 3, 1),
    ("F1", 3, 1),
    ("WD", 2, 0),
    ("IG", 2, 0),
    ("KV", 1, 0),
    ("RF0", 1, 1),
    ("RF0", 1, 0),
    ("KV", 2, 0),
    ("WD", 2, 1),
    ("IG", 2, 1),
    ("WD", 4, 0),
    ("RF1", 4, 1),
    ("IG", 4, 0),
    ("RE0", 0, 1),
    ("KV", 4, 0),
    ("RE0", 4, 0),
    ("RF0", 2, 1),
    ("KV", 2, 1),
    ("RF0", 2, 0),
    ("WD", 4, 1),
    ("IG", 4, 1),
    ("WD", 3, 0),
    ("KV", 4, 1),
    ("RF0", 3, 1),
    ("KV", 3, 0),
    ("RE0", 0, 0),
    ("WD", 3, 1),
    ("KV", 3, 1),
    ("KVC",),
    ("RF0", 3, 0),
    ("RE0", 1, 1),
    ("RF1", 4, 0),
    ("RE0", 1, 0),
    ("RE1", 4, 1),
    ("KVA",),
    ("RF1", 0, 1),
    ("RE0", 2, 1),
    ("RE0", 3, 1),
    ("RF1", 0, 0),
    ("FE", 1),
    ("RE0", 2, 0),
    ("RE1", 4, 0),
    ("RE0", 3, 0),
    ("RF1", 1, 0),
    ("KVF",),
    ("RF1", 1, 1),
    ("RE1", 0, 0),
    ("RE1", 0, 1),
    ("RF1", 2, 0),
    ("RF1", 2, 1),
    ("RF1", 3, 0),
    ("RF1", 3, 1),
    ("RE1", 1, 0),
    ("RE1", 1, 1),
    ("RE1", 2, 0),
    ("FE", 0),
    ("RE1", 2, 1),
    ("RE1", 3, 0),
    ("RE1", 3, 1),
    ("SQ",),
    ("KVE",),
    ("NX",),
    ("IG", 3, 1),
    ("IG", 3, 0),
    ("AD",),
    ("END",),
)
BF = jnp.bfloat16
F32 = jnp.float32


def kernel(
    entries,
    x_in,
    u_in,
    failed_in,
    scale_own_in,
    scale_spare_in,
    master,
    first,
    second,
    sp_master,
    sp_first,
    sp_second,
    kv_out,
    ig_out,
    nm_out,
    nf_out,
    ns_out,
    xbuf,
    xe,
    ubuf,
    ut,
    wsb,
    wbuf,
    dwbuf,
    r1a,
    r1b,
    r1c,
    s1,
    r2a,
    r2b,
    r2c,
    s2,
    gbuf,
    grc,
    ge,
    igb,
    kvp,
    kvs,
    kvr,
    ka,
    kb,
    kc,
    spf,
    spb,
    spr,
    small,
    scs,
    scr,
    scn,
    nacc,
    nsend,
    npl,
    nsend2,
    nxc,
    loc,
    sp_s,
    sp_r,
    u_s,
    u_r,
    x_s,
    x_r,
    w_s,
    w_r,
    we_s,
    we_r,
    ge_s,
    ge_r,
    ag_s,
    ag_r,
    rs_s,
    rs_r,
    g_s,
    g_r,
    ig_s,
    ig_r,
    kv_s,
    kv_r,
    np_s,
    np_r,
    nx_s,
    nx_r,
    sc_s,
    sc_r,
):
    layers, tok, cols = x_in.shape
    half = cols // 2
    rows = master.shape[1]
    feats = u_in.shape[2]
    kept = half - EW // 2
    failed, scale_own, scale_spare = small[0], small[1], small[2]
    y, xh, z, xl, c = (lax.axis_index(a) for a in (Y, XH, Z, XL, CO))
    x = 2 * xh + xl
    me_r = 2 * xl + c

    def ring(v, d):
        return lax.rem(v + (d + 4), 4)

    def to_x(v, core=None):
        dev = {XH: v // 2, XL: lax.rem(v, 2)}
        if core is not None:
            dev[CO] = core
        return dev

    xn = {d: ring(x, d) for d in (1, -1)}
    xn_h = {d: xn[d] // 2 for d in (1, -1)}
    plane_axis = {0: (Y, Z), 1: (Z, Y)}
    plane_pos = {Y: y, Z: z}
    DIRS = ((0, 1), (1, -1))

    def remote(src, dst, ss, rs, dev):
        return pltpu.make_async_remote_copy(
            src_ref=src, dst_ref=dst, send_sem=ss, recv_sem=rs, device_id=dev, device_id_type=MESH_ID
        )

    states = (master, first, second)
    st = (nm_out, nf_out, ns_out)
    spares = (sp_master, sp_first, sp_second)
    loads_sp = [pltpu.make_async_copy(spares[i], spf, loc.at[i]) for i in range(3)]
    loads_st = [pltpu.make_async_copy(states[i], st[i], loc.at[3 + i]) for i in range(3)]
    load_u = pltpu.make_async_copy(u_in, ubuf.at[:, xh], loc.at[6])
    load_small = [
        pltpu.make_async_copy(ref, buf, loc.at[7 + i])
        for i, (ref, buf) in enumerate(
            ((failed_in, small[0]), (scale_own_in, small[1]), (scale_spare_in, small[2]))
        )
    ]
    load_xe = [
        pltpu.make_async_copy(
            x_in.at[:, :, h * half + kept : (h + 1) * half],
            xe.at[:, :, h * (EW // 2) : (h + 1) * (EW // 2)],
            loc.at[10 + h],
        )
        for h in range(2)
    ]
    loads_sp[0].start()
    loads_st[0].start()
    for cp in load_small:
        cp.start()
    load_u.start()
    for cp in load_xe:
        cp.start()
    loads_st[1].start()
    loads_st[2].start()

    nxt_r = lax.rem(me_r + 1, 4)
    prv_r = lax.rem(me_r + 3, 4)
    plane_peers = [(dy, dz) for dy in range(4) for dz in range(4) if (dy, dz) != (0, 0)]
    xc_peers = [(dx, dc) for dx in range(4) for dc in range(2) if (dx, dc) != (0, 0)]

    def plane_dev(dy, dz):
        return {Y: lax.rem(y + dy, 4), Z: lax.rem(z + dz, 4)}

    def xc_dev(dx, dc):
        v = lax.rem(x + dx, 4)
        return {XH: v // 2, XL: lax.rem(v, 2), CO: lax.rem(c + dc, 2)}

    barrier = pltpu.get_barrier_semaphore()
    for p in plane_peers:
        pl.semaphore_signal(barrier, inc=1, device_id=plane_dev(*p), device_id_type=MESH_ID)
    for p in xc_peers:
        pl.semaphore_signal(barrier, inc=1, device_id=xc_dev(*p), device_id_type=MESH_ID)

    nxt_dev = {XL: nxt_r // 2, CO: lax.rem(nxt_r, 2)}

    def spare_copy(i, l):
        if i == 0:
            return remote(spb.at[0, l], spr.at[0, l], sp_s.at[l], sp_r.at[l], nxt_dev)
        return remote(spb.at[i], spr.at[i], sp_s.at[1 + i], sp_r.at[1 + i], nxt_dev)

    scale_copy = remote(scs, scr, sp_s.at[4], sp_r.at[4], nxt_dev)

    def sc_copy(di, d):
        return remote(scr, scn.at[xh], sc_s.at[di], sc_r.at[di], to_x(xn[d]))

    def x_copy(k, l, di, d):
        src = x_in.at[l, :, pl.ds(pl.multiple_of(xn_h[d] * half + OFF[k], 128), WID[k])]
        return remote(src, xbuf[k].at[l, xh], x_s.at[k, l, di], x_r.at[k, l, di], to_x(xn[d]))

    def w_copy(k, l, di, d):
        src = wsb.at[xn_h[d], l, :, OFF[k] : OFF[k] + WID[k]]
        return remote(src, wbuf[k].at[l, y, xh, z], w_s.at[k, l, di], w_r.at[k, l, di], to_x(xn[d]))

    x_far = to_x(ring(x, 2))

    def we_copy(l):
        own = wbuf[NK].at[l, y, xh, z]
        return remote(own, own, we_s.at[l], we_r.at[l], x_far)

    def ge_copy(l):
        return remote(s2[NK].at[l, 1 - xh], grc.at[l], ge_s.at[l], ge_r.at[l], x_far)

    u_far = lax.rem(x + 1 + 2 * (1 - lax.rem(x, 2)), 4)

    def u_copy(part):
        span = slice(part * (tok // 2), (part + 1) * (tok // 2))
        return remote(u_in.at[c, span], ubuf.at[c, xh, span], u_s.at[part], u_r.at[part], to_x(u_far))

    u_fwd = remote(ubuf.at[c, 1 - xh], ubuf.at[c, 1 - xh], u_s.at[2], u_r.at[2], {CO: 1 - c})

    def region(k, l, stage, p, h):
        hs = slice(None) if h is None else h
        if l == 0:
            return wbuf[k].at[0, p, hs, z] if stage == 0 else wbuf[k].at[0, :, hs, p]
        return wbuf[k].at[1, y, hs, p] if stage == 0 else wbuf[k].at[1, p, hs, :]

    def ag_copy(k, l, stage, step, di, d):
        axis = plane_axis[l][stage]
        pos = plane_pos[axis]
        ref = region(k, l, stage, pos, None) if step == 0 else region(k, l, stage, ring(pos, -d), di)
        n = stage * 2 + step
        return remote(ref, ref, ag_s.at[k, l, n, di], ag_r.at[k, l, n, di], {axis: ring(pos, d)})

    def dw_piece(k, l, p, h):
        return dwbuf[k].at[0, :, h, p] if l == 0 else dwbuf[k].at[1, p, h, :]

    def rs_parts(k, l, stage):
        axis = plane_axis[l][1 - stage]
        if stage == 0:
            return axis, (lambda p, h: dw_piece(k, l, p, h)), r1a[k], r1b[k], r1c[k]
        return axis, (lambda p, h: s1[k].at[l, h, p]), r2a[k], r2b[k], r2c[k]

    def rs_copy(k, l, stage, what, di, d):
        axis, piece, ra, rb, rc = rs_parts(k, l, stage)
        pos = plane_pos[axis]
        if what == 0:
            src, dst = piece(ring(pos, 2), di), ra.at[l, di]
        elif what == 1:
            src, dst = piece(ring(pos, d), 1 - di), rb.at[l, di]
        else:
            src, dst = ra.at[l, di], rc.at[l, di]
        n = stage * 3 + what
        return remote(src, dst, rs_s.at[k, l, n, di], rs_r.at[k, l, n, di], {axis: ring(pos, d)})

    def rs_start(k, l, stage):
        for what in (0, 1):
            for di, d in DIRS:
                rs_copy(k, l, stage, what, di, d).start()

    def each(stage, fn):
        if stage == 0:

            @pl.loop(0, 4)
            def _(j):
                fn(j)
        else:
            fn(None)

    def at(ref, j):
        return ref[j] if j is not None else ref[...]

    def rs_forward(k, l, stage):
        axis, piece, ra, rb, rc = rs_parts(k, l, stage)
        pos = plane_pos[axis]
        for di, d in DIRS:
            rs_copy(k, l, stage, 0, di, d).wait_recv()
            own = piece(ring(pos, d), di)
            acc = ra.at[l, di]

            def add(j, own=own, acc=acc):
                total = (at(acc, j).astype(F32) + at(own, j).astype(F32)).astype(BF)
                if j is None:
                    acc[...] = total
                else:
                    acc[j] = total

            each(stage, add)
            rs_copy(k, l, stage, 2, di, d).start()

    def rs_finish(k, l, stage):
        axis, piece, ra, rb, rc = rs_parts(k, l, stage)
        pos = plane_pos[axis]
        for what in (1, 2):
            for di, d in DIRS:
                rs_copy(k, l, stage, what, di, d).wait_recv()
        for h in range(2):
            own = piece(pos, h)
            through = rc.at[l, h]
            direct = rb.at[l, 1 - h]
            out = s1[k].at[l, h] if stage == 0 else s2[k].at[l, h]

            def add(j, own=own, through=through, direct=direct, out=out):
                total = at(own, j).astype(F32) + at(through, j).astype(F32) + at(direct, j).astype(F32)
                if j is None:
                    out[...] = total.astype(BF)
                else:
                    out[j] = total.astype(BF)

            each(stage, add)

    def g_copy(k, l, di, d):
        return remote(
            s2[k].at[l, xn_h[d]], gbuf[k].at[l, xh], g_s.at[k, l, di], g_r.at[k, l, di], to_x(xn[d])
        )

    def ig_copy(k, l, di, d):
        dst = ig_out.at[l, :, pl.ds(pl.multiple_of(xh * half + OFF[k], 128), WID[k])]
        return remote(igb[k].at[l, xn_h[d]], dst, ig_s.at[k, l, di], ig_r.at[k, l, di], to_x(xn[d]))

    kv_core = remote(kvs, kvr, kv_s.at[0], kv_r.at[0], {CO: 1 - c})

    def kv_piece(v, l):
        return kvr.at[lax.rem(v, 2), l, v // 2]

    def kv_copy(what, di, d):
        if what == 0:
            src, dst = kv_piece(ring(x, 2), di), ka.at[di]
        elif what == 1:
            src, dst = kv_piece(ring(x, d), 1 - di), kb.at[di]
        else:
            src, dst = ka.at[di], kc.at[di]
        n = 1 + what * 2 + di
        return remote(src, dst, kv_s.at[n], kv_r.at[n], to_x(xn[d]))

    np_copies = [
        remote(nsend, npl.at[i], np_s.at[i], np_r.at[i], plane_dev(*p)) for i, p in enumerate(plane_peers)
    ]
    nx_copies = [
        remote(nsend2, nxc.at[i], nx_s.at[i], nx_r.at[i], xc_dev(*p)) for i, p in enumerate(xc_peers)
    ]

    def lost(shape):
        return jnp.broadcast_to(failed[...], shape) == me_r

    def begin():
        loads_sp[0].wait()
        for l in range(layers):
            spb[0, l] = spf[l].astype(BF)
        loads_sp[1].start()
        for cp in load_small:
            cp.wait()
        scs[...] = jnp.broadcast_to(scale_spare[...], scs.shape)
        pl.semaphore_wait(barrier, len(plane_peers) + len(xc_peers))
        u_copy(0).start()
        for l in range(layers):
            spare_copy(0, l).start()
        scale_copy.start()
        loads_st[0].wait()

    def recover(l):
        spare_copy(0, l).wait_recv()
        for h in range(2):
            for k in range(NK + 1):
                off, width = (OFF[k], WID[k]) if k < NK else (kept, EW // 2)
                span = slice(h * half + off, h * half + off + width)
                now = jnp.where(lost((rows, width)), spr[0, l, :, span].astype(F32), st[0][l, :, span])
                st[0][l, :, span] = now
                if k < NK:
                    wsb[h, l, :, off : off + width] = now.astype(BF)
                else:
                    wbuf[NK][l, y, xh, z, :, h * width : (h + 1) * width] = now.astype(BF)
        for k in range(NK):
            for di, d in DIRS:
                w_copy(k, l, di, d).start()
        we_copy(l).start()

    def exchange():
        u_copy(1).start()
        n = 0
        for k in range(NK):
            for l in range(layers):
                for di, d in DIRS:
                    x_copy(k, l, di, d).start()
                if n == SPARES_AT:
                    for i in (1, 2):
                        loads_sp[i].wait()
                        for ll in range(layers):
                            spb[i, ll] = spf[ll].astype(BF)
                        if i == 1:
                            loads_sp[2].start()
                        spare_copy(i, 0).start()
                n += 1
        scale_copy.wait_recv()
        scr[...] = jnp.where(lost(scr.shape), scr[...], jnp.broadcast_to(scale_own[...], scr.shape))
        nacc[...] = jnp.zeros(nacc.shape, F32)
        load_u.wait()
        for di, d in DIRS:
            sc_copy(di, d).start()

    def forward_u():
        for part in range(2):
            u_copy(part).wait_recv()
        u_fwd.start()

    def transpose_u():
        u_fwd.wait_recv()
        for l in range(layers):

            @pl.loop(0, 4)
            def _(j):
                span = pl.ds(pl.multiple_of(j * (feats // 4), feats // 4), feats // 4)
                for t in range(2):
                    ut[l, j, :, t * tok : (t + 1) * tok] = ubuf[l, t, :, span].T

    def gather_0(k, l):
        if k == NK:
            we_copy(l).wait_recv()
        else:
            for di, d in DIRS:
                w_copy(k, l, di, d).wait_recv()
        for di, d in DIRS:
            ag_copy(k, l, 0, 0, di, d).start()

    def gather_forward(stage, k, l):
        for di, d in DIRS:
            ag_copy(k, l, stage, 0, di, d).wait_recv()
            ag_copy(k, l, stage, 1, di, d).start()

    def gather_1(k, l):
        for di, d in DIRS:
            ag_copy(k, l, 0, 1, di, d).wait_recv()
        for di, d in DIRS:
            ag_copy(k, l, 1, 0, di, d).start()

    def gathered(k, l):
        for di, d in DIRS:
            ag_copy(k, l, 1, 1, di, d).wait_recv()

    got_x = set()

    def need_x(k, l):
        if (k, l) not in got_x:
            got_x.add((k, l))
            for di, d in DIRS:
                x_copy(k, l, di, d).wait_recv()

    got_xe = set()

    def need_xe():
        if not got_xe:
            got_xe.add(1)
            for cp in load_xe:
                cp.wait()

    def grad_product(k, l):
        if k < NK:
            need_x(k, l)
            width = WID[k]
        else:
            need_xe()
            width = EW

        @pl.loop(0, 4)
        def _(j):
            if k < NK:
                inputs = xbuf[k][l].reshape(2 * tok, width)
                part = jnp.dot(ut[l, j], inputs, preferred_element_type=F32)
            else:
                up = ut[l, j, :, pl.ds(pl.multiple_of(xh * tok, tok), tok)]
                part = jnp.dot(up, xe[l], preferred_element_type=F32)
            dwbuf[k][l, j] = part.astype(BF).reshape(2, 4, rows, width)

        rs_start(k, l, 0)

    def finish_0(k, l):
        rs_finish(k, l, 0)
        rs_start(k, l, 1)

    got_scale = set()

    def add_squares(grad):
        nacc[:, 0 : grad.shape[1]] += grad * grad

    def finish_1(k, l):
        rs_finish(k, l, 1)
        if k == NK:
            ge_copy(l).start()
            return
        for di, d in DIRS:
            g_copy(k, l, di, d).start()
        if not got_scale:
            got_scale.add(1)
            for di, d in DIRS:
                sc_copy(di, d).wait_recv()
        for h in range(2):
            add_squares(s2[k][l, h].astype(F32) / jnp.broadcast_to(scn[h, 0:1, 0:1], (rows, WID[k])))

    def finish_kept(l):
        ge_copy(l).wait_recv()
        grad = s2[NK][l, xh].astype(F32) + grc[l].astype(F32)
        grad = grad / jnp.broadcast_to(scr[0:1, 0:1], (rows, EW))
        ge[l] = grad
        add_squares(grad)

    kv_begun = set()

    def kv_product(k, l):
        fresh = l not in kv_begun
        kv_begun.add(l)
        if k == NK:
            need_xe()
            assert not fresh

            @pl.loop(0, 4)
            def _(j):
                weight = wbuf[k][l, j].reshape(8 * rows, EW)
                part = lax.dot_general(xe[l], weight, (((1,), (1,)), ((), ())), preferred_element_type=F32)
                kvp[j, l, xh] += part

            return
        need_x(k, l)

        @pl.loop(0, 4)
        def _(j):
            inputs = xbuf[k][l].reshape(2 * tok, WID[k])
            weight = wbuf[k][l, j].reshape(8 * rows, WID[k])
            part = lax.dot_general(
                inputs, weight, (((1,), (1,)), ((), ())), preferred_element_type=F32
            ).reshape(2, tok, 8 * rows)
            if fresh:
                kvp[j, l] = part
            else:
                kvp[j, l] += part

    def ig_product(k, l):
        if k == NK:
            weight = wbuf[k][l].reshape(feats, EW)
            grad = jnp.dot(ubuf[l, xh], weight, preferred_element_type=F32).astype(BF)
            for h in range(2):
                ig_out[l, :, h * half + kept : (h + 1) * half] = grad[:, h * (EW // 2) : (h + 1) * (EW // 2)]
            return

        @pl.loop(0, 2)
        def _(t):
            weight = wbuf[k][l].reshape(feats, WID[k])
            igb[k][l, t] = jnp.dot(ubuf[l, t], weight, preferred_element_type=F32).astype(BF)

        for di, d in DIRS:
            ig_copy(k, l, di, d).start()

    def kv_cores():
        for v in range(2):
            kvs[v] = kvp[2 * v + (1 - c)].astype(BF)
        kv_core.start()

    def kv_ring():
        kv_core.wait_recv()
        for v in range(2):
            for l in range(layers):
                kvr[v, l] = (kvr[v, l].astype(F32) + kvp[2 * v + c, l]).astype(BF)
        for what in (0, 1):
            for di, d in DIRS:
                kv_copy(what, di, d).start()

    def kv_forward():
        for di, d in DIRS:
            kv_copy(0, di, d).wait_recv()
            ka[di] = (ka[di].astype(F32) + kv_piece(ring(x, d), di)[...].astype(F32)).astype(BF)
            kv_copy(2, di, d).start()

    def kv_finish():
        for what in (1, 2):
            for di, d in DIRS:
                kv_copy(what, di, d).wait_recv()
        for h in range(2):
            own = kv_piece(x, h)[...].astype(F32)
            kv_out[h] = (own + kc[h].astype(F32) + kb[1 - h].astype(F32)).astype(BF)

    def squares_plane():
        tile = jnp.zeros((8, 128), F32)
        for i in range(rows // 8):
            for j in range(nacc.shape[1] // 128):
                tile = tile + nacc[8 * i : 8 * i + 8, 128 * j : 128 * j + 128]
        nsend[...] = tile
        for cp in np_copies:
            cp.start()

    def squares_rest():
        total = nsend[...]
        for i, cp in enumerate(np_copies):
            cp.wait_recv()
            total = total + npl[i]
        nsend2[...] = total
        for cp in nx_copies:
            cp.start()

    def adam():
        for i in (1, 2):
            loads_st[i].wait()
            spare_copy(i, 0).wait_recv()
        for k in range(NK):
            for l in range(layers):
                for di, d in DIRS:
                    g_copy(k, l, di, d).wait_recv()
        total = nsend2[...]
        for i, cp in enumerate(nx_copies):
            cp.wait_recv()
            total = total + nxc[i]
        squares = jnp.sum(jnp.sum(total, axis=1, keepdims=True), axis=0, keepdims=True)
        factor = jnp.minimum(1.0, lax.rsqrt(squares / entries + MEAN_EPS))

        def update(l, start, grad):
            shape = grad.shape
            span = slice(start, start + shape[1])
            gone = lost(shape)
            clipped = grad * jnp.broadcast_to(factor, shape)
            first_now = jnp.where(gone, spr[1, l, :, span].astype(F32), st[1][l, :, span])
            second_now = jnp.where(gone, spr[2, l, :, span].astype(F32), st[2][l, :, span])
            master_now = st[0][l, :, span]
            new_first = BETA_FIRST * first_now + (1.0 - BETA_FIRST) * clipped
            new_second = BETA_SECOND * second_now + (1.0 - BETA_SECOND) * clipped * clipped
            st[0][l, :, span] = master_now - LEARN_RATE * (
                new_first / (jnp.sqrt(new_second) + ADAM_EPS) + DECAY_RATE * master_now
            )
            st[1][l, :, span] = new_first
            st[2][l, :, span] = new_second

        @pl.loop(0, layers)
        def _(l):
            for h in range(2):
                for k in range(NK):
                    scale = jnp.broadcast_to(scr[0:1, 0:1], (rows, WID[k]))
                    update(l, h * half + OFF[k], gbuf[k][l, h].astype(F32) / scale)
                update(l, h * half + kept, ge[l, :, h * (EW // 2) : (h + 1) * (EW // 2)])

    steps = {
        "INI": begin,
        "WSEL": recover,
        "XREST": exchange,
        "UF": forward_u,
        "TR": transpose_u,
        "A1": gather_0,
        "F0": functools.partial(gather_forward, 0),
        "S1": gather_1,
        "F1": functools.partial(gather_forward, 1),
        "WD": gathered,
        "FE": finish_kept,
        "DW": grad_product,
        "RF0": lambda k, l: rs_forward(k, l, 0),
        "RE0": finish_0,
        "RF1": lambda k, l: rs_forward(k, l, 1),
        "RE1": finish_1,
        "KV": kv_product,
        "IG": ig_product,
        "KVC": kv_cores,
        "KVA": kv_ring,
        "KVF": kv_forward,
        "KVE": kv_finish,
        "SQ": squares_plane,
        "NX": squares_rest,
        "AD": adam,
        "END": lambda: None,
    }
    for name, *where in ORDER:
        steps[name](*where)

    for l in range(layers):
        spare_copy(0, l).wait_send()
    for i in (1, 2):
        spare_copy(i, 0).wait_send()
    scale_copy.wait_send()
    for part in range(2):
        u_copy(part).wait_send()
    for di, d in DIRS:
        sc_copy(di, d).wait_send()
    u_fwd.wait_send()
    kv_core.wait_send()
    for l in range(layers):
        we_copy(l).wait_send()
        ge_copy(l).wait_send()
        for k in range(NK):
            for di, d in DIRS:
                w_copy(k, l, di, d).wait_send()
    for what in range(3):
        for di, d in DIRS:
            kv_copy(what, di, d).wait_send()
    for cp in np_copies + nx_copies:
        cp.wait_send()

    for k in range(NK + 1):
        for l in range(layers):
            for di, d in DIRS:
                for stage in range(2):
                    for step in range(2):
                        ag_copy(k, l, stage, step, di, d).wait_send()
                    for what in range(3):
                        rs_copy(k, l, stage, what, di, d).wait_send()
                if k < NK:
                    x_copy(k, l, di, d).wait_send()
                    ig_copy(k, l, di, d).wait_send()
                    g_copy(k, l, di, d).wait_send()
                    ig_copy(k, l, di, d).wait_recv()


def store(*refs):
    sems = refs[10]
    copies = [pltpu.make_async_copy(refs[i], refs[5 + i], sems.at[i]) for i in range(5)]
    for cp in copies:
        cp.start()
    for cp in copies:
        cp.wait()


def local(
    layer_input,
    kv_cotangent,
    failed_member,
    master,
    first_moment,
    second_moment,
    loss_scale,
    spare_master,
    spare_first,
    spare_second,
    spare_scale,
):
    layers, tok, cols = layer_input.shape
    rows = master.shape[1]
    feats = kv_cotangent.shape[2]
    entries = float(layers * rows * lax.axis_size(FSDP) * cols * lax.axis_size(RED))
    any_ = pl.BlockSpec(memory_space=pl.ANY)
    vmem = pl.BlockSpec(memory_space=pltpu.VMEM)
    sem = pltpu.SemaphoreType.DMA
    every = WID + (EW,)

    def per_chunk(shape, widths):
        return [pltpu.VMEM((*shape, w), BF) for w in widths]

    scratch = [
        per_chunk((layers, 2, tok), WID),
        pltpu.VMEM((layers, tok, EW), BF),
        pltpu.VMEM((layers, 2, tok, feats), BF),
        pltpu.VMEM((layers, 4, feats // 4, 2 * tok), BF),
        pltpu.VMEM((2, layers, rows, cols // 2 - EW // 2), BF),
        per_chunk((layers, 4, 2, 4, rows), every),
        per_chunk((layers, 4, 2, 4, rows), every),
        per_chunk((layers, 2, 4, rows), every),
        per_chunk((layers, 2, 4, rows), every),
        per_chunk((layers, 2, 4, rows), every),
        per_chunk((layers, 2, 4, rows), every),
        per_chunk((layers, 2, rows), every),
        per_chunk((layers, 2, rows), every),
        per_chunk((layers, 2, rows), every),
        per_chunk((layers, 2, rows), every),
        per_chunk((layers, 2, rows), WID),
        pltpu.VMEM((layers, rows, EW), BF),
        pltpu.VMEM((layers, rows, EW), F32),
        per_chunk((layers, 2, tok), WID),
        pltpu.VMEM((4, layers, 2, tok, feats // 4), F32),
        pltpu.VMEM((2, layers, 2, tok, feats // 4), BF),
        pltpu.VMEM((2, layers, 2, tok, feats // 4), BF),
        pltpu.VMEM((2, tok, feats // 4), BF),
        pltpu.VMEM((2, tok, feats // 4), BF),
        pltpu.VMEM((2, tok, feats // 4), BF),
        pltpu.VMEM((layers, rows, cols), F32),
        pltpu.VMEM((3, layers, rows, cols), BF),
        pltpu.VMEM((3, layers, rows, cols), BF),
        [pltpu.VMEM((1, 1), jnp.int32), pltpu.VMEM((1, 1), F32), pltpu.VMEM((1, 1), F32)],
        pltpu.VMEM((8, 128), F32),
        pltpu.VMEM((8, 128), F32),
        pltpu.VMEM((2, 8, 128), F32),
        pltpu.VMEM((rows, max(every)), F32),
        pltpu.VMEM((8, 128), F32),
        pltpu.VMEM((15, 8, 128), F32),
        pltpu.VMEM((8, 128), F32),
        pltpu.VMEM((7, 8, 128), F32),
        sem((12,)),
        sem((5,)),
        sem((5,)),
        sem((3,)),
        sem((3,)),
        sem((NK, layers, 2)),
        sem((NK, layers, 2)),
        sem((NK, layers, 2)),
        sem((NK, layers, 2)),
        sem((layers,)),
        sem((layers,)),
        sem((layers,)),
        sem((layers,)),
        sem((NK + 1, layers, 4, 2)),
        sem((NK + 1, layers, 4, 2)),
        sem((NK + 1, layers, 6, 2)),
        sem((NK + 1, layers, 6, 2)),
        sem((NK, layers, 2)),
        sem((NK, layers, 2)),
        sem((NK, layers, 2)),
        sem((NK, layers, 2)),
        sem((7,)),
        sem((7,)),
        sem((15,)),
        sem((15,)),
        sem((7,)),
        sem((7,)),
        sem((2,)),
        sem((2,)),
    ]
    results = (
        jax.ShapeDtypeStruct((layers, tok, feats // 4), BF),
        jax.ShapeDtypeStruct((layers, tok, cols), BF),
    ) + (jax.ShapeDtypeStruct(master.shape, F32),) * 3
    held = pl.pallas_call(
        functools.partial(kernel, entries),
        out_shape=tuple(pltpu.VMEM(r.shape, r.dtype) for r in results),
        in_specs=[any_] * 11,
        out_specs=(vmem,) * 5,
        scratch_shapes=scratch,
        compiler_params=pltpu.CompilerParams(
            collective_id=0, has_side_effects=True, vmem_limit_bytes=56 << 20
        ),
        name="restore_step",
    )(
        layer_input,
        kv_cotangent,
        failed_member.reshape(1, 1),
        loss_scale,
        spare_scale,
        master,
        first_moment,
        second_moment,
        spare_master,
        spare_first,
        spare_second,
    )
    return pl.pallas_call(
        store,
        out_shape=results,
        in_specs=[vmem] * 5,
        out_specs=(any_,) * 5,
        scratch_shapes=[sem((5,))],
        compiler_params=pltpu.CompilerParams(vmem_limit_bytes=1 << 20),
        name="store_results",
    )(*[pltpu.with_memory_space_constraint(h, pltpu.VMEM) for h in held])


def solution(mesh):
    split = Mesh(mesh.devices.reshape(4, 2, 4, 2, 2), (Y, XH, Z, XL, CO))
    placed = (
        P(None, FSDP, RED),
        P(None, FSDP, None),
        P(FSDP),
        P(None, FSDP, RED),
        P(None, FSDP, RED),
        P(None, FSDP, RED),
        P(FSDP, RED),
        P(None, FSDP, RED),
        P(None, FSDP, RED),
        P(None, FSDP, RED),
        P(FSDP, RED),
    )
    return jax.shard_map(
        local,
        mesh=split,
        in_specs=placed,
        out_specs=(P(None, FSDP, RED),) * 5,
        check_vma=False,
    )
```

```python
import functools

import jax
import jax.numpy as jnp
from jax import lax
from jax.experimental import pallas as pl
from jax.experimental.pallas import tpu as pltpu
from jax.sharding import Mesh
from jax.sharding import PartitionSpec as P

Y, XH, Z, XL, CO = "fsdp_0", "fsdp_1", "fsdp_2", "red_0", "red_1"
RED = (XL, CO)
FSDP = (Y, XH, Z)
MESH_ID = pl.DeviceIdType.MESH

BETA_FIRST = 0.9
BETA_SECOND = 0.95
LEARN_RATE = 0.01
DECAY_RATE = 0.1
ADAM_EPS = 1e-08
MEAN_EPS = 1e-06

NK = 4
WID = (512, 512, 384, 256)
OFF = tuple(sum(WID[:k]) for k in range(NK))
EW = 768
SPARES_AT = 1
ORDER = (
    ("INI",),
    ("TR0",),
    ("DW", 4, 1),
    ("DW", 4, 0),
    ("WSEL", 0),
    ("WSEL", 1),
    ("XREST",),
    ("RF0", 4, 1),
    ("A1", 0, 0),
    ("A1", 2, 0),
    ("A1", 1, 0),
    ("A1", 3, 0),
    ("RF0", 4, 0),
    ("A1", 4, 0),
    ("A1", 1, 1),
    ("A1", 3, 1),
    ("A1", 0, 1),
    ("A1", 2, 1),
    ("RE0", 4, 1),
    ("F0", 0, 0),
    ("RE0", 4, 0),
    ("A1", 4, 1),
    ("F0", 2, 0),
    ("F0", 1, 1),
    ("F0", 1, 0),
    ("F0", 3, 1),
    ("F0", 3, 0),
    ("F0", 0, 1),
    ("UF",),
    ("F0", 2, 1),
    ("F0", 4, 0),
    ("S1", 0, 0),
    ("RF1", 4, 1),
    ("TR",),
    ("RF1", 4, 0),
    ("S1", 2, 0),
    ("F0", 4, 1),
    ("S1", 1, 0),
    ("S1", 3, 0),
    ("S1", 1, 1),
    ("S1", 3, 1),
    ("S1", 4, 0),
    ("S1", 0, 1),
    ("S1", 2, 1),
    ("RE1", 4, 0),
    ("F1", 0, 0),
    ("DW", 0, 0),
    ("F1", 1, 1),
    ("RE1", 4, 1),
    ("F1", 3, 1),
    ("F1", 2, 0),
    ("S1", 4, 1),
    ("F1", 0, 1),
    ("DW", 0, 1),
    ("F1", 1, 0),
    ("DW", 1, 0),
    ("F1", 2, 1),
    ("F1", 3, 0),
    ("WD", 1, 1),
    ("IG", 1, 1),
    ("DW", 1, 1),
    ("WD", 3, 1),
    ("KV", 1, 1),
    ("DW", 2, 0),
    ("F1", 4, 0),
    ("DW", 2, 1),
    ("WD", 0, 0),
    ("F1", 4, 1),
    ("IG", 0, 0),
    ("KV", 0, 0),
    ("DW", 3, 0),
    ("WD", 0, 1),
    ("RF0", 0, 0),
    ("IG", 0, 1),
    ("KV", 0, 1),
    ("RF0", 0, 1),
    ("DW", 3, 1),
    ("KV", 3, 1),
    ("FE", 0),
    ("WD", 2, 0),
    ("IG", 2, 0),
    ("KV", 2, 0),
    ("FE", 1),
    ("WD", 2, 1),
    ("IG", 2, 1),
    ("WD", 1, 0),
    ("IG", 1, 0),
    ("KV", 2, 1),
    ("KV", 1, 0),
    ("RF0", 1, 1),
    ("RF0", 1, 0),
    ("WD", 3, 0),
    ("KV", 3, 0),
    ("RF0", 2, 1),
    ("RF0", 2, 0),
    ("WD", 4, 1),
    ("IG", 4, 1),
    ("KV", 4, 1),
    ("RE0", 0, 1),
    ("WD", 4, 0),
    ("RF0", 3, 0),
    ("IG", 4, 0),
    ("RF0", 3, 1),
    ("KV", 4, 0),
    ("RE0", 0, 0),
    ("KVC",),
    ("RE0", 1, 1),
    ("RE0", 1, 0),
    ("RE0", 2, 1),
    ("RE0", 3, 1),
    ("RE0", 2, 0),
    ("KVA",),
    ("RF1", 0, 0),
    ("RF1", 1, 0),
    ("RF1", 0, 1),
    ("RE0", 3, 0),
    ("RF1", 2, 0),
    ("RF1", 1, 1),
    ("RE1", 0, 0),
    ("RF1", 2, 1),
    ("RE1", 1, 0),
    ("RF1", 3, 0),
    ("RF1", 3, 1),
    ("KVF",),
    ("RE1", 2, 0),
    ("RE1", 0, 1),
    ("RE1", 1, 1),
    ("RE1", 3, 0),
    ("RE1", 2, 1),
    ("RE1", 3, 1),
    ("SQ",),
    ("KVE",),
    ("NX",),
    ("IG", 3, 1),
    ("IG", 3, 0),
    ("AD",),
    ("END",),
)
BF = jnp.bfloat16
F32 = jnp.float32


def kernel(
    entries,
    x_in,
    u_in,
    failed_in,
    scale_own_in,
    scale_spare_in,
    master,
    first,
    second,
    sp_master,
    sp_first,
    sp_second,
    kv_out,
    ig_out,
    nm_out,
    nf_out,
    ns_out,
    xbuf,
    xe,
    ubuf,
    ut,
    wsb,
    wbuf,
    dwbuf,
    r1a,
    r1b,
    r1c,
    s1,
    r2a,
    r2b,
    r2c,
    s2,
    gbuf,
    grc,
    ge,
    igb,
    kvp,
    kvr,
    ka,
    kb,
    kc,
    spf,
    spb,
    spr,
    small,
    scs,
    scr,
    scn,
    nacc,
    nsend,
    npl,
    nsend2,
    nxc,
    loc,
    sp_s,
    sp_r,
    u_s,
    u_r,
    x_s,
    x_r,
    w_s,
    w_r,
    we_s,
    we_r,
    ge_s,
    ge_r,
    ag_s,
    ag_r,
    rs_s,
    rs_r,
    g_s,
    g_r,
    ig_s,
    ig_r,
    kv_s,
    kv_r,
    np_s,
    np_r,
    nx_s,
    nx_r,
    sc_s,
    sc_r,
):
    layers, tok, cols = x_in.shape
    half = cols // 2
    rows = master.shape[1]
    feats = u_in.shape[2]
    kept = half - EW // 2
    failed, scale_own, scale_spare = small[0], small[1], small[2]
    y, xh, z, xl, c = (lax.axis_index(a) for a in (Y, XH, Z, XL, CO))
    x = 2 * xh + xl
    me_r = 2 * xl + c

    def ring(v, d):
        return lax.rem(v + (d + 4), 4)

    def to_x(v, core=None):
        dev = {XH: v // 2, XL: lax.rem(v, 2)}
        if core is not None:
            dev[CO] = core
        return dev

    xn = {d: ring(x, d) for d in (1, -1)}
    xn_h = {d: xn[d] // 2 for d in (1, -1)}
    plane_axis = {0: (Y, Z), 1: (Z, Y)}
    plane_pos = {Y: y, Z: z}
    DIRS = ((0, 1), (1, -1))

    def remote(src, dst, ss, rs, dev):
        return pltpu.make_async_remote_copy(
            src_ref=src, dst_ref=dst, send_sem=ss, recv_sem=rs, device_id=dev, device_id_type=MESH_ID
        )

    states = (master, first, second)
    st = (nm_out, nf_out, ns_out)
    spares = (sp_master, sp_first, sp_second)
    loads_sp = [pltpu.make_async_copy(spares[i], spf, loc.at[i]) for i in range(3)]
    loads_st = [pltpu.make_async_copy(states[i], st[i], loc.at[3 + i]) for i in range(3)]
    load_u = pltpu.make_async_copy(u_in, ubuf.at[:, xh], loc.at[6])
    load_small = [
        pltpu.make_async_copy(ref, buf, loc.at[7 + i])
        for i, (ref, buf) in enumerate(
            ((failed_in, small[0]), (scale_own_in, small[1]), (scale_spare_in, small[2]))
        )
    ]
    load_xe = [
        pltpu.make_async_copy(
            x_in.at[:, :, h * half + kept : (h + 1) * half],
            xe.at[:, :, h * (EW // 2) : (h + 1) * (EW // 2)],
            loc.at[10 + h],
        )
        for h in range(2)
    ]
    loads_sp[0].start()
    loads_st[0].start()
    for cp in load_small:
        cp.start()
    load_u.start()
    for cp in load_xe:
        cp.start()
    loads_st[1].start()
    loads_st[2].start()

    nxt_r = lax.rem(me_r + 1, 4)
    prv_r = lax.rem(me_r + 3, 4)
    plane_peers = [(dy, dz) for dy in range(4) for dz in range(4) if (dy, dz) != (0, 0)]
    xc_peers = [(dx, dc) for dx in range(4) for dc in range(2) if (dx, dc) != (0, 0)]

    def plane_dev(dy, dz):
        return {Y: lax.rem(y + dy, 4), Z: lax.rem(z + dz, 4)}

    def xc_dev(dx, dc):
        v = lax.rem(x + dx, 4)
        return {XH: v // 2, XL: lax.rem(v, 2), CO: lax.rem(c + dc, 2)}

    barrier = pltpu.get_barrier_semaphore()
    for p in plane_peers:
        pl.semaphore_signal(barrier, inc=1, device_id=plane_dev(*p), device_id_type=MESH_ID)
    for p in xc_peers:
        pl.semaphore_signal(barrier, inc=1, device_id=xc_dev(*p), device_id_type=MESH_ID)

    nxt_dev = {XL: nxt_r // 2, CO: lax.rem(nxt_r, 2)}

    def spare_copy(i, l):
        if i == 0:
            return remote(spb.at[0, l], spr.at[0, l], sp_s.at[l], sp_r.at[l], nxt_dev)
        return remote(spb.at[i], spr.at[i], sp_s.at[1 + i], sp_r.at[1 + i], nxt_dev)

    scale_copy = remote(scs, scr, sp_s.at[4], sp_r.at[4], nxt_dev)

    def sc_copy(di, d):
        return remote(scr, scn.at[xh], sc_s.at[di], sc_r.at[di], to_x(xn[d]))

    def x_copy(k, l, di, d):
        src = x_in.at[l, :, pl.ds(pl.multiple_of(xn_h[d] * half + OFF[k], 128), WID[k])]
        return remote(src, xbuf[k].at[l, xh], x_s.at[k, l, di], x_r.at[k, l, di], to_x(xn[d]))

    def w_copy(k, l, di, d):
        src = wsb.at[xn_h[d], l, :, OFF[k] : OFF[k] + WID[k]]
        return remote(src, wbuf[k].at[l, y, xh, z], w_s.at[k, l, di], w_r.at[k, l, di], to_x(xn[d]))

    x_far = to_x(ring(x, 2))

    def we_copy(l):
        own = wbuf[NK].at[l, y, xh, z]
        return remote(own, own, we_s.at[l], we_r.at[l], x_far)

    def ge_copy(l):
        return remote(s2[NK].at[l, 1 - xh], grc.at[l], ge_s.at[l], ge_r.at[l], x_far)

    u_far = lax.rem(x + 1 + 2 * (1 - lax.rem(x, 2)), 4)

    def u_copy(part):
        span = slice(0, tok // 4) if part == 0 else slice(tok // 4, tok)
        return remote(u_in.at[c, span], ubuf.at[c, xh, span], u_s.at[part], u_r.at[part], to_x(u_far))

    u_fwd = remote(ubuf.at[c, 1 - xh], ubuf.at[c, 1 - xh], u_s.at[2], u_r.at[2], {CO: 1 - c})

    def region(k, l, stage, p, h):
        hs = slice(None) if h is None else h
        if l == 0:
            return wbuf[k].at[0, p, hs, z] if stage == 0 else wbuf[k].at[0, :, hs, p]
        return wbuf[k].at[1, y, hs, p] if stage == 0 else wbuf[k].at[1, p, hs, :]

    def ag_copy(k, l, stage, step, di, d):
        axis = plane_axis[l][stage]
        pos = plane_pos[axis]
        ref = region(k, l, stage, pos, None) if step == 0 else region(k, l, stage, ring(pos, -d), di)
        n = stage * 2 + step
        return remote(ref, ref, ag_s.at[k, l, n, di], ag_r.at[k, l, n, di], {axis: ring(pos, d)})

    def dw_piece(k, l, p, h):
        return dwbuf[k].at[0, :, h, p] if l == 0 else dwbuf[k].at[1, p, h, :]

    def rs_parts(k, l, stage):
        axis = plane_axis[l][1 - stage]
        if stage == 0:
            return axis, (lambda p, h: dw_piece(k, l, p, h)), r1a[k], r1b[k], r1c[k]
        return axis, (lambda p, h: s1[k].at[l, h, p]), r2a[k], r2b[k], r2c[k]

    def rs_copy(k, l, stage, what, di, d):
        axis, piece, ra, rb, rc = rs_parts(k, l, stage)
        pos = plane_pos[axis]
        if what == 0:
            src, dst = piece(ring(pos, 2), di), ra.at[l, di]
        elif what == 1:
            src, dst = piece(ring(pos, d), 1 - di), rb.at[l, di]
        else:
            src, dst = ra.at[l, di], rc.at[l, di]
        n = stage * 3 + what
        return remote(src, dst, rs_s.at[k, l, n, di], rs_r.at[k, l, n, di], {axis: ring(pos, d)})

    def rs_start(k, l, stage):
        for what in (0, 1):
            for di, d in DIRS:
                rs_copy(k, l, stage, what, di, d).start()

    def each(stage, fn):
        if stage == 0:

            @pl.loop(0, 4)
            def _(j):
                fn(j)
        else:
            fn(None)

    def at(ref, j):
        return ref[j] if j is not None else ref[...]

    def rs_forward(k, l, stage):
        axis, piece, ra, rb, rc = rs_parts(k, l, stage)
        pos = plane_pos[axis]
        for di, d in DIRS:
            rs_copy(k, l, stage, 0, di, d).wait_recv()
            own = piece(ring(pos, d), di)
            acc = ra.at[l, di]

            def add(j, own=own, acc=acc):
                total = (at(acc, j).astype(F32) + at(own, j).astype(F32)).astype(BF)
                if j is None:
                    acc[...] = total
                else:
                    acc[j] = total

            each(stage, add)
            rs_copy(k, l, stage, 2, di, d).start()

    def rs_finish(k, l, stage):
        axis, piece, ra, rb, rc = rs_parts(k, l, stage)
        pos = plane_pos[axis]
        for what in (1, 2):
            for di, d in DIRS:
                rs_copy(k, l, stage, what, di, d).wait_recv()
        for h in range(2):
            own = piece(pos, h)
            through = rc.at[l, h]
            direct = rb.at[l, 1 - h]
            out = s1[k].at[l, h] if stage == 0 else s2[k].at[l, h]

            def add(j, own=own, through=through, direct=direct, out=out):
                total = at(own, j).astype(F32) + at(through, j).astype(F32) + at(direct, j).astype(F32)
                if j is None:
                    out[...] = total.astype(BF)
                else:
                    out[j] = total.astype(BF)

            each(stage, add)

    def g_copy(k, l, di, d):
        return remote(
            s2[k].at[l, xn_h[d]], gbuf[k].at[l, xh], g_s.at[k, l, di], g_r.at[k, l, di], to_x(xn[d])
        )

    def ig_copy(k, l, di, d):
        dst = ig_out.at[l, :, pl.ds(pl.multiple_of(xh * half + OFF[k], 128), WID[k])]
        return remote(igb[k].at[l, xn_h[d]], dst, ig_s.at[k, l, di], ig_r.at[k, l, di], to_x(xn[d]))

    quarter = feats // 4
    kv_core = remote(xbuf[0], kvr, kv_s.at[0], kv_r.at[0], {CO: 1 - c})

    def kv_piece(v, l):
        span = pl.ds(pl.multiple_of(lax.rem(v, 2) * quarter, quarter), quarter)
        return kvr.at[l, v // 2, :, span]

    def kv_copy(what, di, d):
        if what == 0:
            src, dst = kv_piece(ring(x, 2), di), ka.at[di]
        elif what == 1:
            src, dst = kv_piece(ring(x, d), 1 - di), kb.at[di]
        else:
            src, dst = ka.at[di], kc.at[di]
        n = 1 + what * 2 + di
        return remote(src, dst, kv_s.at[n], kv_r.at[n], to_x(xn[d]))

    np_copies = [
        remote(nsend, npl.at[i], np_s.at[i], np_r.at[i], plane_dev(*p)) for i, p in enumerate(plane_peers)
    ]
    nx_copies = [
        remote(nsend2, nxc.at[i], nx_s.at[i], nx_r.at[i], xc_dev(*p)) for i, p in enumerate(xc_peers)
    ]

    def lost(shape):
        return jnp.broadcast_to(failed[...], shape) == me_r

    def begin():
        loads_sp[0].wait()
        for l in range(layers):
            spb[0, l] = spf[l].astype(BF)
        loads_sp[1].start()
        for cp in load_small:
            cp.wait()
        scs[...] = jnp.broadcast_to(scale_spare[...], scs.shape)
        pl.semaphore_wait(barrier, len(plane_peers) + len(xc_peers))
        u_copy(0).start()
        for l in range(layers):
            spare_copy(0, l).start()
        scale_copy.start()
        loads_st[0].wait()

    def recover(l):
        spare_copy(0, l).wait_recv()
        for h in range(2):
            for k in range(NK + 1):
                off, width = (OFF[k], WID[k]) if k < NK else (kept, EW // 2)
                span = slice(h * half + off, h * half + off + width)
                now = jnp.where(lost((rows, width)), spr[0, l, :, span].astype(F32), st[0][l, :, span])
                st[0][l, :, span] = now
                if k < NK:
                    wsb[h, l, :, off : off + width] = now.astype(BF)
                else:
                    wbuf[NK][l, y, xh, z, :, h * width : (h + 1) * width] = now.astype(BF)
        for k in range(NK):
            for di, d in DIRS:
                w_copy(k, l, di, d).start()
        we_copy(l).start()

    def exchange():
        u_copy(1).start()
        n = 0
        for k in range(NK):
            for l in range(layers):
                for di, d in DIRS:
                    x_copy(k, l, di, d).start()
                if n == SPARES_AT:
                    for i in (1, 2):
                        loads_sp[i].wait()
                        for ll in range(layers):
                            spb[i, ll] = spf[ll].astype(BF)
                        if i == 1:
                            loads_sp[2].start()
                        spare_copy(i, 0).start()
                n += 1
        scale_copy.wait_recv()
        scr[...] = jnp.where(lost(scr.shape), scr[...], jnp.broadcast_to(scale_own[...], scr.shape))
        nacc[...] = jnp.zeros(nacc.shape, F32)
        for di, d in DIRS:
            sc_copy(di, d).start()

    def forward_u():
        for part in range(2):
            u_copy(part).wait_recv()
        u_fwd.start()

    def transpose_u(of):
        for l in range(layers):

            @pl.loop(0, 4)
            def _(j):
                span = pl.ds(pl.multiple_of(j * (feats // 4), feats // 4), feats // 4)
                ut[l, j, of] = ubuf[l, of, :, span].T

    def transpose_own():
        load_u.wait()
        transpose_u(xh)

    def transpose_far():
        u_fwd.wait_recv()
        transpose_u(1 - xh)

    def gather_0(k, l):
        if k == NK:
            we_copy(l).wait_recv()
        else:
            for di, d in DIRS:
                w_copy(k, l, di, d).wait_recv()
        for di, d in DIRS:
            ag_copy(k, l, 0, 0, di, d).start()

    def gather_forward(stage, k, l):
        for di, d in DIRS:
            ag_copy(k, l, stage, 0, di, d).wait_recv()
            ag_copy(k, l, stage, 1, di, d).start()

    def gather_1(k, l):
        for di, d in DIRS:
            ag_copy(k, l, 0, 1, di, d).wait_recv()
        for di, d in DIRS:
            ag_copy(k, l, 1, 0, di, d).start()

    def gathered(k, l):
        for di, d in DIRS:
            ag_copy(k, l, 1, 1, di, d).wait_recv()

    got_x = set()

    def need_x(k, l):
        if (k, l) not in got_x:
            got_x.add((k, l))
            for di, d in DIRS:
                x_copy(k, l, di, d).wait_recv()

    got_xe = set()

    def need_xe():
        if not got_xe:
            got_xe.add(1)
            for cp in load_xe:
                cp.wait()

    def grad_product(k, l):
        if k < NK:
            need_x(k, l)
            width = WID[k]
        else:
            need_xe()
            width = EW

        @pl.loop(0, 4)
        def _(j):
            if k < NK:
                inputs = xbuf[k][l].reshape(2 * tok, width)
                up = jnp.concatenate([ut[l, j, 0], ut[l, j, 1]], axis=1)
                part = jnp.dot(up, inputs, preferred_element_type=F32)
            else:
                part = jnp.dot(ut[l, j, xh], xe[l], preferred_element_type=F32)
            dwbuf[k][l, j] = part.astype(BF).reshape(2, 4, rows, width)

        rs_start(k, l, 0)

    def finish_0(k, l):
        rs_finish(k, l, 0)
        rs_start(k, l, 1)

    got_scale = set()

    def add_squares(grad):
        nacc[:, 0 : grad.shape[1]] += grad * grad

    def finish_1(k, l):
        rs_finish(k, l, 1)
        if k == NK:
            ge_copy(l).start()
            return
        for di, d in DIRS:
            g_copy(k, l, di, d).start()
        if not got_scale:
            got_scale.add(1)
            for di, d in DIRS:
                sc_copy(di, d).wait_recv()
        for h in range(2):
            add_squares(s2[k][l, h].astype(F32) / jnp.broadcast_to(scn[h, 0:1, 0:1], (rows, WID[k])))

    def finish_kept(l):
        ge_copy(l).wait_recv()
        grad = s2[NK][l, xh].astype(F32) + grc[l].astype(F32)
        grad = grad / jnp.broadcast_to(scr[0:1, 0:1], (rows, EW))
        ge[l] = grad
        add_squares(grad)

    kv_begun = set()

    def kv_product(k, l):
        fresh = l not in kv_begun
        kv_begun.add(l)
        if k == NK:
            need_xe()
            assert not fresh

            @pl.loop(0, 4)
            def _(j):
                weight = wbuf[k][l, j].reshape(8 * rows, EW)
                part = lax.dot_general(xe[l], weight, (((1,), (1,)), ((), ())), preferred_element_type=F32)
                kvp[j, l, xh] += part

            return
        need_x(k, l)

        @pl.loop(0, 4)
        def _(j):
            inputs = xbuf[k][l].reshape(2 * tok, WID[k])
            weight = wbuf[k][l, j].reshape(8 * rows, WID[k])
            part = lax.dot_general(
                inputs, weight, (((1,), (1,)), ((), ())), preferred_element_type=F32
            ).reshape(2, tok, 8 * rows)
            if fresh:
                kvp[j, l] = part
            else:
                kvp[j, l] += part

    def ig_product(k, l):
        if k == NK:
            weight = wbuf[k][l].reshape(feats, EW)
            grad = jnp.dot(ubuf[l, xh], weight, preferred_element_type=F32).astype(BF)
            for h in range(2):
                ig_out[l, :, h * half + kept : (h + 1) * half] = grad[:, h * (EW // 2) : (h + 1) * (EW // 2)]
            return

        @pl.loop(0, 2)
        def _(t):
            weight = wbuf[k][l].reshape(feats, WID[k])
            igb[k][l, t] = jnp.dot(ubuf[l, t], weight, preferred_element_type=F32).astype(BF)

        for di, d in DIRS:
            ig_copy(k, l, di, d).start()

    def kv_cores():
        for v in range(2):
            xbuf[0][:, :, :, v * quarter : (v + 1) * quarter] = kvp[2 * v + (1 - c)].astype(BF)
        kv_core.start()

    def kv_ring():
        kv_core.wait_recv()
        for v in range(2):
            for l in range(layers):
                span = slice(v * quarter, (v + 1) * quarter)
                kvr[l, :, :, span] = (kvr[l, :, :, span].astype(F32) + kvp[2 * v + c, l]).astype(BF)
        for what in (0, 1):
            for di, d in DIRS:
                kv_copy(what, di, d).start()

    def kv_forward():
        for di, d in DIRS:
            kv_copy(0, di, d).wait_recv()
            ka[di] = (ka[di].astype(F32) + kv_piece(ring(x, d), di)[...].astype(F32)).astype(BF)
            kv_copy(2, di, d).start()

    def kv_finish():
        for what in (1, 2):
            for di, d in DIRS:
                kv_copy(what, di, d).wait_recv()
        for h in range(2):
            own = kv_piece(x, h)[...].astype(F32)
            kv_out[h] = (own + kc[h].astype(F32) + kb[1 - h].astype(F32)).astype(BF)

    def squares_plane():
        tile = jnp.zeros((8, 128), F32)
        for i in range(rows // 8):
            for j in range(nacc.shape[1] // 128):
                tile = tile + nacc[8 * i : 8 * i + 8, 128 * j : 128 * j + 128]
        nsend[...] = tile
        for cp in np_copies:
            cp.start()

    def squares_rest():
        total = nsend[...]
        for i, cp in enumerate(np_copies):
            cp.wait_recv()
            total = total + npl[i]
        nsend2[...] = total
        for cp in nx_copies:
            cp.start()

    def adam():
        for i in (1, 2):
            loads_st[i].wait()
            spare_copy(i, 0).wait_recv()
        for k in range(NK):
            for l in range(layers):
                for di, d in DIRS:
                    g_copy(k, l, di, d).wait_recv()
        total = nsend2[...]
        for i, cp in enumerate(nx_copies):
            cp.wait_recv()
            total = total + nxc[i]
        squares = jnp.sum(jnp.sum(total, axis=1, keepdims=True), axis=0, keepdims=True)
        factor = jnp.minimum(1.0, lax.rsqrt(squares / entries + MEAN_EPS))

        def update(l, start, grad):
            shape = grad.shape
            span = slice(start, start + shape[1])
            gone = lost(shape)
            clipped = grad * jnp.broadcast_to(factor, shape)
            first_now = jnp.where(gone, spr[1, l, :, span].astype(F32), st[1][l, :, span])
            second_now = jnp.where(gone, spr[2, l, :, span].astype(F32), st[2][l, :, span])
            master_now = st[0][l, :, span]
            new_first = BETA_FIRST * first_now + (1.0 - BETA_FIRST) * clipped
            new_second = BETA_SECOND * second_now + (1.0 - BETA_SECOND) * clipped * clipped
            st[0][l, :, span] = master_now - LEARN_RATE * (
                new_first / (jnp.sqrt(new_second) + ADAM_EPS) + DECAY_RATE * master_now
            )
            st[1][l, :, span] = new_first
            st[2][l, :, span] = new_second

        @pl.loop(0, layers)
        def _(l):
            for h in range(2):
                for k in range(NK):
                    scale = jnp.broadcast_to(scr[0:1, 0:1], (rows, WID[k]))
                    update(l, h * half + OFF[k], gbuf[k][l, h].astype(F32) / scale)
                update(l, h * half + kept, ge[l, :, h * (EW // 2) : (h + 1) * (EW // 2)])

    steps = {
        "INI": begin,
        "WSEL": recover,
        "XREST": exchange,
        "UF": forward_u,
        "TR0": transpose_own,
        "TR": transpose_far,
        "A1": gather_0,
        "F0": functools.partial(gather_forward, 0),
        "S1": gather_1,
        "F1": functools.partial(gather_forward, 1),
        "WD": gathered,
        "FE": finish_kept,
        "DW": grad_product,
        "RF0": lambda k, l: rs_forward(k, l, 0),
        "RE0": finish_0,
        "RF1": lambda k, l: rs_forward(k, l, 1),
        "RE1": finish_1,
        "KV": kv_product,
        "IG": ig_product,
        "KVC": kv_cores,
        "KVA": kv_ring,
        "KVF": kv_forward,
        "KVE": kv_finish,
        "SQ": squares_plane,
        "NX": squares_rest,
        "AD": adam,
        "END": lambda: None,
    }
    for name, *where in ORDER:
        steps[name](*where)

    for l in range(layers):
        spare_copy(0, l).wait_send()
    for i in (1, 2):
        spare_copy(i, 0).wait_send()
    scale_copy.wait_send()
    for part in range(2):
        u_copy(part).wait_send()
    for di, d in DIRS:
        sc_copy(di, d).wait_send()
    u_fwd.wait_send()
    kv_core.wait_send()
    for l in range(layers):
        we_copy(l).wait_send()
        ge_copy(l).wait_send()
        for k in range(NK):
            for di, d in DIRS:
                w_copy(k, l, di, d).wait_send()
    for what in range(3):
        for di, d in DIRS:
            kv_copy(what, di, d).wait_send()
    for cp in np_copies + nx_copies:
        cp.wait_send()

    for k in range(NK + 1):
        for l in range(layers):
            for di, d in DIRS:
                for stage in range(2):
                    for step in range(2):
                        ag_copy(k, l, stage, step, di, d).wait_send()
                    for what in range(3):
                        rs_copy(k, l, stage, what, di, d).wait_send()
                if k < NK:
                    x_copy(k, l, di, d).wait_send()
                    ig_copy(k, l, di, d).wait_send()
                    g_copy(k, l, di, d).wait_send()
                    ig_copy(k, l, di, d).wait_recv()


def store(*refs):
    sems = refs[10]
    copies = [pltpu.make_async_copy(refs[i], refs[5 + i], sems.at[i]) for i in range(5)]
    for cp in copies:
        cp.start()
    for cp in copies:
        cp.wait()


def local(
    layer_input,
    kv_cotangent,
    failed_member,
    master,
    first_moment,
    second_moment,
    loss_scale,
    spare_master,
    spare_first,
    spare_second,
    spare_scale,
):
    layers, tok, cols = layer_input.shape
    rows = master.shape[1]
    feats = kv_cotangent.shape[2]
    entries = float(layers * rows * lax.axis_size(FSDP) * cols * lax.axis_size(RED))
    any_ = pl.BlockSpec(memory_space=pl.ANY)
    vmem = pl.BlockSpec(memory_space=pltpu.VMEM)
    sem = pltpu.SemaphoreType.DMA
    every = WID + (EW,)

    def per_chunk(shape, widths):
        return [pltpu.VMEM((*shape, w), BF) for w in widths]

    scratch = [
        per_chunk((layers, 2, tok), WID),
        pltpu.VMEM((layers, tok, EW), BF),
        pltpu.VMEM((layers, 2, tok, feats), BF),
        pltpu.VMEM((layers, 4, 2, feats // 4, tok), BF),
        pltpu.VMEM((2, layers, rows, cols // 2 - EW // 2), BF),
        per_chunk((layers, 4, 2, 4, rows), every),
        per_chunk((layers, 4, 2, 4, rows), every),
        per_chunk((layers, 2, 4, rows), every),
        per_chunk((layers, 2, 4, rows), every),
        per_chunk((layers, 2, 4, rows), every),
        per_chunk((layers, 2, 4, rows), every),
        per_chunk((layers, 2, rows), every),
        per_chunk((layers, 2, rows), every),
        per_chunk((layers, 2, rows), every),
        per_chunk((layers, 2, rows), every),
        per_chunk((layers, 2, rows), WID),
        pltpu.VMEM((layers, rows, EW), BF),
        pltpu.VMEM((layers, rows, EW), F32),
        per_chunk((layers, 2, tok), WID),
        pltpu.VMEM((4, layers, 2, tok, feats // 4), F32),
        pltpu.VMEM((layers, 2, tok, feats // 2), BF),
        pltpu.VMEM((2, tok, feats // 4), BF),
        pltpu.VMEM((2, tok, feats // 4), BF),
        pltpu.VMEM((2, tok, feats // 4), BF),
        pltpu.VMEM((layers, rows, cols), F32),
        pltpu.VMEM((3, layers, rows, cols), BF),
        pltpu.VMEM((3, layers, rows, cols), BF),
        [pltpu.VMEM((1, 1), jnp.int32), pltpu.VMEM((1, 1), F32), pltpu.VMEM((1, 1), F32)],
        pltpu.VMEM((8, 128), F32),
        pltpu.VMEM((8, 128), F32),
        pltpu.VMEM((2, 8, 128), F32),
        pltpu.VMEM((rows, max(every)), F32),
        pltpu.VMEM((8, 128), F32),
        pltpu.VMEM((15, 8, 128), F32),
        pltpu.VMEM((8, 128), F32),
        pltpu.VMEM((7, 8, 128), F32),
        sem((12,)),
        sem((5,)),
        sem((5,)),
        sem((3,)),
        sem((3,)),
        sem((NK, layers, 2)),
        sem((NK, layers, 2)),
        sem((NK, layers, 2)),
        sem((NK, layers, 2)),
        sem((layers,)),
        sem((layers,)),
        sem((layers,)),
        sem((layers,)),
        sem((NK + 1, layers, 4, 2)),
        sem((NK + 1, layers, 4, 2)),
        sem((NK + 1, layers, 6, 2)),
        sem((NK + 1, layers, 6, 2)),
        sem((NK, layers, 2)),
        sem((NK, layers, 2)),
        sem((NK, layers, 2)),
        sem((NK, layers, 2)),
        sem((7,)),
        sem((7,)),
        sem((15,)),
        sem((15,)),
        sem((7,)),
        sem((7,)),
        sem((2,)),
        sem((2,)),
    ]
    results = (
        jax.ShapeDtypeStruct((layers, tok, feats // 4), BF),
        jax.ShapeDtypeStruct((layers, tok, cols), BF),
    ) + (jax.ShapeDtypeStruct(master.shape, F32),) * 3
    held = pl.pallas_call(
        functools.partial(kernel, entries),
        out_shape=tuple(pltpu.VMEM(r.shape, r.dtype) for r in results),
        in_specs=[any_] * 11,
        out_specs=(vmem,) * 5,
        scratch_shapes=scratch,
        compiler_params=pltpu.CompilerParams(
            collective_id=0, has_side_effects=True, vmem_limit_bytes=56 << 20
        ),
        name="restore_step",
    )(
        layer_input,
        kv_cotangent,
        failed_member.reshape(1, 1),
        loss_scale,
        spare_scale,
        master,
        first_moment,
        second_moment,
        spare_master,
        spare_first,
        spare_second,
    )
    return pl.pallas_call(
        store,
        out_shape=results,
        in_specs=[vmem] * 5,
        out_specs=(any_,) * 5,
        scratch_shapes=[sem((5,))],
        compiler_params=pltpu.CompilerParams(vmem_limit_bytes=1 << 20),
        name="store_results",
    )(*[pltpu.with_memory_space_constraint(h, pltpu.VMEM) for h in held])


def solution(mesh):
    split = Mesh(mesh.devices.reshape(4, 2, 4, 2, 2), (Y, XH, Z, XL, CO))
    placed = (
        P(None, FSDP, RED),
        P(None, FSDP, None),
        P(FSDP),
        P(None, FSDP, RED),
        P(None, FSDP, RED),
        P(None, FSDP, RED),
        P(FSDP, RED),
        P(None, FSDP, RED),
        P(None, FSDP, RED),
        P(None, FSDP, RED),
        P(FSDP, RED),
    )
    return jax.shard_map(
        local,
        mesh=split,
        in_specs=placed,
        out_specs=(P(None, FSDP, RED),) * 5,
        check_vma=False,
    )
```

```python
import functools

import jax
import jax.numpy as jnp
from jax import lax
from jax.experimental import pallas as pl
from jax.experimental.pallas import tpu as pltpu
from jax.sharding import Mesh
from jax.sharding import PartitionSpec as P

Y, XH, Z, XL, CO = "fsdp_0", "fsdp_1", "fsdp_2", "red_0", "red_1"
RED = (XL, CO)
FSDP = (Y, XH, Z)
MESH_ID = pl.DeviceIdType.MESH

BETA_FIRST = 0.9
BETA_SECOND = 0.95
LEARN_RATE = 0.01
DECAY_RATE = 0.1
ADAM_EPS = 1e-08
MEAN_EPS = 1e-06

NK = 4
WID = (512, 512, 384, 256)
OFF = tuple(sum(WID[:k]) for k in range(NK))
EW = 768
SPARES_AT = 1
ORDER = (
    ("INI",),
    ("TR0",),
    ("DW", 4, 1),
    ("DW", 4, 0),
    ("WSEL", 0),
    ("WSEL", 1),
    ("XREST",),
    ("RF0", 4, 1),
    ("A1", 0, 0),
    ("A1", 2, 0),
    ("A1", 1, 0),
    ("A1", 3, 0),
    ("RF0", 4, 0),
    ("A1", 4, 0),
    ("A1", 1, 1),
    ("A1", 3, 1),
    ("A1", 0, 1),
    ("A1", 2, 1),
    ("RE0", 4, 1),
    ("F0", 0, 0),
    ("RE0", 4, 0),
    ("A1", 4, 1),
    ("F0", 2, 0),
    ("F0", 1, 1),
    ("F0", 1, 0),
    ("F0", 3, 1),
    ("F0", 3, 0),
    ("F0", 0, 1),
    ("UF",),
    ("F0", 2, 1),
    ("F0", 4, 0),
    ("S1", 0, 0),
    ("RF1", 4, 1),
    ("TR",),
    ("RF1", 4, 0),
    ("S1", 2, 0),
    ("F0", 4, 1),
    ("S1", 1, 0),
    ("S1", 3, 0),
    ("S1", 1, 1),
    ("S1", 3, 1),
    ("S1", 4, 0),
    ("S1", 0, 1),
    ("S1", 2, 1),
    ("RE1", 4, 0),
    ("F1", 0, 0),
    ("DW", 0, 0),
    ("F1", 1, 1),
    ("RE1", 4, 1),
    ("F1", 3, 1),
    ("F1", 2, 0),
    ("S1", 4, 1),
    ("F1", 0, 1),
    ("DW", 0, 1),
    ("F1", 1, 0),
    ("DW", 1, 0),
    ("F1", 2, 1),
    ("F1", 3, 0),
    ("WD", 1, 1),
    ("IG", 1, 1),
    ("DW", 1, 1),
    ("WD", 3, 1),
    ("KV", 1, 1),
    ("DW", 2, 0),
    ("F1", 4, 0),
    ("DW", 2, 1),
    ("WD", 0, 0),
    ("F1", 4, 1),
    ("IG", 0, 0),
    ("KV", 0, 0),
    ("DW", 3, 0),
    ("WD", 0, 1),
    ("RF0", 0, 0),
    ("IG", 0, 1),
    ("KV", 0, 1),
    ("RF0", 0, 1),
    ("DW", 3, 1),
    ("KV", 3, 1),
    ("FE", 0),
    ("WD", 2, 0),
    ("IG", 2, 0),
    ("KV", 2, 0),
    ("FE", 1),
    ("WD", 2, 1),
    ("IG", 2, 1),
    ("WD", 1, 0),
    ("IG", 1, 0),
    ("KV", 2, 1),
    ("KV", 1, 0),
    ("RF0", 1, 1),
    ("RF0", 1, 0),
    ("WD", 3, 0),
    ("KV", 3, 0),
    ("RF0", 2, 1),
    ("RF0", 2, 0),
    ("WD", 4, 1),
    ("IG", 4, 1),
    ("KV", 4, 1),
    ("RE0", 0, 1),
    ("WD", 4, 0),
    ("RF0", 3, 0),
    ("IG", 4, 0),
    ("RF0", 3, 1),
    ("KV", 4, 0),
    ("RE0", 0, 0),
    ("IG", 3, 1),
    ("KVC",),
    ("RE0", 1, 1),
    ("RE0", 1, 0),
    ("RE0", 2, 1),
    ("RE0", 3, 1),
    ("RE0", 2, 0),
    ("KVA",),
    ("RF1", 0, 0),
    ("RF1", 1, 0),
    ("RF1", 0, 1),
    ("RE0", 3, 0),
    ("RF1", 2, 0),
    ("RF1", 1, 1),
    ("RE1", 0, 0),
    ("RF1", 2, 1),
    ("RE1", 1, 0),
    ("RF1", 3, 0),
    ("RF1", 3, 1),
    ("KVF",),
    ("RE1", 2, 0),
    ("RE1", 0, 1),
    ("RE1", 1, 1),
    ("RE1", 3, 0),
    ("RE1", 2, 1),
    ("RE1", 3, 1),
    ("SQ",),
    ("KVE",),
    ("NX",),
    ("IG", 3, 0),
    ("AD",),
    ("END",),
)
BF = jnp.bfloat16
F32 = jnp.float32


def kernel(
    entries,
    x_in,
    u_in,
    failed_in,
    scale_own_in,
    scale_spare_in,
    master,
    first,
    second,
    sp_master,
    sp_first,
    sp_second,
    kv_out,
    ig_out,
    nm_out,
    nf_out,
    ns_out,
    xbuf,
    xe,
    ubuf,
    ut,
    wsb,
    wbuf,
    dwbuf,
    r1a,
    r1b,
    r1c,
    s1,
    r2a,
    r2b,
    r2c,
    s2,
    gbuf,
    grc,
    ge,
    igb,
    kvp,
    kvr,
    ka,
    kb,
    kc,
    spf,
    spb,
    spr,
    small,
    scs,
    scr,
    scn,
    nacc,
    nsend,
    npl,
    nsend2,
    nxc,
    loc,
    sp_s,
    sp_r,
    u_s,
    u_r,
    x_s,
    x_r,
    w_s,
    w_r,
    we_s,
    we_r,
    ge_s,
    ge_r,
    ag_s,
    ag_r,
    rs_s,
    rs_r,
    g_s,
    g_r,
    ig_s,
    ig_r,
    kv_s,
    kv_r,
    np_s,
    np_r,
    nx_s,
    nx_r,
    sc_s,
    sc_r,
):
    layers, tok, cols = x_in.shape
    half = cols // 2
    rows = master.shape[1]
    feats = u_in.shape[2]
    kept = half - EW // 2
    failed, scale_own, scale_spare = small[0], small[1], small[2]
    y, xh, z, xl, c = (lax.axis_index(a) for a in (Y, XH, Z, XL, CO))
    x = 2 * xh + xl
    me_r = 2 * xl + c

    def ring(v, d):
        return lax.rem(v + (d + 4), 4)

    def to_x(v, core=None):
        dev = {XH: v // 2, XL: lax.rem(v, 2)}
        if core is not None:
            dev[CO] = core
        return dev

    xn = {d: ring(x, d) for d in (1, -1)}
    xn_h = {d: xn[d] // 2 for d in (1, -1)}
    plane_axis = {0: (Y, Z), 1: (Z, Y)}
    plane_pos = {Y: y, Z: z}
    DIRS = ((0, 1), (1, -1))

    def remote(src, dst, ss, rs, dev):
        return pltpu.make_async_remote_copy(
            src_ref=src, dst_ref=dst, send_sem=ss, recv_sem=rs, device_id=dev, device_id_type=MESH_ID
        )

    states = (master, first, second)
    st = (nm_out, nf_out, ns_out)
    spares = (sp_master, sp_first, sp_second)
    loads_sp = [pltpu.make_async_copy(spares[i], spf, loc.at[i]) for i in range(3)]
    loads_st = [pltpu.make_async_copy(states[i], st[i], loc.at[3 + i]) for i in range(3)]
    load_u = pltpu.make_async_copy(u_in, ubuf.at[:, xh], loc.at[6])
    load_small = [
        pltpu.make_async_copy(ref, buf, loc.at[7 + i])
        for i, (ref, buf) in enumerate(
            ((failed_in, small[0]), (scale_own_in, small[1]), (scale_spare_in, small[2]))
        )
    ]
    load_xe = [
        pltpu.make_async_copy(
            x_in.at[:, :, h * half + kept : (h + 1) * half],
            xe.at[:, :, h * (EW // 2) : (h + 1) * (EW // 2)],
            loc.at[10 + h],
        )
        for h in range(2)
    ]
    loads_sp[0].start()
    loads_st[0].start()
    for cp in load_small:
        cp.start()
    load_u.start()
    for cp in load_xe:
        cp.start()
    loads_st[1].start()
    loads_st[2].start()

    nxt_r = lax.rem(me_r + 1, 4)
    prv_r = lax.rem(me_r + 3, 4)
    plane_peers = [(dy, dz) for dy in range(4) for dz in range(4) if (dy, dz) != (0, 0)]
    xc_peers = [(dx, dc) for dx in range(4) for dc in range(2) if (dx, dc) != (0, 0)]

    def plane_dev(dy, dz):
        return {Y: lax.rem(y + dy, 4), Z: lax.rem(z + dz, 4)}

    def xc_dev(dx, dc):
        v = lax.rem(x + dx, 4)
        return {XH: v // 2, XL: lax.rem(v, 2), CO: lax.rem(c + dc, 2)}

    barrier = pltpu.get_barrier_semaphore()
    for axis in (Y, Z):
        for _, d in DIRS:
            pl.semaphore_signal(
                barrier, inc=1, device_id={axis: ring(plane_pos[axis], d)}, device_id_type=MESH_ID
            )
    for p in xc_peers:
        pl.semaphore_signal(barrier, inc=1, device_id=xc_dev(*p), device_id_type=MESH_ID)

    nxt_dev = {XL: nxt_r // 2, CO: lax.rem(nxt_r, 2)}

    def spare_copy(i, l):
        if i == 0:
            return remote(spb.at[0, l], spr.at[0, l], sp_s.at[l], sp_r.at[l], nxt_dev)
        return remote(spb.at[i], spr.at[i], sp_s.at[1 + i], sp_r.at[1 + i], nxt_dev)

    scale_copy = remote(scs, scr, sp_s.at[4], sp_r.at[4], nxt_dev)

    def sc_copy(di, d):
        return remote(scr, scn.at[xh], sc_s.at[di], sc_r.at[di], to_x(xn[d]))

    def x_copy(k, l, di, d):
        src = x_in.at[l, :, pl.ds(pl.multiple_of(xn_h[d] * half + OFF[k], 128), WID[k])]
        return remote(src, xbuf[k].at[l, xh], x_s.at[k, l, di], x_r.at[k, l, di], to_x(xn[d]))

    def w_copy(k, l, di, d):
        src = wsb.at[xn_h[d], l, :, OFF[k] : OFF[k] + WID[k]]
        return remote(src, wbuf[k].at[l, y, xh, z], w_s.at[k, l, di], w_r.at[k, l, di], to_x(xn[d]))

    x_far = to_x(ring(x, 2))

    def we_copy(l):
        own = wbuf[NK].at[l, y, xh, z]
        return remote(own, own, we_s.at[l], we_r.at[l], x_far)

    def ge_copy(l):
        return remote(s2[NK].at[l, 1 - xh], grc.at[l], ge_s.at[l], ge_r.at[l], x_far)

    u_far = lax.rem(x + 1 + 2 * (1 - lax.rem(x, 2)), 4)

    def u_copy(part):
        span = slice(0, tok // 4) if part == 0 else slice(tok // 4, tok)
        return remote(u_in.at[c, span], ubuf.at[c, xh, span], u_s.at[part], u_r.at[part], to_x(u_far))

    u_fwd = remote(ubuf.at[c, 1 - xh], ubuf.at[c, 1 - xh], u_s.at[2], u_r.at[2], {CO: 1 - c})

    def region(k, l, stage, p, h):
        hs = slice(None) if h is None else h
        if l == 0:
            return wbuf[k].at[0, p, hs, z] if stage == 0 else wbuf[k].at[0, :, hs, p]
        return wbuf[k].at[1, y, hs, p] if stage == 0 else wbuf[k].at[1, p, hs, :]

    def ag_copy(k, l, stage, step, di, d):
        axis = plane_axis[l][stage]
        pos = plane_pos[axis]
        ref = region(k, l, stage, pos, None) if step == 0 else region(k, l, stage, ring(pos, -d), di)
        n = stage * 2 + step
        return remote(ref, ref, ag_s.at[k, l, n, di], ag_r.at[k, l, n, di], {axis: ring(pos, d)})

    def dw_piece(k, l, p, h):
        return dwbuf[k].at[0, :, h, p] if l == 0 else dwbuf[k].at[1, p, h, :]

    def rs_parts(k, l, stage):
        axis = plane_axis[l][1 - stage]
        if stage == 0:
            return axis, (lambda p, h: dw_piece(k, l, p, h)), r1a[k], r1b[k], r1c[k]
        return axis, (lambda p, h: s1[k].at[l, h, p]), r2a[k], r2b[k], r2c[k]

    def rs_copy(k, l, stage, what, di, d):
        axis, piece, ra, rb, rc = rs_parts(k, l, stage)
        pos = plane_pos[axis]
        if what == 0:
            src, dst = piece(ring(pos, 2), di), ra.at[l, di]
        elif what == 1:
            src, dst = piece(ring(pos, d), 1 - di), rb.at[l, di]
        else:
            src, dst = ra.at[l, di], rc.at[l, di]
        n = stage * 3 + what
        return remote(src, dst, rs_s.at[k, l, n, di], rs_r.at[k, l, n, di], {axis: ring(pos, d)})

    def rs_start(k, l, stage):
        for what in (0, 1):
            for di, d in DIRS:
                rs_copy(k, l, stage, what, di, d).start()

    def each(stage, fn):
        if stage == 0:

            @pl.loop(0, 4)
            def _(j):
                fn(j)
        else:
            fn(None)

    def at(ref, j):
        return ref[j] if j is not None else ref[...]

    def rs_forward(k, l, stage):
        axis, piece, ra, rb, rc = rs_parts(k, l, stage)
        pos = plane_pos[axis]
        for di, d in DIRS:
            rs_copy(k, l, stage, 0, di, d).wait_recv()
            own = piece(ring(pos, d), di)
            acc = ra.at[l, di]

            def add(j, own=own, acc=acc):
                total = (at(acc, j).astype(F32) + at(own, j).astype(F32)).astype(BF)
                if j is None:
                    acc[...] = total
                else:
                    acc[j] = total

            each(stage, add)
            rs_copy(k, l, stage, 2, di, d).start()

    def rs_finish(k, l, stage):
        axis, piece, ra, rb, rc = rs_parts(k, l, stage)
        pos = plane_pos[axis]
        for what in (1, 2):
            for di, d in DIRS:
                rs_copy(k, l, stage, what, di, d).wait_recv()
        for h in range(2):
            own = piece(pos, h)
            through = rc.at[l, h]
            direct = rb.at[l, 1 - h]
            out = s1[k].at[l, h] if stage == 0 else s2[k].at[l, h]

            def add(j, own=own, through=through, direct=direct, out=out):
                total = at(own, j).astype(F32) + at(through, j).astype(F32) + at(direct, j).astype(F32)
                if j is None:
                    out[...] = total.astype(BF)
                else:
                    out[j] = total.astype(BF)

            each(stage, add)

    def g_copy(k, l, di, d):
        return remote(
            s2[k].at[l, xn_h[d]], gbuf[k].at[l, xh], g_s.at[k, l, di], g_r.at[k, l, di], to_x(xn[d])
        )

    def ig_copy(k, l, di, d):
        dst = ig_out.at[l, :, pl.ds(pl.multiple_of(xh * half + OFF[k], 128), WID[k])]
        return remote(igb[k].at[l, xn_h[d]], dst, ig_s.at[k, l, di], ig_r.at[k, l, di], to_x(xn[d]))

    quarter = feats // 4
    kv_core = remote(xbuf[0], kvr, kv_s.at[0], kv_r.at[0], {CO: 1 - c})

    def kv_piece(v, l):
        span = pl.ds(pl.multiple_of(lax.rem(v, 2) * quarter, quarter), quarter)
        return kvr.at[l, v // 2, :, span]

    def kv_copy(what, di, d):
        if what == 0:
            src, dst = kv_piece(ring(x, 2), di), ka.at[di]
        elif what == 1:
            src, dst = kv_piece(ring(x, d), 1 - di), kb.at[di]
        else:
            src, dst = ka.at[di], kc.at[di]
        n = 1 + what * 2 + di
        return remote(src, dst, kv_s.at[n], kv_r.at[n], to_x(xn[d]))

    np_copies = [
        remote(nsend, npl.at[i], np_s.at[i], np_r.at[i], plane_dev(*p)) for i, p in enumerate(plane_peers)
    ]
    nx_copies = [
        remote(nsend2, nxc.at[i], nx_s.at[i], nx_r.at[i], xc_dev(*p)) for i, p in enumerate(xc_peers)
    ]

    def lost(shape):
        return jnp.broadcast_to(failed[...], shape) == me_r

    def begin():
        loads_sp[0].wait()
        for l in range(layers):
            spb[0, l] = spf[l].astype(BF)
        loads_sp[1].start()
        for cp in load_small:
            cp.wait()
        scs[...] = jnp.broadcast_to(scale_spare[...], scs.shape)
        pl.semaphore_wait(barrier, 4 + len(xc_peers))
        u_copy(0).start()
        for l in range(layers):
            spare_copy(0, l).start()
        scale_copy.start()
        loads_st[0].wait()

    def recover(l):
        spare_copy(0, l).wait_recv()
        for h in range(2):
            for k in range(NK + 1):
                off, width = (OFF[k], WID[k]) if k < NK else (kept, EW // 2)
                span = slice(h * half + off, h * half + off + width)
                now = jnp.where(lost((rows, width)), spr[0, l, :, span].astype(F32), st[0][l, :, span])
                st[0][l, :, span] = now
                if k < NK:
                    wsb[h, l, :, off : off + width] = now.astype(BF)
                else:
                    wbuf[NK][l, y, xh, z, :, h * width : (h + 1) * width] = now.astype(BF)
        for k in range(NK):
            for di, d in DIRS:
                w_copy(k, l, di, d).start()
        we_copy(l).start()

    def exchange():
        u_copy(1).start()
        n = 0
        for k in range(NK):
            for l in range(layers):
                for di, d in DIRS:
                    x_copy(k, l, di, d).start()
                if n == SPARES_AT:
                    for i in (1, 2):
                        loads_sp[i].wait()
                        for ll in range(layers):
                            spb[i, ll] = spf[ll].astype(BF)
                        if i == 1:
                            loads_sp[2].start()
                        spare_copy(i, 0).start()
                n += 1
        scale_copy.wait_recv()
        scr[...] = jnp.where(lost(scr.shape), scr[...], jnp.broadcast_to(scale_own[...], scr.shape))
        nacc[...] = jnp.zeros(nacc.shape, F32)
        for di, d in DIRS:
            sc_copy(di, d).start()

    def forward_u():
        for part in range(2):
            u_copy(part).wait_recv()
        u_fwd.start()

    def transpose_u(of):
        for l in range(layers):

            @pl.loop(0, 4)
            def _(j):
                span = pl.ds(pl.multiple_of(j * (feats // 4), feats // 4), feats // 4)
                ut[l, j, of] = ubuf[l, of, :, span].T

    def transpose_own():
        load_u.wait()
        transpose_u(xh)

    def transpose_far():
        u_fwd.wait_recv()
        transpose_u(1 - xh)

    def gather_0(k, l):
        if k == NK:
            we_copy(l).wait_recv()
        else:
            for di, d in DIRS:
                w_copy(k, l, di, d).wait_recv()
        for di, d in DIRS:
            ag_copy(k, l, 0, 0, di, d).start()

    def gather_forward(stage, k, l):
        for di, d in DIRS:
            ag_copy(k, l, stage, 0, di, d).wait_recv()
            ag_copy(k, l, stage, 1, di, d).start()

    def gather_1(k, l):
        for di, d in DIRS:
            ag_copy(k, l, 0, 1, di, d).wait_recv()
        for di, d in DIRS:
            ag_copy(k, l, 1, 0, di, d).start()

    def gathered(k, l):
        for di, d in DIRS:
            ag_copy(k, l, 1, 1, di, d).wait_recv()

    got_x = set()

    def need_x(k, l):
        if (k, l) not in got_x:
            got_x.add((k, l))
            for di, d in DIRS:
                x_copy(k, l, di, d).wait_recv()

    got_xe = set()

    def need_xe():
        if not got_xe:
            got_xe.add(1)
            for cp in load_xe:
                cp.wait()

    def grad_product(k, l):
        if k < NK:
            need_x(k, l)
            width = WID[k]
        else:
            need_xe()
            width = EW

        @pl.loop(0, 4)
        def _(j):
            if k < NK:
                inputs = xbuf[k][l].reshape(2 * tok, width)
                up = jnp.concatenate([ut[l, j, 0], ut[l, j, 1]], axis=1)
                part = jnp.dot(up, inputs, preferred_element_type=F32)
            else:
                part = jnp.dot(ut[l, j, xh], xe[l], preferred_element_type=F32)
            dwbuf[k][l, j] = part.astype(BF).reshape(2, 4, rows, width)

        rs_start(k, l, 0)

    def finish_0(k, l):
        rs_finish(k, l, 0)
        rs_start(k, l, 1)

    got_scale = set()

    def add_squares(grad):
        nacc[:, 0 : grad.shape[1]] += grad * grad

    def finish_1(k, l):
        rs_finish(k, l, 1)
        if k == NK:
            ge_copy(l).start()
            return
        for di, d in DIRS:
            g_copy(k, l, di, d).start()
        if not got_scale:
            got_scale.add(1)
            for di, d in DIRS:
                sc_copy(di, d).wait_recv()
        for h in range(2):
            add_squares(s2[k][l, h].astype(F32) / jnp.broadcast_to(scn[h, 0:1, 0:1], (rows, WID[k])))

    def finish_kept(l):
        ge_copy(l).wait_recv()
        grad = s2[NK][l, xh].astype(F32) + grc[l].astype(F32)
        grad = grad / jnp.broadcast_to(scr[0:1, 0:1], (rows, EW))
        ge[l] = grad
        add_squares(grad)

    kv_begun = set()

    def kv_product(k, l):
        fresh = l not in kv_begun
        kv_begun.add(l)
        if k == NK:
            need_xe()
            assert not fresh

            @pl.loop(0, 4)
            def _(j):
                weight = wbuf[k][l, j].reshape(8 * rows, EW)
                part = lax.dot_general(xe[l], weight, (((1,), (1,)), ((), ())), preferred_element_type=F32)
                kvp[j, l, xh] += part

            return
        need_x(k, l)

        @pl.loop(0, 4)
        def _(j):
            inputs = xbuf[k][l].reshape(2 * tok, WID[k])
            weight = wbuf[k][l, j].reshape(8 * rows, WID[k])
            part = lax.dot_general(
                inputs, weight, (((1,), (1,)), ((), ())), preferred_element_type=F32
            ).reshape(2, tok, 8 * rows)
            if fresh:
                kvp[j, l] = part
            else:
                kvp[j, l] += part

    def ig_product(k, l):
        if k == NK:
            weight = wbuf[k][l].reshape(feats, EW)
            grad = jnp.dot(ubuf[l, xh], weight, preferred_element_type=F32).astype(BF)
            for h in range(2):
                ig_out[l, :, h * half + kept : (h + 1) * half] = grad[:, h * (EW // 2) : (h + 1) * (EW // 2)]
            return

        @pl.loop(0, 2)
        def _(t):
            weight = wbuf[k][l].reshape(feats, WID[k])
            igb[k][l, t] = jnp.dot(ubuf[l, t], weight, preferred_element_type=F32).astype(BF)

        for di, d in DIRS:
            ig_copy(k, l, di, d).start()

    def kv_cores():
        for v in range(2):
            xbuf[0][:, :, :, v * quarter : (v + 1) * quarter] = kvp[2 * v + (1 - c)].astype(BF)
        kv_core.start()

    def kv_ring():
        kv_core.wait_recv()
        for v in range(2):
            for l in range(layers):
                span = slice(v * quarter, (v + 1) * quarter)
                kvr[l, :, :, span] = (kvr[l, :, :, span].astype(F32) + kvp[2 * v + c, l]).astype(BF)
        for what in (0, 1):
            for di, d in DIRS:
                kv_copy(what, di, d).start()

    def kv_forward():
        for di, d in DIRS:
            kv_copy(0, di, d).wait_recv()
            ka[di] = (ka[di].astype(F32) + kv_piece(ring(x, d), di)[...].astype(F32)).astype(BF)
            kv_copy(2, di, d).start()

    def kv_finish():
        for what in (1, 2):
            for di, d in DIRS:
                kv_copy(what, di, d).wait_recv()
        for h in range(2):
            own = kv_piece(x, h)[...].astype(F32)
            kv_out[h] = (own + kc[h].astype(F32) + kb[1 - h].astype(F32)).astype(BF)

    def squares_plane():
        tile = jnp.zeros((8, 128), F32)
        for i in range(rows // 8):
            for j in range(nacc.shape[1] // 128):
                tile = tile + nacc[8 * i : 8 * i + 8, 128 * j : 128 * j + 128]
        nsend[...] = tile
        for cp in np_copies:
            cp.start()

    def squares_rest():
        total = nsend[...]
        for i, cp in enumerate(np_copies):
            cp.wait_recv()
            total = total + npl[i]
        nsend2[...] = total
        for cp in nx_copies:
            cp.start()

    def adam():
        for i in (1, 2):
            loads_st[i].wait()
            spare_copy(i, 0).wait_recv()
        for k in range(NK):
            for l in range(layers):
                for di, d in DIRS:
                    g_copy(k, l, di, d).wait_recv()
        total = nsend2[...]
        for i, cp in enumerate(nx_copies):
            cp.wait_recv()
            total = total + nxc[i]
        squares = jnp.sum(jnp.sum(total, axis=1, keepdims=True), axis=0, keepdims=True)
        factor = jnp.minimum(1.0, lax.rsqrt(squares / entries + MEAN_EPS))

        def update(l, start, grad):
            shape = grad.shape
            span = slice(start, start + shape[1])
            gone = lost(shape)
            clipped = grad * jnp.broadcast_to(factor, shape)
            first_now = jnp.where(gone, spr[1, l, :, span].astype(F32), st[1][l, :, span])
            second_now = jnp.where(gone, spr[2, l, :, span].astype(F32), st[2][l, :, span])
            master_now = st[0][l, :, span]
            new_first = BETA_FIRST * first_now + (1.0 - BETA_FIRST) * clipped
            new_second = BETA_SECOND * second_now + (1.0 - BETA_SECOND) * clipped * clipped
            st[0][l, :, span] = master_now - LEARN_RATE * (
                new_first / (jnp.sqrt(new_second) + ADAM_EPS) + DECAY_RATE * master_now
            )
            st[1][l, :, span] = new_first
            st[2][l, :, span] = new_second

        @pl.loop(0, layers)
        def _(l):
            for h in range(2):
                for k in range(NK):
                    scale = jnp.broadcast_to(scr[0:1, 0:1], (rows, WID[k]))
                    update(l, h * half + OFF[k], gbuf[k][l, h].astype(F32) / scale)
                update(l, h * half + kept, ge[l, :, h * (EW // 2) : (h + 1) * (EW // 2)])

    steps = {
        "INI": begin,
        "WSEL": recover,
        "XREST": exchange,
        "UF": forward_u,
        "TR0": transpose_own,
        "TR": transpose_far,
        "A1": gather_0,
        "F0": functools.partial(gather_forward, 0),
        "S1": gather_1,
        "F1": functools.partial(gather_forward, 1),
        "WD": gathered,
        "FE": finish_kept,
        "DW": grad_product,
        "RF0": lambda k, l: rs_forward(k, l, 0),
        "RE0": finish_0,
        "RF1": lambda k, l: rs_forward(k, l, 1),
        "RE1": finish_1,
        "KV": kv_product,
        "IG": ig_product,
        "KVC": kv_cores,
        "KVA": kv_ring,
        "KVF": kv_forward,
        "KVE": kv_finish,
        "SQ": squares_plane,
        "NX": squares_rest,
        "AD": adam,
        "END": lambda: None,
    }
    for name, *where in ORDER:
        steps[name](*where)

    for l in range(layers):
        spare_copy(0, l).wait_send()
    for i in (1, 2):
        spare_copy(i, 0).wait_send()
    scale_copy.wait_send()
    for part in range(2):
        u_copy(part).wait_send()
    for di, d in DIRS:
        sc_copy(di, d).wait_send()
    u_fwd.wait_send()
    kv_core.wait_send()
    for l in range(layers):
        we_copy(l).wait_send()
        ge_copy(l).wait_send()
        for k in range(NK):
            for di, d in DIRS:
                w_copy(k, l, di, d).wait_send()
    for what in range(3):
        for di, d in DIRS:
            kv_copy(what, di, d).wait_send()
    for cp in np_copies + nx_copies:
        cp.wait_send()

    for k in range(NK + 1):
        for l in range(layers):
            for di, d in DIRS:
                for stage in range(2):
                    for step in range(2):
                        ag_copy(k, l, stage, step, di, d).wait_send()
                    for what in range(3):
                        rs_copy(k, l, stage, what, di, d).wait_send()
                if k < NK:
                    x_copy(k, l, di, d).wait_send()
                    ig_copy(k, l, di, d).wait_send()
                    g_copy(k, l, di, d).wait_send()
                    ig_copy(k, l, di, d).wait_recv()


def store(*refs):
    sems = refs[10]
    copies = [pltpu.make_async_copy(refs[i], refs[5 + i], sems.at[i]) for i in range(5)]
    for cp in copies:
        cp.start()
    for cp in copies:
        cp.wait()


def local(
    layer_input,
    kv_cotangent,
    failed_member,
    master,
    first_moment,
    second_moment,
    loss_scale,
    spare_master,
    spare_first,
    spare_second,
    spare_scale,
):
    layers, tok, cols = layer_input.shape
    rows = master.shape[1]
    feats = kv_cotangent.shape[2]
    entries = float(layers * rows * lax.axis_size(FSDP) * cols * lax.axis_size(RED))
    any_ = pl.BlockSpec(memory_space=pl.ANY)
    vmem = pl.BlockSpec(memory_space=pltpu.VMEM)
    sem = pltpu.SemaphoreType.DMA
    every = WID + (EW,)

    def per_chunk(shape, widths):
        return [pltpu.VMEM((*shape, w), BF) for w in widths]

    scratch = [
        per_chunk((layers, 2, tok), WID),
        pltpu.VMEM((layers, tok, EW), BF),
        pltpu.VMEM((layers, 2, tok, feats), BF),
        pltpu.VMEM((layers, 4, 2, feats // 4, tok), BF),
        pltpu.VMEM((2, layers, rows, cols // 2 - EW // 2), BF),
        per_chunk((layers, 4, 2, 4, rows), every),
        per_chunk((layers, 4, 2, 4, rows), every),
        per_chunk((layers, 2, 4, rows), every),
        per_chunk((layers, 2, 4, rows), every),
        per_chunk((layers, 2, 4, rows), every),
        per_chunk((layers, 2, 4, rows), every),
        per_chunk((layers, 2, rows), every),
        per_chunk((layers, 2, rows), every),
        per_chunk((layers, 2, rows), every),
        per_chunk((layers, 2, rows), every),
        per_chunk((layers, 2, rows), WID),
        pltpu.VMEM((layers, rows, EW), BF),
        pltpu.VMEM((layers, rows, EW), F32),
        per_chunk((layers, 2, tok), WID),
        pltpu.VMEM((4, layers, 2, tok, feats // 4), F32),
        pltpu.VMEM((layers, 2, tok, feats // 2), BF),
        pltpu.VMEM((2, tok, feats // 4), BF),
        pltpu.VMEM((2, tok, feats // 4), BF),
        pltpu.VMEM((2, tok, feats // 4), BF),
        pltpu.VMEM((layers, rows, cols), F32),
        pltpu.VMEM((3, layers, rows, cols), BF),
        pltpu.VMEM((3, layers, rows, cols), BF),
        [pltpu.VMEM((1, 1), jnp.int32), pltpu.VMEM((1, 1), F32), pltpu.VMEM((1, 1), F32)],
        pltpu.VMEM((8, 128), F32),
        pltpu.VMEM((8, 128), F32),
        pltpu.VMEM((2, 8, 128), F32),
        pltpu.VMEM((rows, max(every)), F32),
        pltpu.VMEM((8, 128), F32),
        pltpu.VMEM((15, 8, 128), F32),
        pltpu.VMEM((8, 128), F32),
        pltpu.VMEM((7, 8, 128), F32),
        sem((12,)),
        sem((5,)),
        sem((5,)),
        sem((3,)),
        sem((3,)),
        sem((NK, layers, 2)),
        sem((NK, layers, 2)),
        sem((NK, layers, 2)),
        sem((NK, layers, 2)),
        sem((layers,)),
        sem((layers,)),
        sem((layers,)),
        sem((layers,)),
        sem((NK + 1, layers, 4, 2)),
        sem((NK + 1, layers, 4, 2)),
        sem((NK + 1, layers, 6, 2)),
        sem((NK + 1, layers, 6, 2)),
        sem((NK, layers, 2)),
        sem((NK, layers, 2)),
        sem((NK, layers, 2)),
        sem((NK, layers, 2)),
        sem((7,)),
        sem((7,)),
        sem((15,)),
        sem((15,)),
        sem((7,)),
        sem((7,)),
        sem((2,)),
        sem((2,)),
    ]
    results = (
        jax.ShapeDtypeStruct((layers, tok, feats // 4), BF),
        jax.ShapeDtypeStruct((layers, tok, cols), BF),
    ) + (jax.ShapeDtypeStruct(master.shape, F32),) * 3
    held = pl.pallas_call(
        functools.partial(kernel, entries),
        out_shape=tuple(pltpu.VMEM(r.shape, r.dtype) for r in results),
        in_specs=[any_] * 11,
        out_specs=(vmem,) * 5,
        scratch_shapes=scratch,
        compiler_params=pltpu.CompilerParams(
            collective_id=0, has_side_effects=True, vmem_limit_bytes=56 << 20
        ),
        name="restore_step",
    )(
        layer_input,
        kv_cotangent,
        failed_member.reshape(1, 1),
        loss_scale,
        spare_scale,
        master,
        first_moment,
        second_moment,
        spare_master,
        spare_first,
        spare_second,
    )
    return pl.pallas_call(
        store,
        out_shape=results,
        in_specs=[vmem] * 5,
        out_specs=(any_,) * 5,
        scratch_shapes=[sem((5,))],
        compiler_params=pltpu.CompilerParams(vmem_limit_bytes=1 << 20),
        name="store_results",
    )(*[pltpu.with_memory_space_constraint(h, pltpu.VMEM) for h in held])


def solution(mesh):
    split = Mesh(mesh.devices.reshape(4, 2, 4, 2, 2), (Y, XH, Z, XL, CO))
    placed = (
        P(None, FSDP, RED),
        P(None, FSDP, None),
        P(FSDP),
        P(None, FSDP, RED),
        P(None, FSDP, RED),
        P(None, FSDP, RED),
        P(FSDP, RED),
        P(None, FSDP, RED),
        P(None, FSDP, RED),
        P(None, FSDP, RED),
        P(FSDP, RED),
    )
    return jax.shard_map(
        local,
        mesh=split,
        in_specs=placed,
        out_specs=(P(None, FSDP, RED),) * 5,
        check_vma=False,
    )
```
